32 devices in a mesh: dp: 16 (over z, y, core), tensor: 2 (over x).
Axes of the slice: x: 2, y: 2, z: 4, core: 2. Of those that a mesh axis runs over, the one named last changes fastest.
Arguments:
- tokens: bfloat16 [8192, 1024], P(('dp', 'tensor')), may hold values from -6 to 6
- cotangent: bfloat16 [8192, 1024], P(('dp', 'tensor')), may hold values from -6 to 6
- lengths: int32 [16], replicated, may hold values from 128 to 512, as said below
- bucket_table: int32 [1023], replicated, may hold values from 0 to 31, as said below
- routes: int32 [8192, 2], P('dp'), may hold values from 0 to 15, all different within a row
- gate_values: bfloat16 [8192, 2], P('dp'), may hold values from 0.19921875 to 1
- qkv_weight: bfloat16 [3, 1024, 1024], P(None, 'dp', 'tensor'), may hold values from -0.1875 to 0.1875
- out_weight: bfloat16 [1024, 1024], P('dp', 'tensor'), may hold values from -2 to 2
- norm_gains: bfloat16 [2, 1024], P(None, 'dp'), may hold values from 0.5 to 1.5
- rel_bias: bfloat16 [16, 32], P('tensor'), may hold values from -3 to 3
- gate_weight: bfloat16 [16, 1024, 2816], P(None, 'dp', 'tensor'), may hold values from -0.1875 to 0.1875
- up_weight: bfloat16 [16, 1024, 2816], P(None, 'dp', 'tensor'), may hold values from -0.1875 to 0.1875
- down_weight: bfloat16 [16, 1024, 2816], P(None, 'dp', 'tensor'), may hold values from -0.109375 to 0.109375
Outputs:
- mixed: bfloat16 [8192, 1024], P(('dp', 'tensor'))
- input_grad: float32 [8192, 1024], P(('dp', 'tensor'))
- qkv_grad: float32 [3, 1024, 1024], P(None, 'dp', 'tensor')
- out_grad: float32 [1024, 1024], P('dp', 'tensor')
- gains_grad: float32 [2, 1024], P(None, 'dp')
- bias_grad: float32 [16, 32], P('tensor')
- gate_grad: float32 [16, 1024, 2816], P(None, 'dp', 'tensor')
- up_grad: float32 [16, 1024, 2816], P(None, 'dp', 'tensor')
- down_grad: float32 [16, 1024, 2816], P(None, 'dp', 'tensor')
The draws below stay inside these ranges and needn't reach their ends.
Inputs may be any that keep to these rules, and one draw needn't show every extreme that they name: `lengths`: one sequence is 512 long and another a quarter of 512. `bucket_table`: entry r + 511 is the bucket of a key r positions after its query (before it for negative r); it depends only on the sign of r and on |r|, and never falls as |r| grows on either side. `routes`: each token names two different experts.
All inputs are finite; a program needn't handle non-finite values.
Results may differ from the reference program's by a relative error of at most 0.018.
Values may be sent and summed in bfloat16 or wider, within the bound.
No kernel may reach another device: no remote copies, remote signals or barrier semaphores. Data moves between devices by JAX's collectives and lax.ppermute only.
A program may use at most 192 MiB of HBM per device.

```python
import math
import jax
import jax.numpy as jnp
from jax import lax

D = 1024
HEADS = 16
HEAD_DIM = 64
FF = 2816
BUCKETS = 32
EXPERTS = 16
ROWS = 512
LEN = 512
SEQS = 16
TOKENS = 8192
CAP = 72
N_DP = 16


def draw_lengths(key, part):
    first_key = jax.random.fold_in(key, 11)
    second_key = jax.random.fold_in(key, 12)
    drawn_lengths = jax.random.randint(first_key, (SEQS,), LEN // 4, LEN + 1, dtype=jnp.int32)
    shuffled = jax.random.permutation(second_key, SEQS)
    drawn_lengths = drawn_lengths.at[shuffled[0]].set(LEN)
    drawn_lengths = drawn_lengths.at[shuffled[1]].set(LEN // 4)
    return drawn_lengths.astype(jnp.int32)


def draw_bucket_table(key, part):
    half_count = BUCKETS // 2
    exact_count = half_count // 2
    shuffled = jax.random.permutation(jax.random.fold_in(key, 21), LEN // 2 - exact_count - 1)
    far_edges = jnp.sort(shuffled[:half_count - 1 - exact_count].astype(jnp.int32) + exact_count + 1)
    edge_list = jnp.concatenate([jnp.arange(1, exact_count + 1, dtype=jnp.int32), far_edges.astype(jnp.int32)])
    offsets = jnp.arange(2 * LEN - 1, dtype=jnp.int32) - (LEN - 1)
    distance = jnp.abs(offsets)
    bucket = jnp.sum((distance[:, None] >= edge_list[None, :]).astype(jnp.int32), axis=1)
    return (bucket + half_count * (offsets > 0).astype(jnp.int32)).astype(jnp.int32)


def levels(own_key, extent, cuts, low, high):
    loudness, own = 1.0, jax.random.fold_in(own_key, 6)
    for dim, blocks in cuts:
        heights = jnp.exp(jax.random.uniform(jax.random.fold_in(own, dim), (blocks,), jnp.float32, low / len(cuts), high / len(cuts)))
        loudness = loudness * jnp.repeat(heights, extent[dim] // blocks).reshape([-1 if axis == dim else 1 for axis in range(len(extent))])
    return loudness


def picks_of(stream_key, rows, count, top, lift):
    sequence = jax.random.permutation(jax.random.fold_in(stream_key, 1), count)
    favour = sequence
    for power in range(3):
        favour = favour * favour // count
    favour = favour * lift // count
    chance = jax.random.randint(jax.random.fold_in(stream_key, 2), (rows, count), 0, 4096) + favour
    holders = jax.random.permutation(jax.random.fold_in(stream_key, 3), rows)[jnp.arange(count) % rows]
    chance = jnp.where(jnp.arange(rows)[:, None] == holders[None, :], 1 << 14, chance)
    priority = chance * count + jnp.arange(count)
    return lax.top_k(priority.astype(jnp.int32), top)[1].astype(jnp.int32)


def bell_draw(key, shape, spread, bound, cuts=(), kind=jnp.bfloat16):
    factor_of = levels(key, shape, cuts, -0.22, 0.18) if cuts else 1.0
    drawn = jax.random.normal(key, shape, jnp.float32) * spread * factor_of
    return jnp.minimum(jnp.maximum(drawn, -bound), bound).astype(kind)


def setup_inputs(seed: int = 0) -> dict:
    key_list = jax.random.split(jax.random.key(seed), 14)
    tokens = bell_draw(key_list[0], (TOKENS, D), 1.0, 6.0, ((0, 32),))
    cotangent = bell_draw(key_list[1], (TOKENS, D), 1.0, 6.0, ((0, 32),))
    lengths = draw_lengths(jax.random.fold_in(key_list[13], 71), 0)
    bucket_table = draw_bucket_table(jax.random.fold_in(key_list[13], 71), 0)
    routes = picks_of(key_list[4], TOKENS, EXPERTS, 2, 1024)
    gate_values = jnp.clip(0.19921875 + 0.80078125 * jax.random.uniform(key_list[5], (TOKENS, 2), jnp.float32) ** levels(key_list[5], (TOKENS, 2), ((0, 16),), -0.2, 0.2), 0.19921875, 1.0).astype(jnp.bfloat16)
    qkv_weight = bell_draw(key_list[6], (3, D, D), D ** -0.5, 0.1875, ((1, 16), (2, 2)))
    out_weight = bell_draw(key_list[7], (D, D), (max(1, 4 * D // LEN)) ** -0.5, 2.0, ((0, 16), (1, 2)))
    norm_gains = jnp.clip(1.0 + 0.1 * jax.random.normal(key_list[8], (2, D), jnp.float32), 0.5, 1.5).astype(jnp.bfloat16)
    rel_bias = bell_draw(key_list[9], (HEADS, BUCKETS), 0.5, 3.0, ((0, 2),))
    gate_weight = bell_draw(key_list[10], (EXPERTS, D, FF), D ** -0.5, 0.1875, ((1, 16), (2, 2)))
    up_weight = bell_draw(key_list[11], (EXPERTS, D, FF), D ** -0.5, 0.1875, ((1, 16), (2, 2)))
    down_weight = bell_draw(key_list[12], (EXPERTS, D, FF), FF ** -0.5, 0.109375, ((1, 16), (2, 2)))
    return dict(tokens=tokens, cotangent=cotangent, lengths=lengths, bucket_table=bucket_table, routes=routes, gate_values=gate_values, qkv_weight=qkv_weight, out_weight=out_weight, norm_gains=norm_gains, rel_bias=rel_bias, gate_weight=gate_weight, up_weight=up_weight, down_weight=down_weight)


EPSILON = 1e-06
MASKED_SCORE = -1e+30
HIGHEST = lax.Precision.HIGHEST

@jax.custom_vjp
def low(v):
    return lax.optimization_barrier(v.astype(jnp.bfloat16)).astype(jnp.float32)

@jax.custom_vjp
def low_back(v):
    return v

def low_keep(v):
    return (low(v), None)

def low_pass(kept, grad):
    return (grad,)

def back_keep(v):
    return (v, None)

def back_low(kept, grad):
    return (low(grad),)
low.defvjp(low_keep, low_pass)
low_back.defvjp(back_keep, back_low)

def matmul_high(left_side, right_side):
    return jnp.dot(left_side, right_side, precision=HIGHEST, preferred_element_type=jnp.float32)

def rms_norm(activations, gain_row):
    row_scale = lax.rsqrt(lax.optimization_barrier(jnp.mean(activations * activations, axis=-1, keepdims=True)) + EPSILON)
    return activations * row_scale * gain_row

def geglu(gate_pre, up_pre):
    return jax.nn.gelu(gate_pre, approximate=True) * up_pre

def attend_group(queries, keys_all, values_all, lengths_group, bias_table):
    scores = jnp.einsum('gqhd,gkhd->ghqk', queries, keys_all, precision=HIGHEST) * 0.125 + bias_table[None]
    scores = low_back(scores)
    positions = jnp.arange(LEN, dtype=jnp.int32)
    key_valid = positions[None, :] < lengths_group[:, None]
    scores = jnp.where(key_valid[:, None, None, :], scores, MASKED_SCORE)
    softmax_rows = jax.nn.softmax(scores, axis=-1)
    return jnp.einsum('ghqk,gkhd->gqhd', low(softmax_rows), values_all, precision=HIGHEST)

def expert_apply(items):
    expert_in, gate_w, up_w, down_w = items
    gate_pre = low_back(matmul_high(expert_in, gate_w))
    up_pre = low_back(matmul_high(expert_in, up_w))
    hidden = low(geglu(gate_pre, up_pre))
    return low_back(jnp.dot(hidden, down_w.T, precision=HIGHEST, preferred_element_type=jnp.float32))

def reference(tokens, cotangent, lengths, bucket_table, routes, gate_values, qkv_weight, out_weight, norm_gains, rel_bias, gate_weight, up_weight, down_weight):
    token_ids = jnp.arange(TOKENS, dtype=jnp.int32)
    valid_rows = (token_ids % LEN < lengths[(token_ids // LEN).astype(jnp.int32)]).astype(jnp.float32)
    offsets = jnp.arange(LEN, dtype=jnp.int32)
    bucket_index = bucket_table[(offsets[None, :] - offsets[:, None] + (LEN - 1)).astype(jnp.int32)]
    pair_expert = routes.reshape(N_DP, 2 * ROWS)
    pair_valid = jnp.repeat(valid_rows, 2).reshape(N_DP, 2 * ROWS) > 0.5
    expert_ids = jnp.arange(EXPERTS, dtype=jnp.int32)
    chosen = ((pair_expert[:, :, None] == expert_ids[None, None, :]) & pair_valid[:, :, None]).astype(jnp.int32)
    earlier = jnp.cumsum(chosen, axis=1) - chosen
    position = lax.optimization_barrier(jnp.sum(earlier * chosen, axis=2))
    kept_pair = pair_valid & (position < CAP)
    group_ids = jnp.arange(N_DP, dtype=jnp.int32)[:, None]
    target = pair_expert * (N_DP * CAP) + group_ids * CAP + position
    target = jnp.where(kept_pair, target, EXPERTS * N_DP * CAP).reshape(TOKENS, 2).astype(jnp.int32)
    pair_token = jnp.arange(2 * TOKENS, dtype=jnp.int32) // 2
    slot_token = jnp.full((EXPERTS * N_DP * CAP,), TOKENS, jnp.int32).at[target.reshape(-1)].set(pair_token, mode='drop')
    gate_float = gate_values.astype(jnp.float32)
    group_count = math.gcd(SEQS, max(1, 4096 // LEN))

    def forward(inputs, qkv_w, out_w, gains, bias_rows, gate_w, up_w, down_w):
        norm_one = low(rms_norm(inputs, gains[0]))
        queries = low_back(low(matmul_high(norm_one, qkv_w[0])))
        keys_all = low_back(low(matmul_high(norm_one, qkv_w[1])))
        values_all = low_back(low(matmul_high(norm_one, qkv_w[2])))
        bias_table = bias_rows[:, bucket_index]

        def shaped(array):
            return array.reshape(SEQS // group_count, group_count, LEN, HEADS, HEAD_DIM)

        def attend_items(items):
            return attend_group(items[0], items[1], items[2], items[3], bias_table)
        attended = lax.map(jax.checkpoint(attend_items), (shaped(queries), shaped(keys_all), shaped(values_all), lengths.reshape(SEQS // group_count, group_count)))
        attended = low_back(low(attended.reshape(TOKENS, D)))
        branch = low_back(jnp.dot(attended, out_w.T, precision=HIGHEST, preferred_element_type=jnp.float32))
        residual_mid = inputs + valid_rows[:, None] * branch
        norm_two = low(rms_norm(residual_mid, gains[1]))
        expert_in = jnp.take(norm_two, slot_token, axis=0, mode='fill', fill_value=0.0).reshape(EXPERTS, N_DP * CAP, D)
        expert_out = lax.map(jax.checkpoint(expert_apply), (expert_in, gate_w, up_w, down_w)).reshape(EXPERTS * N_DP * CAP, D)
        first_out = jnp.take(expert_out, target[:, 0], axis=0, mode='fill', fill_value=0.0)
        second_out = jnp.take(expert_out, target[:, 1], axis=0, mode='fill', fill_value=0.0)
        expert_mix = low_back(gate_float[:, 0:1] * first_out + gate_float[:, 1:2] * second_out)
        return residual_mid + valid_rows[:, None] * expert_mix
    outputs, pull = jax.vjp(forward, tokens.astype(jnp.float32), qkv_weight.astype(jnp.float32), out_weight.astype(jnp.float32), norm_gains.astype(jnp.float32), rel_bias.astype(jnp.float32), gate_weight.astype(jnp.float32), up_weight.astype(jnp.float32), down_weight.astype(jnp.float32))
    grads = pull(valid_rows[:, None] * cotangent.astype(jnp.float32))
    return (outputs.astype(jnp.bfloat16), grads[0], grads[1], grads[2], grads[3], grads[4], grads[5], grads[6], grads[7])
```

```python
import jax
import jax.numpy as jnp
from jax import lax
from jax.experimental import pallas as pl
from jax.experimental.pallas import tpu as pltpu
from jax.sharding import PartitionSpec as P

HEAD_DIM = 64
EPSILON = 1e-06
MASKED_SCORE = -1e30
HIGHEST = lax.Precision.HIGHEST
SCORE_SCALE = 0.125
QUERY_COLS = 256
LANES = 128
GELU_SCALE = 0.7978845608028654
GELU_CUBIC = 0.044715


def dot_nt(left, right):
    return lax.dot_general(
        left, right, (((1,), (1,)), ((), ())), preferred_element_type=jnp.float32
    )


def dot_nn(left, right):
    return lax.dot_general(
        left, right, (((1,), (0,)), ((), ())), preferred_element_type=jnp.float32
    )


def dot_tn(left, right):
    return lax.dot_general(
        left, right, (((0,), (0,)), ((), ())), preferred_element_type=jnp.float32
    )


def bias_base(bias_row, seq):
    return pltpu.roll(
        jnp.broadcast_to(bias_row, (LANES, 2 * seq)),
        2 * seq - (LANES - 1),
        1,
        stride=1,
        stride_axis=0,
    )


def masked_scores(keys, query_block, base_ref, start, seq, cols, length):
    scores = dot_nt(keys, query_block) * SCORE_SCALE
    blocks = []
    for first in range(0, seq, LANES):
        offset = seq - LANES - first + start
        block = scores[first : first + LANES] + base_ref[:, offset : offset + cols]
        key_index = lax.broadcasted_iota(jnp.int32, block.shape, 0) + first
        blocks.append(jnp.where(key_index < length, block, MASKED_SCORE))
    return jnp.concatenate(blocks, axis=0)


def head_part(ref, start, cols, head):
    lane = lax.broadcasted_iota(jnp.int32, (cols, LANES), 1)
    return jnp.where(
        lane // HEAD_DIM == head, ref[start : start + cols, :], jnp.zeros((), jnp.bfloat16)
    )


def forward_kernel(
    length_ref, query_ref, key_ref, value_ref, bias_ref, out_ref, total_ref, base_ref
):
    seq = query_ref.shape[0]
    cols = min(QUERY_COLS, seq)
    length = length_ref[0]
    values_t = value_ref[...].T
    keys = key_ref[...]
    starts = range(0, seq, cols)
    outs = {}
    for head in range(LANES // HEAD_DIM):
        base_ref[...] = bias_base(bias_ref[0, head : head + 1, :], seq)
        for start in starts:
            query_block = head_part(query_ref, start, cols, head)
            scores = masked_scores(keys, query_block, base_ref, start, seq, cols, length)
            top = jnp.max(scores, axis=0, keepdims=True)
            exponent = jnp.exp(scores - top)
            total = jnp.sum(exponent, axis=0, keepdims=True)
            probs = (exponent * (1.0 / total)).astype(jnp.bfloat16)
            total_ref[0, head : head + 1, start : start + cols] = top + jnp.log(total)
            outs[start, head] = dot_nn(
                values_t[head * HEAD_DIM : (head + 1) * HEAD_DIM], probs
            )
    for start in starts:
        joined = jnp.concatenate(
            [outs[start, head] for head in range(LANES // HEAD_DIM)], axis=0
        )
        out_ref[start : start + cols, :] = joined.T.astype(jnp.bfloat16)


def attend_forward(length, queries, keys, values, bias_rows):
    seq, width = queries.shape
    pairs = width // LANES
    heads = LANES // HEAD_DIM
    column = pl.BlockSpec((seq, LANES), lambda i: (0, i))
    return pl.pallas_call(
        forward_kernel,
        grid=(pairs,),
        in_specs=[
            pl.BlockSpec(memory_space=pltpu.SMEM),
            column,
            column,
            column,
            pl.BlockSpec((1, heads, 2 * seq), lambda i: (i, 0, 0)),
        ],
        out_specs=[column, pl.BlockSpec((1, heads, seq), lambda i: (i, 0, 0))],
        out_shape=[
            jax.ShapeDtypeStruct((seq, width), jnp.bfloat16),
            jax.ShapeDtypeStruct((pairs, heads, seq), jnp.float32),
        ],
        scratch_shapes=[pltpu.VMEM((LANES, 2 * seq), jnp.float32)],
        cost_estimate=pl.CostEstimate(
            flops=16 * seq * seq * width,
            transcendentals=seq * seq * width // HEAD_DIM,
            bytes_accessed=8 * seq * width,
        ),
        name="attend_forward",
    )(length, queries, keys, values, bias_rows)


def diagonal_sums(acc_ref, seq):
    period = 2 * seq
    folded = acc_ref[0:8, :]
    for first in range(8, LANES, 8):
        folded = folded + pltpu.roll(acc_ref[first : first + 8, :], period - first, 1)
    row = lax.broadcasted_iota(jnp.int32, folded.shape, 0)
    for bit in (1, 2, 4):
        folded = jnp.where((row & bit) != 0, pltpu.roll(folded, period - bit, 1), folded)
    return pltpu.roll(jnp.sum(folded, axis=0, keepdims=True), LANES - 1, 1)


def backward_kernel(
    length_ref,
    query_ref,
    key_ref,
    value_ref,
    grad_ref,
    total_ref,
    bias_ref,
    query_grad_ref,
    key_grad_ref,
    value_grad_ref,
    bias_grad_ref,
    base_ref,
    acc_ref,
):
    seq = query_ref.shape[0]
    cols = min(QUERY_COLS, seq)
    length = length_ref[0]
    keys = key_ref[...]
    values = value_ref[...]
    keys_t = keys.T
    starts = range(0, seq, cols)
    key_acc = jnp.zeros((seq, LANES), jnp.float32)
    value_acc = jnp.zeros((seq, LANES), jnp.float32)
    query_parts = {}
    for head in range(LANES // HEAD_DIM):
        base_ref[...] = bias_base(bias_ref[0, head : head + 1, :], seq)
        acc_ref[...] = jnp.zeros_like(acc_ref)
        for start in starts:
            query_block = head_part(query_ref, start, cols, head)
            grad_block = head_part(grad_ref, start, cols, head)
            scores = masked_scores(keys, query_block, base_ref, start, seq, cols, length)
            probs = jnp.exp(scores - total_ref[0, head : head + 1, start : start + cols])
            probs_grad = dot_nt(values, grad_block)
            mean_grad = jnp.sum(probs * probs_grad, axis=0, keepdims=True)
            score_grad = (probs * (probs_grad - mean_grad)).astype(jnp.bfloat16)
            value_acc = value_acc + dot_nn(probs.astype(jnp.bfloat16), grad_block)
            key_acc = key_acc + dot_nn(score_grad, query_block)
            query_parts[start, head] = dot_nn(
                keys_t[head * HEAD_DIM : (head + 1) * HEAD_DIM], score_grad
            )
            for first in range(0, seq, LANES):
                offset = seq - LANES - first + start
                acc_ref[:, offset : offset + cols] += score_grad[
                    first : first + LANES
                ].astype(jnp.float32)
        bias_grad_ref[0, head : head + 1, :] = diagonal_sums(acc_ref, seq)
    key_grad_ref[...] = (key_acc * SCORE_SCALE).astype(jnp.bfloat16)
    value_grad_ref[...] = value_acc.astype(jnp.bfloat16)
    for start in starts:
        joined = jnp.concatenate(
            [query_parts[start, head] for head in range(LANES // HEAD_DIM)], axis=0
        )
        query_grad_ref[start : start + cols, :] = (joined * SCORE_SCALE).T.astype(
            jnp.bfloat16
        )


def attend_backward(length, queries, keys, values, attended_grad, totals, bias_rows):
    seq, width = queries.shape
    pairs = width // LANES
    heads = LANES // HEAD_DIM
    column = pl.BlockSpec((seq, LANES), lambda i: (0, i))
    vector = pl.BlockSpec((1, heads, 2 * seq), lambda i: (i, 0, 0))
    grad_shape = jax.ShapeDtypeStruct((seq, width), jnp.bfloat16)
    return pl.pallas_call(
        backward_kernel,
        grid=(pairs,),
        in_specs=[
            pl.BlockSpec(memory_space=pltpu.SMEM),
            column,
            column,
            column,
            column,
            pl.BlockSpec((1, heads, seq), lambda i: (i, 0, 0)),
            vector,
        ],
        out_specs=[column, column, column, vector],
        out_shape=[
            grad_shape,
            grad_shape,
            grad_shape,
            jax.ShapeDtypeStruct((pairs, heads, 2 * seq), jnp.float32),
        ],
        scratch_shapes=[
            pltpu.VMEM((LANES, 2 * seq), jnp.float32),
            pltpu.VMEM((LANES, 2 * seq), jnp.float32),
        ],
        cost_estimate=pl.CostEstimate(
            flops=40 * seq * seq * width,
            transcendentals=seq * seq * width // HEAD_DIM,
            bytes_accessed=14 * seq * width,
        ),
        name="attend_backward",
    )(length, queries, keys, values, attended_grad, totals, bias_rows)


def gelu_parts(gate_pre):
    inner = jnp.tanh(GELU_SCALE * (gate_pre + GELU_CUBIC * gate_pre * gate_pre * gate_pre))
    gelu = 0.5 * gate_pre * (1.0 + inner)
    slope = 0.5 * (1.0 + inner) + 0.5 * gate_pre * (1.0 - inner * inner) * GELU_SCALE * (
        1.0 + 3.0 * GELU_CUBIC * gate_pre * gate_pre
    )
    return gelu, slope


def on_device(
    tokens,
    cotangent,
    lengths,
    bucket_table,
    routes,
    gate_values,
    qkv_weight,
    out_weight,
    norm_gains,
    rel_bias,
    gate_weight,
    up_weight,
    down_weight,
):
    tok_rows, width = tokens.shape
    half = width // 2
    dp_count = lax.axis_size("dp")
    tensor_count = lax.axis_size("tensor")
    seq = tok_rows * tensor_count
    expert_count, shard_rows, hidden_cols = gate_weight.shape
    head_cols = qkv_weight.shape[2]
    head_count, bucket_count = rel_bias.shape
    capacity = 9 * seq // 64
    group_size = dp_count // expert_count
    slot_count = (capacity + group_size - 1) // group_size
    total_slots = dp_count * slot_count
    dp_index = lax.axis_index("dp")
    tensor_index = lax.axis_index("tensor")
    first_tensor = tensor_index == 0
    length = lengths[dp_index]
    length_row = length[None]
    group_valid = jnp.arange(seq, dtype=jnp.int32) < length
    own_valid = lax.dynamic_slice_in_dim(group_valid, tensor_index * tok_rows, tok_rows, 0)
    own_valid = own_valid.astype(jnp.float32)[:, None]

    def swap(block):
        return lax.ppermute(block, "tensor", [(0, 1), (1, 0)])

    def after(block, *earlier):
        return lax.optimization_barrier((block, *earlier))[0]

    def ordered(own, other, axis):
        return jnp.where(
            first_tensor,
            jnp.concatenate([own, other], axis=axis),
            jnp.concatenate([other, own], axis=axis),
        )

    def own_part(block, axis):
        size = block.shape[axis] // 2
        return lax.dynamic_slice_in_dim(block, tensor_index * size, size, axis)

    def other_part(block, axis):
        size = block.shape[axis] // 2
        return lax.dynamic_slice_in_dim(block, (1 - tensor_index) * size, size, axis)

    def exchange(block):
        return lax.all_to_all(block, "dp", split_axis=0, concat_axis=0, tiled=True)

    def home_order(weight):
        return jnp.repeat(weight, group_size, axis=0)

    def fetch(weight, *earlier):
        arrived = exchange(after(home_order(weight), *earlier))
        return arrived.reshape(dp_count * shard_rows, weight.shape[2])

    def send_grad(grad, *earlier):
        return exchange(after(grad.reshape(dp_count, shard_rows, grad.shape[1]), *earlier))

    def route(rows, *earlier):
        arrived = exchange(after(rows.reshape(dp_count, slot_count, rows.shape[1]), *earlier))
        return arrived.reshape(total_slots, rows.shape[1])

    def regroup(arrived):
        return jnp.sum(
            arrived.astype(jnp.float32).reshape(
                expert_count, group_size, shard_rows, arrived.shape[2]
            ),
            axis=1,
        )

    gain_pad = jnp.pad(norm_gains, ((0, 14), (0, head_cols - shard_rows)))
    layer_shard = jnp.concatenate(
        [qkv_weight.reshape(3 * shard_rows, head_cols), gain_pad], axis=0
    )
    layer_all = lax.all_gather(layer_shard, "dp", axis=0, tiled=False)
    tokens_other = swap(tokens)
    mix_grad = (own_valid * cotangent.astype(jnp.float32)).astype(jnp.bfloat16)
    mix_other = swap(other_part(mix_grad, 1))
    out_all = lax.all_gather(out_weight, "dp", axis=0, tiled=True)
    gate_up_all = fetch(jnp.concatenate([gate_weight, up_weight], axis=2))

    pair_expert = routes.reshape(-1)
    pair_valid = jnp.repeat(group_valid, 2)
    chosen = (
        pair_expert[:, None] == jnp.arange(expert_count, dtype=jnp.int32)[None, :]
    ) & pair_valid[:, None]
    pair_index = jnp.arange(2 * seq, dtype=jnp.int32)
    before = (pair_index[:, None] > pair_index[None, :]).astype(jnp.bfloat16)
    earlier_pairs = dot_nn(before, chosen.astype(jnp.bfloat16))
    position = jnp.sum(jnp.where(chosen, earlier_pairs, 0.0), axis=1).astype(jnp.int32)
    kept_pair = pair_valid & (position < capacity)
    device = pair_expert * group_size + position // slot_count
    pair_slot = jnp.where(
        kept_pair, device * slot_count + position % slot_count, total_slots
    ).reshape(seq, 2)
    slot_index = jnp.arange(total_slots, dtype=jnp.int32)
    first_hit = pair_slot[:, 0][None, :] == slot_index[:, None]
    second_hit = pair_slot[:, 1][None, :] == slot_index[:, None]
    no_gate = jnp.zeros((), jnp.bfloat16)
    pick = (first_hit | second_hit).astype(jnp.bfloat16)
    pick_gate = jnp.where(
        first_hit,
        gate_values[:, 0][None, :],
        jnp.where(second_hit, gate_values[:, 1][None, :], no_gate),
    )

    out_grad_cols = dot_nn(
        pick_gate, ordered(own_part(mix_grad, 1), mix_other, 0)
    ).astype(jnp.bfloat16)
    slot_grad_half = route(out_grad_cols, gate_up_all)
    slot_grad = ordered(slot_grad_half, swap(slot_grad_half), 1)

    distance = jnp.arange(2 * seq, dtype=jnp.int32)
    table_reversed = jnp.concatenate(
        [bucket_table[::-1], jnp.full((1,), bucket_count, jnp.int32)]
    )
    hot = (
        jnp.arange(bucket_count, dtype=jnp.int32)[:, None] == table_reversed[None, :]
    ).astype(jnp.float32)
    bias_rows = jnp.dot(rel_bias.astype(jnp.float32), hot, precision=HIGHEST).reshape(
        head_count // 2, 2, 2 * seq
    )
    gains_all = jnp.transpose(
        layer_all[:, 3 * shard_rows : 3 * shard_rows + 2, :shard_rows], (1, 0, 2)
    ).reshape(2, width)
    gain_one = gains_all[0].astype(jnp.float32)
    gain_two = gains_all[1].astype(jnp.float32)
    projections = [
        layer_all[:, i * shard_rows : (i + 1) * shard_rows].reshape(width, head_cols)
        for i in range(3)
    ]
    inputs_all = ordered(tokens, tokens_other, 0).astype(jnp.float32)
    scale_all = lax.rsqrt(jnp.mean(inputs_all * inputs_all, axis=-1, keepdims=True) + EPSILON)
    norm_one_all = (inputs_all * scale_all * gain_one).astype(jnp.bfloat16)
    queries, keys, values = [
        dot_nn(norm_one_all, weight).astype(jnp.bfloat16) for weight in projections
    ]
    attended, totals = attend_forward(length_row, queries, keys, values, bias_rows)
    branch = dot_nt(attended, out_all)
    branch_other = swap(other_part(branch, 0).astype(jnp.bfloat16))
    inputs = tokens.astype(jnp.float32)
    mid = inputs + own_valid * (own_part(branch, 0) + branch_other.astype(jnp.float32))
    mid_scale = lax.rsqrt(jnp.mean(mid * mid, axis=-1, keepdims=True) + EPSILON)
    norm_two = (mid * mid_scale * gain_two).astype(jnp.bfloat16)
    norm_two_cols = ordered(own_part(norm_two, 1), swap(other_part(norm_two, 1)), 0)
    expert_half = route(
        dot_nn(pick, norm_two_cols).astype(jnp.bfloat16), slot_grad_half
    )
    down_all = fetch(down_weight, expert_half)
    expert_in = ordered(expert_half, swap(expert_half), 1)

    pre = dot_nn(expert_in, gate_up_all)
    gate_pre = pre[:, :hidden_cols]
    up_pre = pre[:, hidden_cols:]
    gelu, slope = gelu_parts(gate_pre)
    hidden = (gelu * up_pre).astype(jnp.bfloat16)
    down_back = send_grad(dot_tn(slot_grad, hidden).astype(jnp.bfloat16), down_all)
    hidden_grad = dot_nn(slot_grad, down_all)
    pre_grad = jnp.concatenate(
        [
            (hidden_grad * up_pre * slope).astype(jnp.bfloat16),
            (hidden_grad * gelu).astype(jnp.bfloat16),
        ],
        axis=1,
    )
    slot_back_part = dot_nt(pre_grad, gate_up_all)
    slot_back_half = (
        own_part(slot_back_part, 1)
        + swap(other_part(slot_back_part, 1).astype(jnp.bfloat16)).astype(jnp.float32)
    ).astype(jnp.bfloat16)
    slot_back = route(slot_back_half, down_back)
    expert_out_part = dot_nt(hidden, down_all)
    expert_out_half = (
        own_part(expert_out_part, 1)
        + swap(other_part(expert_out_part, 1).astype(jnp.bfloat16)).astype(jnp.float32)
    ).astype(jnp.bfloat16)
    returned = route(expert_out_half, slot_back)
    gate_up_back = send_grad(dot_tn(expert_in, pre_grad).astype(jnp.bfloat16), returned)

    mix_cols = dot_tn(pick_gate, returned)
    mix_own = ordered(
        own_part(mix_cols, 0), swap(other_part(mix_cols, 0).astype(jnp.bfloat16)).astype(jnp.float32), 1
    )
    mixed = (mid + own_valid * mix_own).astype(jnp.bfloat16)
    back_cols = dot_tn(pick, slot_back)
    norm_two_grad = ordered(
        own_part(back_cols, 0), swap(other_part(back_cols, 0).astype(jnp.bfloat16)).astype(jnp.float32), 1
    )
    mid_unit = mid * mid_scale
    mid_inner = norm_two_grad * gain_two
    mid_grad = own_valid * cotangent.astype(jnp.float32) + mid_scale * (
        mid_inner - mid_unit * jnp.mean(mid_inner * mid_unit, axis=-1, keepdims=True)
    )
    gain_two_grad = jnp.sum(norm_two_grad * mid_unit, axis=0)
    branch_grad = (own_valid * mid_grad).astype(jnp.bfloat16)
    branch_grad_all = ordered(branch_grad, swap(branch_grad), 0)

    attended_grad = dot_nn(branch_grad_all, out_all).astype(jnp.bfloat16)
    out_part = dot_tn(branch_grad_all, attended).astype(jnp.bfloat16)
    out_grad = lax.psum_scatter(out_part, "dp", scatter_dimension=0, tiled=True)
    query_grad, key_grad, value_grad, bias_sums = attend_backward(
        length_row, queries, keys, values, attended_grad, totals, bias_rows
    )
    bias_grad = jnp.dot(
        bias_sums.reshape(head_count, 2 * seq), hot.T, precision=HIGHEST
    )
    norm_one_part = (
        dot_nt(query_grad, projections[0])
        + dot_nt(key_grad, projections[1])
        + dot_nt(value_grad, projections[2])
    )
    qkv_part = jnp.stack(
        [
            dot_tn(norm_one_all, grad).astype(jnp.bfloat16)
            for grad in (query_grad, key_grad, value_grad)
        ]
    )
    qkv_grad = lax.psum_scatter(qkv_part, "dp", scatter_dimension=1, tiled=True)
    gain_one_grad = jnp.sum(norm_one_part * (inputs_all * scale_all), axis=0)
    norm_one_grad = own_part(norm_one_part, 0) + swap(
        other_part(norm_one_part, 0).astype(jnp.bfloat16)
    ).astype(jnp.float32)
    scale = lax.rsqrt(jnp.mean(inputs * inputs, axis=-1, keepdims=True) + EPSILON)
    unit = inputs * scale
    inner = norm_one_grad * gain_one
    input_grad = mid_grad + scale * (
        inner - unit * jnp.mean(inner * unit, axis=-1, keepdims=True)
    )

    bias_full = lax.dynamic_update_slice_in_dim(
        jnp.zeros((head_count * tensor_count, bucket_count), jnp.float32),
        bias_grad,
        tensor_index * head_count,
        0,
    )
    gain_sums, bias_sums = lax.psum(
        (jnp.stack([gain_one_grad, gain_two_grad]), bias_full), ("dp", "tensor")
    )
    gains_grad = lax.dynamic_slice_in_dim(gain_sums, dp_index * shard_rows, shard_rows, 1)
    bias_out = lax.dynamic_slice_in_dim(bias_sums, tensor_index * head_count, head_count, 0)
    return (
        mixed,
        input_grad,
        qkv_grad.astype(jnp.float32),
        out_grad.astype(jnp.float32),
        gains_grad,
        bias_out,
        regroup(gate_up_back[:, :, :hidden_cols]),
        regroup(gate_up_back[:, :, hidden_cols:]),
        regroup(down_back),
    )


def solution(mesh):
    rows = P(("dp", "tensor"), None)
    shard = P("dp", "tensor")
    stacked = P(None, "dp", "tensor")
    return jax.shard_map(
        on_device,
        mesh=mesh,
        in_specs=(
            rows,
            rows,
            P(),
            P(),
            P("dp", None),
            P("dp", None),
            stacked,
            shard,
            P(None, "dp"),
            P("tensor", None),
            stacked,
            stacked,
            stacked,
        ),
        out_specs=(
            rows,
            rows,
            stacked,
            shard,
            P(None, "dp"),
            P("tensor", None),
            stacked,
            stacked,
            stacked,
        ),
        check_vma=False,
    )
```

```python
import jax
import jax.numpy as jnp
from jax import lax
from jax.experimental import pallas as pl
from jax.experimental.pallas import tpu as pltpu
from jax.sharding import PartitionSpec as P

HEAD_DIM = 64
EPSILON = 1e-06
MASKED_SCORE = -1e30
HIGHEST = lax.Precision.HIGHEST
SCORE_SCALE = 0.125
QUERY_COLS = 256
LANES = 128
GELU_SCALE = 0.7978845608028654
GELU_CUBIC = 0.044715
GAIN_ROWS = 16


def dot_nt(left, right):
    return lax.dot_general(
        left, right, (((1,), (1,)), ((), ())), preferred_element_type=jnp.float32
    )


def dot_nn(left, right):
    return lax.dot_general(
        left, right, (((1,), (0,)), ((), ())), preferred_element_type=jnp.float32
    )


def dot_tn(left, right):
    return lax.dot_general(
        left, right, (((0,), (0,)), ((), ())), preferred_element_type=jnp.float32
    )


def bias_base(bias_row, seq):
    return pltpu.roll(
        jnp.broadcast_to(bias_row, (LANES, 2 * seq)),
        2 * seq - (LANES - 1),
        1,
        stride=1,
        stride_axis=0,
    )


def masked_scores(keys, query_block, base_ref, start, seq, cols, length):
    scores = dot_nt(keys, query_block) * SCORE_SCALE
    blocks = []
    for first in range(0, seq, LANES):
        offset = seq - LANES - first + start
        block = scores[first : first + LANES] + base_ref[:, offset : offset + cols]
        key_index = lax.broadcasted_iota(jnp.int32, block.shape, 0) + first
        blocks.append(jnp.where(key_index < length, block, MASKED_SCORE))
    return jnp.concatenate(blocks, axis=0)


def head_part(ref, start, cols, head):
    lane = lax.broadcasted_iota(jnp.int32, (cols, LANES), 1)
    return jnp.where(
        lane // HEAD_DIM == head, ref[start : start + cols, :], jnp.zeros((), jnp.bfloat16)
    )


def forward_kernel(length_ref, joined_ref, bias_ref, out_ref, total_ref, base_ref):
    query_ref, key_ref, value_ref = [
        joined_ref.at[:, i * LANES : (i + 1) * LANES] for i in range(3)
    ]
    seq = joined_ref.shape[0]
    cols = min(QUERY_COLS, seq)
    length = length_ref[0]
    values_t = value_ref[...].T
    keys = key_ref[...]
    starts = range(0, seq, cols)
    outs = {}
    for head in range(LANES // HEAD_DIM):
        base_ref[...] = bias_base(bias_ref[0, head : head + 1, :], seq)
        for start in starts:
            query_block = head_part(query_ref, start, cols, head)
            scores = masked_scores(keys, query_block, base_ref, start, seq, cols, length)
            top = jnp.max(scores, axis=0, keepdims=True)
            exponent = jnp.exp(scores - top)
            total = jnp.sum(exponent, axis=0, keepdims=True)
            probs = (exponent * (1.0 / total)).astype(jnp.bfloat16)
            total_ref[0, head : head + 1, start : start + cols] = top + jnp.log(total)
            outs[start, head] = dot_nn(
                values_t[head * HEAD_DIM : (head + 1) * HEAD_DIM], probs
            )
    for start in starts:
        joined = jnp.concatenate(
            [outs[start, head] for head in range(LANES // HEAD_DIM)], axis=0
        )
        out_ref[start : start + cols, :] = joined.T.astype(jnp.bfloat16)


def attend_forward(length, joined, bias_rows):
    seq = joined.shape[0]
    width = joined.shape[1] // 3
    pairs = width // LANES
    heads = LANES // HEAD_DIM
    column = pl.BlockSpec((seq, LANES), lambda i: (0, i))
    return pl.pallas_call(
        forward_kernel,
        grid=(pairs,),
        in_specs=[
            pl.BlockSpec(memory_space=pltpu.SMEM),
            pl.BlockSpec((seq, 3 * LANES), lambda i: (0, i)),
            pl.BlockSpec((1, heads, 2 * seq), lambda i: (i, 0, 0)),
        ],
        out_specs=[column, pl.BlockSpec((1, heads, seq), lambda i: (i, 0, 0))],
        out_shape=[
            jax.ShapeDtypeStruct((seq, width), jnp.bfloat16),
            jax.ShapeDtypeStruct((pairs, heads, seq), jnp.float32),
        ],
        scratch_shapes=[pltpu.VMEM((LANES, 2 * seq), jnp.float32)],
        cost_estimate=pl.CostEstimate(
            flops=16 * seq * seq * width,
            transcendentals=seq * seq * width // HEAD_DIM,
            bytes_accessed=8 * seq * width,
        ),
        name="attend_forward",
    )(length, joined, bias_rows)


def diagonal_sums(acc_ref, seq):
    period = 2 * seq
    folded = acc_ref[0:8, :]
    for first in range(8, LANES, 8):
        folded = folded + pltpu.roll(acc_ref[first : first + 8, :], period - first, 1)
    row = lax.broadcasted_iota(jnp.int32, folded.shape, 0)
    for bit in (1, 2, 4):
        folded = jnp.where((row & bit) != 0, pltpu.roll(folded, period - bit, 1), folded)
    return pltpu.roll(jnp.sum(folded, axis=0, keepdims=True), LANES - 1, 1)


def backward_kernel(
    length_ref,
    joined_ref,
    grad_ref,
    total_ref,
    bias_ref,
    joined_grad_ref,
    bias_grad_ref,
    base_ref,
    acc_ref,
):
    query_ref, key_ref, value_ref = [
        joined_ref.at[:, i * LANES : (i + 1) * LANES] for i in range(3)
    ]
    seq = joined_ref.shape[0]
    cols = min(QUERY_COLS, seq)
    length = length_ref[0]
    keys = key_ref[...]
    values = value_ref[...]
    keys_t = keys.T
    starts = range(0, seq, cols)
    key_acc = jnp.zeros((seq, LANES), jnp.float32)
    value_acc = jnp.zeros((seq, LANES), jnp.float32)
    query_parts = {}
    for head in range(LANES // HEAD_DIM):
        base_ref[...] = bias_base(bias_ref[0, head : head + 1, :], seq)
        acc_ref[...] = jnp.zeros_like(acc_ref)
        for start in starts:
            query_block = head_part(query_ref, start, cols, head)
            grad_block = head_part(grad_ref, start, cols, head)
            scores = masked_scores(keys, query_block, base_ref, start, seq, cols, length)
            probs = jnp.exp(scores - total_ref[0, head : head + 1, start : start + cols])
            probs_grad = dot_nt(values, grad_block)
            mean_grad = jnp.sum(probs * probs_grad, axis=0, keepdims=True)
            score_grad = (probs * (probs_grad - mean_grad)).astype(jnp.bfloat16)
            value_acc = value_acc + dot_nn(probs.astype(jnp.bfloat16), grad_block)
            key_acc = key_acc + dot_nn(score_grad, query_block)
            query_parts[start, head] = dot_nn(
                keys_t[head * HEAD_DIM : (head + 1) * HEAD_DIM], score_grad
            )
            for first in range(0, seq, LANES):
                offset = seq - LANES - first + start
                acc_ref[:, offset : offset + cols] += score_grad[
                    first : first + LANES
                ].astype(jnp.float32)
        bias_grad_ref[0, head : head + 1, :] = diagonal_sums(acc_ref, seq)
    joined_grad_ref[:, LANES : 2 * LANES] = (key_acc * SCORE_SCALE).astype(jnp.bfloat16)
    joined_grad_ref[:, 2 * LANES :] = value_acc.astype(jnp.bfloat16)
    for start in starts:
        joined = jnp.concatenate(
            [query_parts[start, head] for head in range(LANES // HEAD_DIM)], axis=0
        )
        joined_grad_ref[start : start + cols, :LANES] = (joined * SCORE_SCALE).T.astype(
            jnp.bfloat16
        )


def attend_backward(length, joined, attended_grad, totals, bias_rows):
    seq, width = attended_grad.shape
    pairs = width // LANES
    heads = LANES // HEAD_DIM
    column = pl.BlockSpec((seq, LANES), lambda i: (0, i))
    triple = pl.BlockSpec((seq, 3 * LANES), lambda i: (0, i))
    vector = pl.BlockSpec((1, heads, 2 * seq), lambda i: (i, 0, 0))
    return pl.pallas_call(
        backward_kernel,
        grid=(pairs,),
        in_specs=[
            pl.BlockSpec(memory_space=pltpu.SMEM),
            triple,
            column,
            pl.BlockSpec((1, heads, seq), lambda i: (i, 0, 0)),
            vector,
        ],
        out_specs=[triple, vector],
        out_shape=[
            jax.ShapeDtypeStruct((seq, 3 * width), jnp.bfloat16),
            jax.ShapeDtypeStruct((pairs, heads, 2 * seq), jnp.float32),
        ],
        scratch_shapes=[
            pltpu.VMEM((LANES, 2 * seq), jnp.float32),
            pltpu.VMEM((LANES, 2 * seq), jnp.float32),
        ],
        cost_estimate=pl.CostEstimate(
            flops=40 * seq * seq * width,
            transcendentals=seq * seq * width // HEAD_DIM,
            bytes_accessed=14 * seq * width,
        ),
        name="attend_backward",
    )(length, joined, attended_grad, totals, bias_rows)


def assemble_kernel(place_ref, *refs):
    parts, (weight_ref, out_ref, gain_ref) = refs[:-3], refs[-3:]
    rows = weight_ref.shape[0]
    pairs = weight_ref.shape[1] // (3 * LANES)
    wanted = pl.program_id(1) ^ place_ref[1]
    for index, part_ref in enumerate(parts):

        @pl.when(wanted == index)
        def _(part_ref=part_ref):
            for kind in range(3):
                for pair in range(pairs):
                    first = (3 * pair + kind) * LANES
                    weight_ref[:, first : first + LANES] = part_ref[
                        0, kind * rows : (kind + 1) * rows, pair * LANES : (pair + 1) * LANES
                    ]
            out_ref[...] = part_ref[0, 3 * rows : 4 * rows, :]
            gain_ref[0] = part_ref[0, 4 * rows :, :]


def assemble(place, parts):
    outer, block_rows, cols = parts[0].shape
    inner = len(parts)
    rows = (block_rows - GAIN_ROWS) // 4
    block = pl.BlockSpec(
        (1, block_rows, cols), lambda i, j, place_ref: (i ^ place_ref[0], 0, 0)
    )
    return pl.pallas_call(
        assemble_kernel,
        grid_spec=pltpu.PrefetchScalarGridSpec(
            num_scalar_prefetch=1,
            grid=(outer, inner),
            in_specs=[block] * inner,
            out_specs=[
                pl.BlockSpec((rows, 3 * cols), lambda i, j, place_ref: (i * inner + j, 0)),
                pl.BlockSpec((rows, cols), lambda i, j, place_ref: (i * inner + j, 0)),
                pl.BlockSpec(
                    (1, GAIN_ROWS, cols), lambda i, j, place_ref: (i * inner + j, 0, 0)
                ),
            ],
        ),
        out_shape=[
            jax.ShapeDtypeStruct((outer * inner * rows, 3 * cols), jnp.bfloat16),
            jax.ShapeDtypeStruct((outer * inner * rows, cols), jnp.bfloat16),
            jax.ShapeDtypeStruct((outer * inner, GAIN_ROWS, cols), jnp.bfloat16),
        ],
        name="assemble",
    )(place, *parts)


def gelu_parts(gate_pre):
    inner = jnp.tanh(GELU_SCALE * (gate_pre + GELU_CUBIC * gate_pre * gate_pre * gate_pre))
    gelu = 0.5 * gate_pre * (1.0 + inner)
    slope = 0.5 * (1.0 + inner) + 0.5 * gate_pre * (1.0 - inner * inner) * GELU_SCALE * (
        1.0 + 3.0 * GELU_CUBIC * gate_pre * gate_pre
    )
    return gelu, slope


def on_device(
    tokens,
    cotangent,
    lengths,
    bucket_table,
    routes,
    gate_values,
    qkv_weight,
    out_weight,
    norm_gains,
    rel_bias,
    gate_weight,
    up_weight,
    down_weight,
):
    tok_rows, width = tokens.shape
    half = width // 2
    dp_count = lax.axis_size("dp")
    tensor_count = lax.axis_size("tensor")
    seq = tok_rows * tensor_count
    expert_count, shard_rows, hidden_cols = gate_weight.shape
    head_cols = qkv_weight.shape[2]
    head_count, bucket_count = rel_bias.shape
    capacity = 9 * seq // 64
    group_size = dp_count // expert_count
    slot_count = (capacity + group_size - 1) // group_size
    total_slots = dp_count * slot_count
    dp_index = lax.axis_index("dp")
    tensor_index = lax.axis_index("tensor")
    first_tensor = tensor_index == 0
    length = lengths[dp_index]
    length_row = length[None]
    group_valid = jnp.arange(seq, dtype=jnp.int32) < length
    own_valid = lax.dynamic_slice_in_dim(group_valid, tensor_index * tok_rows, tok_rows, 0)
    own_valid = own_valid.astype(jnp.float32)[:, None]

    def swap(block):
        return lax.ppermute(block, "tensor", [(0, 1), (1, 0)])

    def chain(block, earlier):
        return lax.optimization_barrier((block, earlier))

    def ordered(own, other, axis):
        return jnp.where(
            first_tensor,
            jnp.concatenate([own, other], axis=axis),
            jnp.concatenate([other, own], axis=axis),
        )

    def own_part(block, axis):
        size = block.shape[axis] // 2
        return lax.dynamic_slice_in_dim(block, tensor_index * size, size, axis)

    def other_part(block, axis):
        size = block.shape[axis] // 2
        return lax.dynamic_slice_in_dim(block, (1 - tensor_index) * size, size, axis)

    def exchange(block):
        return lax.all_to_all(block, "dp", split_axis=0, concat_axis=0, tiled=True)

    def home_order(weight):
        return jnp.repeat(weight, group_size, axis=0)

    def fetch(weight):
        return exchange(home_order(weight)).reshape(dp_count * shard_rows, weight.shape[2])

    def send_grad(grad):
        return exchange(grad.reshape(dp_count, shard_rows, grad.shape[1]))

    def route(rows):
        arrived = exchange(rows.reshape(dp_count, slot_count, rows.shape[1]))
        return arrived.reshape(total_slots, rows.shape[1])

    def regroup(arrived):
        return jnp.sum(
            arrived.astype(jnp.float32).reshape(
                expert_count, group_size, shard_rows, arrived.shape[2]
            ),
            axis=1,
        )

    gain_pad = jnp.pad(norm_gains, ((0, GAIN_ROWS - 2), (0, head_cols - shard_rows)))
    layer_shard = jnp.concatenate(
        [qkv_weight.reshape(3 * shard_rows, head_cols), out_weight, gain_pad], axis=0
    )
    pairs = head_cols // LANES
    pair_expert = routes.reshape(-1)
    pair_valid = jnp.repeat(group_valid, 2)
    chosen = (
        pair_expert[:, None] == jnp.arange(expert_count, dtype=jnp.int32)[None, :]
    ) & pair_valid[:, None]
    pair_index = jnp.arange(2 * seq, dtype=jnp.int32)
    before = (pair_index[:, None] > pair_index[None, :]).astype(jnp.bfloat16)
    earlier_pairs = dot_nn(before, chosen.astype(jnp.bfloat16))
    position = jnp.sum(jnp.where(chosen, earlier_pairs, 0.0), axis=1).astype(jnp.int32)
    kept_pair = pair_valid & (position < capacity)
    device = pair_expert * group_size + position // slot_count
    pair_slot = jnp.where(
        kept_pair, device * slot_count + position % slot_count, total_slots
    ).reshape(seq, 2)
    slot_index = jnp.arange(total_slots, dtype=jnp.int32)
    first_hit = pair_slot[:, 0][None, :] == slot_index[:, None]
    second_hit = pair_slot[:, 1][None, :] == slot_index[:, None]
    no_gate = jnp.zeros((), jnp.bfloat16)
    pick = (first_hit | second_hit).astype(jnp.bfloat16)
    pick_gate = jnp.where(
        first_hit,
        gate_values[:, 0][None, :],
        jnp.where(second_hit, gate_values[:, 1][None, :], no_gate),
    )

    tokens_other = swap(tokens)
    mix_grad = lax.optimization_barrier(
        (own_valid * cotangent.astype(jnp.float32)).astype(jnp.bfloat16)
    )
    mix_other = swap(other_part(mix_grad, 1))
    out_grad_cols = dot_nn(
        pick_gate, ordered(own_part(mix_grad, 1), mix_other, 0)
    ).astype(jnp.bfloat16)
    residual, out_grad_cols = chain(tokens, out_grad_cols)
    gate_up = jnp.concatenate([gate_weight, up_weight], axis=2)
    if dp_count == 16:
        across = [
            lax.ppermute(layer_shard, "dp", [(i, i ^ (4 * k)) for i in range(16)])
            for k in range(1, 4)
        ]
        gate_up, across = chain(gate_up, across)
        near = jnp.stack([layer_shard, *across])
        side = lax.ppermute(near, "dp", [(i, i ^ 2) for i in range(16)])
        core = [(i, i ^ 1) for i in range(16)]
        parts = [near, lax.ppermute(near, "dp", core), side, lax.ppermute(side, "dp", core)]
        place = jnp.stack([dp_index // 4, dp_index % 4])
        projection, out_all, gain_rows = assemble(place, parts)
    else:
        layer_all = lax.all_gather(layer_shard, "dp", axis=0, tiled=False)
        gate_up, layer_all = chain(gate_up, layer_all)
        projection = (
            layer_all[:, : 3 * shard_rows]
            .reshape(dp_count, 3, shard_rows, pairs, LANES)
            .transpose(0, 2, 3, 1, 4)
            .reshape(width, 3 * head_cols)
        )
        out_all = layer_all[:, 3 * shard_rows : 4 * shard_rows].reshape(width, head_cols)
        gain_rows = layer_all[:, 4 * shard_rows :]
    out_grad_cols, gate_up_all = chain(out_grad_cols, fetch(gate_up))
    slot_grad_half = route(out_grad_cols)

    distance = jnp.arange(2 * seq, dtype=jnp.int32)
    table_reversed = jnp.concatenate(
        [bucket_table[::-1], jnp.full((1,), bucket_count, jnp.int32)]
    )
    hot = (
        jnp.arange(bucket_count, dtype=jnp.int32)[:, None] == table_reversed[None, :]
    ).astype(jnp.float32)
    bias_rows = jnp.dot(rel_bias.astype(jnp.float32), hot, precision=HIGHEST).reshape(
        head_count // 2, 2, 2 * seq
    )
    gains_all = jnp.transpose(gain_rows[:, :2, :shard_rows], (1, 0, 2)).reshape(2, width)
    gain_one = gains_all[0].astype(jnp.float32)
    gain_two = gains_all[1].astype(jnp.float32)
    inputs_all = ordered(tokens, tokens_other, 0).astype(jnp.float32)
    scale_all = lax.rsqrt(jnp.mean(inputs_all * inputs_all, axis=-1, keepdims=True) + EPSILON)
    norm_one_all = (inputs_all * scale_all * gain_one).astype(jnp.bfloat16)
    joined = dot_nn(norm_one_all, projection).astype(jnp.bfloat16)
    attended, totals = attend_forward(length_row, joined, bias_rows)
    branch = dot_nt(attended, out_all)
    branch_other = swap(other_part(branch, 0).astype(jnp.bfloat16))
    inputs = residual.astype(jnp.float32)
    mid = inputs + own_valid * (own_part(branch, 0) + branch_other.astype(jnp.float32))
    mid_scale = lax.rsqrt(jnp.mean(mid * mid, axis=-1, keepdims=True) + EPSILON)
    norm_two = (mid * mid_scale * gain_two).astype(jnp.bfloat16)
    norm_two_away, gate_up_all = chain(other_part(norm_two, 1), gate_up_all)
    norm_two_cols = ordered(own_part(norm_two, 1), swap(norm_two_away), 0)
    expert_rows, slot_grad_half = chain(
        dot_nn(pick, norm_two_cols).astype(jnp.bfloat16), slot_grad_half
    )
    slot_grad_other = swap(slot_grad_half)
    down_late, (expert_half, slot_grad_other) = chain(
        down_weight, (route(expert_rows), slot_grad_other)
    )
    down_all = fetch(down_late)
    expert_in = ordered(expert_half, swap(expert_half), 1)
    slot_grad = ordered(slot_grad_half, slot_grad_other, 1)

    pre = dot_nn(expert_in, gate_up_all)
    gate_pre = pre[:, :hidden_cols]
    up_pre = pre[:, hidden_cols:]
    gelu, slope = gelu_parts(gate_pre)
    hidden = lax.optimization_barrier((gelu * up_pre).astype(jnp.bfloat16))
    down_grad, down_all = chain(dot_tn(slot_grad, hidden).astype(jnp.bfloat16), down_all)
    down_back = send_grad(down_grad)
    hidden_grad = dot_nn(slot_grad, down_all)
    pre_grad = jnp.concatenate(
        [
            (hidden_grad * up_pre * slope).astype(jnp.bfloat16),
            (hidden_grad * gelu).astype(jnp.bfloat16),
        ],
        axis=1,
    )
    slot_back_part = dot_nt(pre_grad, gate_up_all)
    slot_back_away = other_part(slot_back_part, 1).astype(jnp.bfloat16)
    hidden_late, slot_back_away = chain(hidden, slot_back_away)
    slot_back_other = swap(slot_back_away)
    expert_out_part = dot_nt(hidden_late, down_all)
    expert_out_away, slot_back_other = chain(
        other_part(expert_out_part, 1).astype(jnp.bfloat16), slot_back_other
    )
    slot_back_half = (
        own_part(slot_back_part, 1) + slot_back_other.astype(jnp.float32)
    ).astype(jnp.bfloat16)
    expert_out_half = (
        own_part(expert_out_part, 1) + swap(expert_out_away).astype(jnp.float32)
    ).astype(jnp.bfloat16)
    slot_back_half, down_back = chain(slot_back_half, down_back)
    expert_out_half, slot_back = chain(expert_out_half, route(slot_back_half))
    gate_up_grad, returned = chain(
        dot_tn(expert_in, pre_grad).astype(jnp.bfloat16), route(expert_out_half)
    )
    gate_up_back = send_grad(gate_up_grad)

    mix_cols = dot_tn(pick_gate, returned)
    mix_own = ordered(
        own_part(mix_cols, 0), swap(other_part(mix_cols, 0).astype(jnp.bfloat16)).astype(jnp.float32), 1
    )
    mixed = (mid + own_valid * mix_own).astype(jnp.bfloat16)
    back_cols = dot_tn(pick, slot_back)
    norm_two_grad = ordered(
        own_part(back_cols, 0), swap(other_part(back_cols, 0).astype(jnp.bfloat16)).astype(jnp.float32), 1
    )
    mid_unit = mid * mid_scale
    mid_inner = norm_two_grad * gain_two
    mid_grad = own_valid * cotangent.astype(jnp.float32) + mid_scale * (
        mid_inner - mid_unit * jnp.mean(mid_inner * mid_unit, axis=-1, keepdims=True)
    )
    gain_two_grad = jnp.sum(norm_two_grad * mid_unit, axis=0)
    branch_grad = (own_valid * mid_grad).astype(jnp.bfloat16)
    branch_grad_all = ordered(branch_grad, swap(branch_grad), 0)

    attended_grad = dot_nn(branch_grad_all, out_all).astype(jnp.bfloat16)
    joined_grad, bias_sums = attend_backward(
        length_row, joined, attended_grad, totals, bias_rows
    )
    bias_grad = jnp.dot(
        bias_sums.reshape(head_count, 2 * seq), hot.T, precision=HIGHEST
    )
    norm_one_part = dot_nt(joined_grad, projection)
    layer_part = jnp.concatenate(
        [
            dot_tn(norm_one_all, joined_grad).astype(jnp.bfloat16),
            dot_tn(branch_grad_all, attended).astype(jnp.bfloat16),
        ],
        axis=1,
    )
    if dp_count == 16:
        blocks = layer_part.reshape(dp_count, shard_rows, layer_part.shape[1])
        for step in (1, 2):
            pieces = blocks.reshape(-1, 2, shard_rows, blocks.shape[2])
            bit = (dp_index // step) % 2
            away = lax.dynamic_index_in_dim(pieces, 1 - bit, 1, keepdims=False)
            stay = lax.dynamic_index_in_dim(pieces, bit, 1, keepdims=False)
            arrived = lax.ppermute(away, "dp", [(i, i ^ step) for i in range(dp_count)])
            blocks = (stay.astype(jnp.float32) + arrived.astype(jnp.float32)).astype(
                jnp.bfloat16
            )
        place_out = dp_index // 4
        layer_grad = lax.dynamic_index_in_dim(blocks, place_out, 0, keepdims=False).astype(
            jnp.float32
        )
        for k in range(1, 4):
            away = lax.dynamic_index_in_dim(blocks, place_out ^ k, 0, keepdims=False)
            layer_grad = layer_grad + lax.ppermute(
                away, "dp", [(i, i ^ (4 * k)) for i in range(dp_count)]
            ).astype(jnp.float32)
    else:
        layer_grad = lax.psum_scatter(
            layer_part, "dp", scatter_dimension=0, tiled=True
        ).astype(jnp.float32)
    qkv_grad = (
        layer_grad[:, : 3 * head_cols]
        .reshape(shard_rows, pairs, 3, LANES)
        .transpose(2, 0, 1, 3)
        .reshape(3, shard_rows, head_cols)
    )
    out_grad = layer_grad[:, 3 * head_cols :]
    gain_one_grad = jnp.sum(norm_one_part * (inputs_all * scale_all), axis=0)
    norm_one_grad = own_part(norm_one_part, 0) + swap(
        other_part(norm_one_part, 0).astype(jnp.bfloat16)
    ).astype(jnp.float32)
    scale = lax.rsqrt(jnp.mean(inputs * inputs, axis=-1, keepdims=True) + EPSILON)
    unit = inputs * scale
    inner = norm_one_grad * gain_one
    input_grad = mid_grad + scale * (
        inner - unit * jnp.mean(inner * unit, axis=-1, keepdims=True)
    )

    gain_size = 2 * width
    gain_part = jnp.concatenate([gain_one_grad, gain_two_grad]).reshape(-1, LANES)
    small = jnp.concatenate(
        [gain_part + swap(gain_part), bias_grad.reshape(-1, LANES)], axis=0
    )
    step = 1
    while step < dp_count:
        last = min(4, dp_count // step) if step >= 4 else 2
        small = small + sum(
            lax.ppermute(small, "dp", [(i, i ^ (k * step)) for i in range(dp_count)])
            for k in range(1, last)
        )
        step *= last
    gain_sums = small.reshape(-1)[:gain_size].reshape(2, width)
    bias_out = small.reshape(-1)[gain_size:].reshape(head_count, bucket_count)
    gains_grad = lax.dynamic_slice_in_dim(gain_sums, dp_index * shard_rows, shard_rows, 1)
    return (
        mixed,
        input_grad,
        qkv_grad,
        out_grad,
        gains_grad,
        bias_out,
        regroup(gate_up_back[:, :, :hidden_cols]),
        regroup(gate_up_back[:, :, hidden_cols:]),
        regroup(down_back),
    )


def solution(mesh):
    rows = P(("dp", "tensor"), None)
    shard = P("dp", "tensor")
    stacked = P(None, "dp", "tensor")
    return jax.shard_map(
        on_device,
        mesh=mesh,
        in_specs=(
            rows,
            rows,
            P(),
            P(),
            P("dp", None),
            P("dp", None),
            stacked,
            shard,
            P(None, "dp"),
            P("tensor", None),
            stacked,
            stacked,
            stacked,
        ),
        out_specs=(
            rows,
            rows,
            stacked,
            shard,
            P(None, "dp"),
            P("tensor", None),
            stacked,
            stacked,
            stacked,
        ),
        check_vma=False,
    )
```

```python
import jax
import jax.numpy as jnp
from jax import lax
from jax.experimental import pallas as pl
from jax.experimental.pallas import tpu as pltpu
from jax.sharding import PartitionSpec as P

HEAD_DIM = 64
EPSILON = 1e-06
MASKED_SCORE = -1e30
HIGHEST = lax.Precision.HIGHEST
SCORE_SCALE = 0.125
QUERY_COLS = 256
LANES = 128
GELU_SCALE = 0.7978845608028654
GELU_CUBIC = 0.044715
GAIN_ROWS = 16


def dot_nt(left, right):
    return lax.dot_general(
        left, right, (((1,), (1,)), ((), ())), preferred_element_type=jnp.float32
    )


def dot_nn(left, right):
    return lax.dot_general(
        left, right, (((1,), (0,)), ((), ())), preferred_element_type=jnp.float32
    )


def dot_tn(left, right):
    return lax.dot_general(
        left, right, (((0,), (0,)), ((), ())), preferred_element_type=jnp.float32
    )


def bias_base(bias_row, seq):
    return pltpu.roll(
        jnp.broadcast_to(bias_row, (LANES, 2 * seq)),
        2 * seq - (LANES - 1),
        1,
        stride=1,
        stride_axis=0,
    )


def masked_scores(keys, query_block, base_ref, start, seq, cols, length):
    scores = dot_nt(keys, query_block) * SCORE_SCALE
    blocks = []
    for first in range(0, seq, LANES):
        offset = seq - LANES - first + start
        block = scores[first : first + LANES] + base_ref[:, offset : offset + cols]
        key_index = lax.broadcasted_iota(jnp.int32, block.shape, 0) + first
        blocks.append(jnp.where(key_index < length, block, MASKED_SCORE))
    return jnp.concatenate(blocks, axis=0)


def head_part(ref, start, cols, head):
    lane = lax.broadcasted_iota(jnp.int32, (cols, LANES), 1)
    return jnp.where(
        lane // HEAD_DIM == head, ref[start : start + cols, :], jnp.zeros((), jnp.bfloat16)
    )


def forward_kernel(length_ref, joined_ref, bias_ref, out_ref, total_ref, base_ref):
    query_ref, key_ref, value_ref = [
        joined_ref.at[:, i * LANES : (i + 1) * LANES] for i in range(3)
    ]
    seq = joined_ref.shape[0]
    cols = min(QUERY_COLS, seq)
    length = length_ref[0]
    values_t = value_ref[...].T
    keys = key_ref[...]
    starts = range(0, seq, cols)
    outs = {}
    for head in range(LANES // HEAD_DIM):
        base_ref[...] = bias_base(bias_ref[0, head : head + 1, :], seq)
        for start in starts:
            query_block = head_part(query_ref, start, cols, head)
            scores = masked_scores(keys, query_block, base_ref, start, seq, cols, length)
            top = jnp.max(scores, axis=0, keepdims=True)
            exponent = jnp.exp(scores - top)
            total = jnp.sum(exponent, axis=0, keepdims=True)
            probs = (exponent * (1.0 / total)).astype(jnp.bfloat16)
            total_ref[0, head : head + 1, start : start + cols] = top + jnp.log(total)
            outs[start, head] = dot_nn(
                values_t[head * HEAD_DIM : (head + 1) * HEAD_DIM], probs
            )
    for start in starts:
        joined = jnp.concatenate(
            [outs[start, head] for head in range(LANES // HEAD_DIM)], axis=0
        )
        out_ref[start : start + cols, :] = joined.T.astype(jnp.bfloat16)


def attend_forward(length, joined, bias_rows):
    seq = joined.shape[0]
    width = joined.shape[1] // 3
    pairs = width // LANES
    heads = LANES // HEAD_DIM
    column = pl.BlockSpec((seq, LANES), lambda i: (0, i))
    return pl.pallas_call(
        forward_kernel,
        grid=(pairs,),
        in_specs=[
            pl.BlockSpec(memory_space=pltpu.SMEM),
            pl.BlockSpec((seq, 3 * LANES), lambda i: (0, i)),
            pl.BlockSpec((1, heads, 2 * seq), lambda i: (i, 0, 0)),
        ],
        out_specs=[column, pl.BlockSpec((1, heads, seq), lambda i: (i, 0, 0))],
        out_shape=[
            jax.ShapeDtypeStruct((seq, width), jnp.bfloat16),
            jax.ShapeDtypeStruct((pairs, heads, seq), jnp.float32),
        ],
        scratch_shapes=[pltpu.VMEM((LANES, 2 * seq), jnp.float32)],
        cost_estimate=pl.CostEstimate(
            flops=16 * seq * seq * width,
            transcendentals=seq * seq * width // HEAD_DIM,
            bytes_accessed=8 * seq * width,
        ),
        name="attend_forward",
    )(length, joined, bias_rows)


def diagonal_sums(acc_ref, seq):
    period = 2 * seq
    folded = acc_ref[0:8, :]
    for first in range(8, LANES, 8):
        folded = folded + pltpu.roll(acc_ref[first : first + 8, :], period - first, 1)
    row = lax.broadcasted_iota(jnp.int32, folded.shape, 0)
    for bit in (1, 2, 4):
        folded = jnp.where((row & bit) != 0, pltpu.roll(folded, period - bit, 1), folded)
    return pltpu.roll(jnp.sum(folded, axis=0, keepdims=True), LANES - 1, 1)


def backward_kernel(
    length_ref,
    joined_ref,
    grad_ref,
    total_ref,
    bias_ref,
    joined_grad_ref,
    bias_grad_ref,
    base_ref,
    acc_ref,
):
    query_ref, key_ref, value_ref = [
        joined_ref.at[:, i * LANES : (i + 1) * LANES] for i in range(3)
    ]
    seq = joined_ref.shape[0]
    cols = min(QUERY_COLS, seq)
    length = length_ref[0]
    keys = key_ref[...]
    values = value_ref[...]
    keys_t = keys.T
    starts = range(0, seq, cols)
    key_acc = jnp.zeros((seq, LANES), jnp.float32)
    value_acc = jnp.zeros((seq, LANES), jnp.float32)
    query_parts = {}
    for head in range(LANES // HEAD_DIM):
        base_ref[...] = bias_base(bias_ref[0, head : head + 1, :], seq)
        acc_ref[...] = jnp.zeros_like(acc_ref)
        for start in starts:
            query_block = head_part(query_ref, start, cols, head)
            grad_block = head_part(grad_ref, start, cols, head)
            scores = masked_scores(keys, query_block, base_ref, start, seq, cols, length)
            probs = jnp.exp(scores - total_ref[0, head : head + 1, start : start + cols])
            probs_grad = dot_nt(values, grad_block)
            mean_grad = jnp.sum(probs * probs_grad, axis=0, keepdims=True)
            score_grad = (probs * (probs_grad - mean_grad)).astype(jnp.bfloat16)
            value_acc = value_acc + dot_nn(probs.astype(jnp.bfloat16), grad_block)
            key_acc = key_acc + dot_nn(score_grad, query_block)
            query_parts[start, head] = dot_nn(
                keys_t[head * HEAD_DIM : (head + 1) * HEAD_DIM], score_grad
            )
            for first in range(0, seq, LANES):
                offset = seq - LANES - first + start
                acc_ref[:, offset : offset + cols] += score_grad[
                    first : first + LANES
                ].astype(jnp.float32)
        bias_grad_ref[0, head : head + 1, :] = diagonal_sums(acc_ref, seq)
    joined_grad_ref[:, LANES : 2 * LANES] = (key_acc * SCORE_SCALE).astype(jnp.bfloat16)
    joined_grad_ref[:, 2 * LANES :] = value_acc.astype(jnp.bfloat16)
    for start in starts:
        joined = jnp.concatenate(
            [query_parts[start, head] for head in range(LANES // HEAD_DIM)], axis=0
        )
        joined_grad_ref[start : start + cols, :LANES] = (joined * SCORE_SCALE).T.astype(
            jnp.bfloat16
        )


def attend_backward(length, joined, attended_grad, totals, bias_rows):
    seq, width = attended_grad.shape
    pairs = width // LANES
    heads = LANES // HEAD_DIM
    column = pl.BlockSpec((seq, LANES), lambda i: (0, i))
    triple = pl.BlockSpec((seq, 3 * LANES), lambda i: (0, i))
    vector = pl.BlockSpec((1, heads, 2 * seq), lambda i: (i, 0, 0))
    return pl.pallas_call(
        backward_kernel,
        grid=(pairs,),
        in_specs=[
            pl.BlockSpec(memory_space=pltpu.SMEM),
            triple,
            column,
            pl.BlockSpec((1, heads, seq), lambda i: (i, 0, 0)),
            vector,
        ],
        out_specs=[triple, vector],
        out_shape=[
            jax.ShapeDtypeStruct((seq, 3 * width), jnp.bfloat16),
            jax.ShapeDtypeStruct((pairs, heads, 2 * seq), jnp.float32),
        ],
        scratch_shapes=[
            pltpu.VMEM((LANES, 2 * seq), jnp.float32),
            pltpu.VMEM((LANES, 2 * seq), jnp.float32),
        ],
        cost_estimate=pl.CostEstimate(
            flops=40 * seq * seq * width,
            transcendentals=seq * seq * width // HEAD_DIM,
            bytes_accessed=14 * seq * width,
        ),
        name="attend_backward",
    )(length, joined, attended_grad, totals, bias_rows)


def assemble_kernel(place_ref, *refs):
    parts, (weight_ref, out_ref, gain_ref) = refs[:-3], refs[-3:]
    rows = weight_ref.shape[0]
    pairs = weight_ref.shape[1] // (3 * LANES)
    wanted = pl.program_id(1) ^ place_ref[1]
    for index, part_ref in enumerate(parts):

        @pl.when(wanted == index)
        def _(part_ref=part_ref):
            for kind in range(3):
                for pair in range(pairs):
                    first = (3 * pair + kind) * LANES
                    weight_ref[:, first : first + LANES] = part_ref[
                        0, kind * rows : (kind + 1) * rows, pair * LANES : (pair + 1) * LANES
                    ]
            out_ref[...] = part_ref[0, 3 * rows : 4 * rows, :]
            gain_ref[0] = part_ref[0, 4 * rows :, :]


def assemble(place, parts):
    outer, block_rows, cols = parts[0].shape
    inner = len(parts)
    rows = (block_rows - GAIN_ROWS) // 4
    block = pl.BlockSpec(
        (1, block_rows, cols), lambda i, j, place_ref: (i ^ place_ref[0], 0, 0)
    )
    return pl.pallas_call(
        assemble_kernel,
        grid_spec=pltpu.PrefetchScalarGridSpec(
            num_scalar_prefetch=1,
            grid=(outer, inner),
            in_specs=[block] * inner,
            out_specs=[
                pl.BlockSpec((rows, 3 * cols), lambda i, j, place_ref: (i * inner + j, 0)),
                pl.BlockSpec((rows, cols), lambda i, j, place_ref: (i * inner + j, 0)),
                pl.BlockSpec(
                    (1, GAIN_ROWS, cols), lambda i, j, place_ref: (i * inner + j, 0, 0)
                ),
            ],
        ),
        out_shape=[
            jax.ShapeDtypeStruct((outer * inner * rows, 3 * cols), jnp.bfloat16),
            jax.ShapeDtypeStruct((outer * inner * rows, cols), jnp.bfloat16),
            jax.ShapeDtypeStruct((outer * inner, GAIN_ROWS, cols), jnp.bfloat16),
        ],
        name="assemble",
    )(place, *parts)


def gelu_parts(gate_pre):
    inner = jnp.tanh(GELU_SCALE * (gate_pre + GELU_CUBIC * gate_pre * gate_pre * gate_pre))
    gelu = 0.5 * gate_pre * (1.0 + inner)
    slope = 0.5 * (1.0 + inner) + 0.5 * gate_pre * (1.0 - inner * inner) * GELU_SCALE * (
        1.0 + 3.0 * GELU_CUBIC * gate_pre * gate_pre
    )
    return gelu, slope


def on_device(
    tokens,
    cotangent,
    lengths,
    bucket_table,
    routes,
    gate_values,
    qkv_weight,
    out_weight,
    norm_gains,
    rel_bias,
    gate_weight,
    up_weight,
    down_weight,
):
    tok_rows, width = tokens.shape
    half = width // 2
    dp_count = lax.axis_size("dp")
    tensor_count = lax.axis_size("tensor")
    seq = tok_rows * tensor_count
    expert_count, shard_rows, hidden_cols = gate_weight.shape
    head_cols = qkv_weight.shape[2]
    head_count, bucket_count = rel_bias.shape
    capacity = 9 * seq // 64
    group_size = dp_count // expert_count
    slot_count = (capacity + group_size - 1) // group_size
    total_slots = dp_count * slot_count
    dp_index = lax.axis_index("dp")
    tensor_index = lax.axis_index("tensor")
    first_tensor = tensor_index == 0
    length = lengths[dp_index]
    length_row = length[None]
    group_valid = jnp.arange(seq, dtype=jnp.int32) < length
    own_valid = lax.dynamic_slice_in_dim(group_valid, tensor_index * tok_rows, tok_rows, 0)
    own_valid = own_valid.astype(jnp.float32)[:, None]

    def swap(block):
        return lax.ppermute(block, "tensor", [(0, 1), (1, 0)])

    def chain(block, earlier):
        return lax.optimization_barrier((block, earlier))

    def ordered(own, other, axis):
        return jnp.where(
            first_tensor,
            jnp.concatenate([own, other], axis=axis),
            jnp.concatenate([other, own], axis=axis),
        )

    def own_part(block, axis):
        size = block.shape[axis] // 2
        return lax.dynamic_slice_in_dim(block, tensor_index * size, size, axis)

    def other_part(block, axis):
        size = block.shape[axis] // 2
        return lax.dynamic_slice_in_dim(block, (1 - tensor_index) * size, size, axis)

    def exchange(block):
        return lax.all_to_all(block, "dp", split_axis=0, concat_axis=0, tiled=True)

    def home_order(weight):
        return jnp.repeat(weight, group_size, axis=0)

    def fetch(weight):
        return exchange(home_order(weight)).reshape(dp_count * shard_rows, weight.shape[2])

    def send_grad(grad):
        return exchange(grad.reshape(dp_count, shard_rows, grad.shape[1]))

    def route(rows):
        arrived = exchange(rows.reshape(dp_count, slot_count, rows.shape[1]))
        return arrived.reshape(total_slots, rows.shape[1])

    spare = slot_count - shard_rows
    fold = shard_rows // spare

    def pack(rows):
        blocks = rows.reshape(dp_count, slot_count, half)
        tail = blocks[:, shard_rows:].reshape(dp_count, spare, fold, half // fold)
        tail = tail.transpose(0, 2, 1, 3).reshape(dp_count, shard_rows, half // fold)
        return jnp.concatenate([blocks[:, :shard_rows], tail], axis=2)

    def unpack(packed):
        tail = packed[:, :, half:].reshape(dp_count, fold, spare, half // fold)
        tail = tail.transpose(0, 2, 1, 3).reshape(dp_count, spare, half)
        return jnp.concatenate([packed[:, :, :half], tail], axis=1).reshape(total_slots, half)

    def regroup(arrived):
        return jnp.sum(
            arrived.astype(jnp.float32).reshape(
                expert_count, group_size, shard_rows, arrived.shape[2]
            ),
            axis=1,
        )

    gain_pad = jnp.pad(norm_gains, ((0, GAIN_ROWS - 2), (0, head_cols - shard_rows)))
    layer_shard = jnp.concatenate(
        [qkv_weight.reshape(3 * shard_rows, head_cols), out_weight, gain_pad], axis=0
    )
    pairs = head_cols // LANES
    pair_expert = routes.reshape(-1)
    pair_valid = jnp.repeat(group_valid, 2)
    chosen = (
        pair_expert[:, None] == jnp.arange(expert_count, dtype=jnp.int32)[None, :]
    ) & pair_valid[:, None]
    pair_index = jnp.arange(2 * seq, dtype=jnp.int32)
    before = (pair_index[:, None] > pair_index[None, :]).astype(jnp.bfloat16)
    earlier_pairs = dot_nn(before, chosen.astype(jnp.bfloat16))
    position = jnp.sum(jnp.where(chosen, earlier_pairs, 0.0), axis=1).astype(jnp.int32)
    kept_pair = pair_valid & (position < capacity)
    device = pair_expert * group_size + position // slot_count
    pair_slot = jnp.where(
        kept_pair, device * slot_count + position % slot_count, total_slots
    ).reshape(seq, 2)
    slot_index = jnp.arange(total_slots, dtype=jnp.int32)
    first_hit = pair_slot[:, 0][None, :] == slot_index[:, None]
    second_hit = pair_slot[:, 1][None, :] == slot_index[:, None]
    no_gate = jnp.zeros((), jnp.bfloat16)
    pick = (first_hit | second_hit).astype(jnp.bfloat16)
    pick_gate = jnp.where(
        first_hit,
        gate_values[:, 0][None, :],
        jnp.where(second_hit, gate_values[:, 1][None, :], no_gate),
    )

    tokens_other = swap(tokens)
    mix_grad = lax.optimization_barrier(
        (own_valid * cotangent.astype(jnp.float32)).astype(jnp.bfloat16)
    )
    mix_other = swap(other_part(mix_grad, 1))
    out_grad_cols = dot_nn(
        pick_gate, ordered(own_part(mix_grad, 1), mix_other, 0)
    ).astype(jnp.bfloat16)
    residual, out_grad_cols = chain(tokens, out_grad_cols)
    gate_up = jnp.concatenate(
        [home_order(gate_weight), home_order(up_weight), pack(out_grad_cols)], axis=2
    )
    if dp_count == 16:
        across = [
            lax.ppermute(layer_shard, "dp", [(i, i ^ (4 * k)) for i in range(16)])
            for k in range(1, 4)
        ]
        gate_up, across = chain(gate_up, across)
        near = jnp.stack([layer_shard, *across])
        side = lax.ppermute(near, "dp", [(i, i ^ 2) for i in range(16)])
        core = [(i, i ^ 1) for i in range(16)]
        parts = [near, lax.ppermute(near, "dp", core), side, lax.ppermute(side, "dp", core)]
        place = jnp.stack([dp_index // 4, dp_index % 4])
        projection, out_all, gain_rows = assemble(place, parts)
    else:
        layer_all = lax.all_gather(layer_shard, "dp", axis=0, tiled=False)
        gate_up, layer_all = chain(gate_up, layer_all)
        projection = (
            layer_all[:, : 3 * shard_rows]
            .reshape(dp_count, 3, shard_rows, pairs, LANES)
            .transpose(0, 2, 3, 1, 4)
            .reshape(width, 3 * head_cols)
        )
        out_all = layer_all[:, 3 * shard_rows : 4 * shard_rows].reshape(width, head_cols)
        gain_rows = layer_all[:, 4 * shard_rows :]
    arrived = exchange(gate_up)
    gate_up_all = arrived.reshape(width, arrived.shape[2])
    slot_grad_half = unpack(arrived[:, :, 2 * hidden_cols :])

    distance = jnp.arange(2 * seq, dtype=jnp.int32)
    table_reversed = jnp.concatenate(
        [bucket_table[::-1], jnp.full((1,), bucket_count, jnp.int32)]
    )
    hot = (
        jnp.arange(bucket_count, dtype=jnp.int32)[:, None] == table_reversed[None, :]
    ).astype(jnp.float32)
    bias_rows = jnp.dot(rel_bias.astype(jnp.float32), hot, precision=HIGHEST).reshape(
        head_count // 2, 2, 2 * seq
    )
    gains_all = jnp.transpose(gain_rows[:, :2, :shard_rows], (1, 0, 2)).reshape(2, width)
    gain_one = gains_all[0].astype(jnp.float32)
    gain_two = gains_all[1].astype(jnp.float32)
    inputs_all = ordered(tokens, tokens_other, 0).astype(jnp.float32)
    scale_all = lax.rsqrt(jnp.mean(inputs_all * inputs_all, axis=-1, keepdims=True) + EPSILON)
    norm_one_all = (inputs_all * scale_all * gain_one).astype(jnp.bfloat16)
    joined = dot_nn(norm_one_all, projection).astype(jnp.bfloat16)
    attended, totals = attend_forward(length_row, joined, bias_rows)
    branch = dot_nt(attended, out_all)
    branch_other = swap(other_part(branch, 0).astype(jnp.bfloat16))
    inputs = residual.astype(jnp.float32)
    mid = inputs + own_valid * (own_part(branch, 0) + branch_other.astype(jnp.float32))
    mid_scale = lax.rsqrt(jnp.mean(mid * mid, axis=-1, keepdims=True) + EPSILON)
    norm_two = (mid * mid_scale * gain_two).astype(jnp.bfloat16)
    norm_two_cols = ordered(own_part(norm_two, 1), swap(other_part(norm_two, 1)), 0)
    expert_rows, slot_grad_half = chain(
        dot_nn(pick, norm_two_cols).astype(jnp.bfloat16), slot_grad_half
    )
    slot_grad_other = swap(slot_grad_half)
    down_late, (expert_half, slot_grad_other) = chain(
        down_weight, (route(expert_rows), slot_grad_other)
    )
    down_all = fetch(down_late)
    expert_in = ordered(expert_half, swap(expert_half), 1)
    slot_grad = ordered(slot_grad_half, slot_grad_other, 1)

    pre = dot_nn(expert_in, gate_up_all)
    gate_pre = pre[:, :hidden_cols]
    up_pre = pre[:, hidden_cols : 2 * hidden_cols]
    gelu, slope = gelu_parts(gate_pre)
    hidden = lax.optimization_barrier((gelu * up_pre).astype(jnp.bfloat16))
    down_grad, down_all = chain(dot_tn(slot_grad, hidden).astype(jnp.bfloat16), down_all)
    down_back = send_grad(down_grad)
    hidden_grad = dot_nn(slot_grad, down_all)
    pre_grad = jnp.concatenate(
        [
            (hidden_grad * up_pre * slope).astype(jnp.bfloat16),
            (hidden_grad * gelu).astype(jnp.bfloat16),
            jnp.zeros((total_slots, half + half // fold), jnp.bfloat16),
        ],
        axis=1,
    )
    slot_back_part = dot_nt(pre_grad, gate_up_all)
    slot_back_away = other_part(slot_back_part, 1).astype(jnp.bfloat16)
    hidden_late, slot_back_away = chain(hidden, slot_back_away)
    slot_back_other = swap(slot_back_away)
    expert_out_part = dot_nt(hidden_late, down_all)
    expert_out_away, slot_back_other = chain(
        other_part(expert_out_part, 1).astype(jnp.bfloat16), slot_back_other
    )
    slot_back_half = (
        own_part(slot_back_part, 1) + slot_back_other.astype(jnp.float32)
    ).astype(jnp.bfloat16)
    expert_out_half = (
        own_part(expert_out_part, 1) + swap(expert_out_away).astype(jnp.float32)
    ).astype(jnp.bfloat16)
    slot_back_half, down_back = chain(slot_back_half, down_back)
    last, slot_back = chain(
        lax.dynamic_update_slice(
            dot_tn(expert_in, pre_grad)
            .astype(jnp.bfloat16)
            .reshape(dp_count, shard_rows, pre_grad.shape[1]),
            pack(expert_out_half),
            (0, 0, 2 * hidden_cols),
        ),
        route(slot_back_half),
    )
    arrived_back = exchange(last)

    back_cols = dot_tn(pick, slot_back)
    norm_two_grad = ordered(
        own_part(back_cols, 0), swap(other_part(back_cols, 0).astype(jnp.bfloat16)).astype(jnp.float32), 1
    )
    mid_unit = mid * mid_scale
    mid_inner = norm_two_grad * gain_two
    mid_grad = own_valid * cotangent.astype(jnp.float32) + mid_scale * (
        mid_inner - mid_unit * jnp.mean(mid_inner * mid_unit, axis=-1, keepdims=True)
    )
    gain_two_grad = jnp.sum(norm_two_grad * mid_unit, axis=0)
    branch_grad = (own_valid * mid_grad).astype(jnp.bfloat16)
    branch_grad_all = ordered(branch_grad, swap(branch_grad), 0)

    attended_grad = dot_nn(branch_grad_all, out_all).astype(jnp.bfloat16)
    joined_grad, bias_sums = attend_backward(
        length_row, joined, attended_grad, totals, bias_rows
    )
    bias_grad = jnp.dot(
        bias_sums.reshape(head_count, 2 * seq), hot.T, precision=HIGHEST
    )
    norm_one_part = dot_nt(joined_grad, projection)
    layer_part = jnp.concatenate(
        [
            dot_tn(norm_one_all, joined_grad).astype(jnp.bfloat16),
            dot_tn(branch_grad_all, attended).astype(jnp.bfloat16),
        ],
        axis=1,
    )
    gain_one_grad = jnp.sum(norm_one_part * (inputs_all * scale_all), axis=0)
    norm_one_grad = own_part(norm_one_part, 0) + swap(
        other_part(norm_one_part, 0).astype(jnp.bfloat16)
    ).astype(jnp.float32)
    scale = lax.rsqrt(jnp.mean(inputs * inputs, axis=-1, keepdims=True) + EPSILON)
    unit = inputs * scale
    inner = norm_one_grad * gain_one
    input_grad = mid_grad + scale * (
        inner - unit * jnp.mean(inner * unit, axis=-1, keepdims=True)
    )
    gain_part = jnp.concatenate([gain_one_grad, gain_two_grad]).reshape(-1, LANES)
    small = jnp.concatenate(
        [gain_part + swap(gain_part), bias_grad.reshape(-1, LANES)], axis=0
    )

    def partner(block, offset):
        return lax.ppermute(block, "dp", [(i, i ^ offset) for i in range(dp_count)])

    row_size = layer_part.shape[1]
    small = jnp.pad(small.reshape(-1), (0, -small.size % row_size)).reshape(-1, row_size)
    small_rows = small.shape[0]

    def with_small(block):
        high = lax.reduce_precision(small, 8, 7)
        rows = jnp.concatenate([high, small - high], axis=0).astype(jnp.bfloat16)
        rows = jnp.pad(rows, ((0, -rows.shape[0] % 8), (0, 0)))
        return jnp.concatenate([block, rows], axis=0)

    def small_of(block, first):
        rows = block[first : first + 2 * small_rows].astype(jnp.float32)
        return rows[:small_rows] + rows[small_rows:]

    if dp_count == 16:
        blocks = layer_part.reshape(dp_count, shard_rows, row_size)
        for step in (1, 2):
            pieces = blocks.reshape(-1, 2, shard_rows, row_size)
            bit = (dp_index // step) % 2
            away = lax.dynamic_index_in_dim(pieces, 1 - bit, 1, keepdims=False)
            stay = lax.dynamic_index_in_dim(pieces, bit, 1, keepdims=False)
            if step == 1:
                came = partner(away, step)
                small = small + partner(small, step)
            else:
                came = partner(with_small(away.reshape(-1, row_size)), step)
                came = chain(came, input_grad)[0]
                small = small + small_of(came, away.shape[0] * shard_rows)
                came = came[: away.shape[0] * shard_rows].reshape(away.shape)
            blocks = (stay.astype(jnp.float32) + came.astype(jnp.float32)).astype(jnp.bfloat16)
        outer = dp_index // 4
        leaving = [
            with_small(lax.dynamic_index_in_dim(blocks, outer ^ k, 0, keepdims=False))
            for k in range(1, 4)
        ]
        stay = lax.dynamic_index_in_dim(blocks, outer, 0, keepdims=False)
        arrived_back = chain(arrived_back, leaving)[0]
        came = [partner(piece, 4 * k) for k, piece in zip(range(1, 4), leaving, strict=True)]
    else:
        step = 1
        while step < dp_count:
            small = small + partner(small, step)
            step *= 2
    returned = unpack(arrived_back[:, :, 2 * hidden_cols :])
    mix_cols = dot_tn(pick_gate, returned)
    mix_away = other_part(mix_cols, 0).astype(jnp.bfloat16)
    arrived_back = chain(arrived_back, mix_away)[0]
    gate_grad = regroup(arrived_back[:, :, :hidden_cols])
    up_grad = regroup(arrived_back[:, :, hidden_cols : 2 * hidden_cols])
    mix_own = ordered(own_part(mix_cols, 0), swap(mix_away).astype(jnp.float32), 1)
    mixed = (mid + own_valid * mix_own).astype(jnp.bfloat16)
    if dp_count == 16:
        came = chain(came, (gate_grad, up_grad, mixed))[0]
        small = small + sum(small_of(piece, shard_rows) for piece in came)
        layer_grad = stay.astype(jnp.float32) + sum(
            piece[:shard_rows].astype(jnp.float32) for piece in came
        )
    else:
        layer_grad = lax.psum_scatter(
            layer_part, "dp", scatter_dimension=0, tiled=True
        ).astype(jnp.float32)
    qkv_grad = (
        layer_grad[:, : 3 * head_cols]
        .reshape(shard_rows, pairs, 3, LANES)
        .transpose(2, 0, 1, 3)
        .reshape(3, shard_rows, head_cols)
    )
    out_grad = layer_grad[:, 3 * head_cols :]
    gain_size = 2 * width
    gain_sums = small.reshape(-1)[:gain_size].reshape(2, width)
    bias_out = small.reshape(-1)[gain_size : gain_size + head_count * bucket_count].reshape(
        head_count, bucket_count
    )
    gains_grad = lax.dynamic_slice_in_dim(gain_sums, dp_index * shard_rows, shard_rows, 1)
    return (
        mixed,
        input_grad,
        qkv_grad,
        out_grad,
        gains_grad,
        bias_out,
        gate_grad,
        up_grad,
        regroup(down_back),
    )


def solution(mesh):
    rows = P(("dp", "tensor"), None)
    shard = P("dp", "tensor")
    stacked = P(None, "dp", "tensor")
    return jax.shard_map(
        on_device,
        mesh=mesh,
        in_specs=(
            rows,
            rows,
            P(),
            P(),
            P("dp", None),
            P("dp", None),
            stacked,
            shard,
            P(None, "dp"),
            P("tensor", None),
            stacked,
            stacked,
            stacked,
        ),
        out_specs=(
            rows,
            rows,
            stacked,
            shard,
            P(None, "dp"),
            P("tensor", None),
            stacked,
            stacked,
            stacked,
        ),
        check_vma=False,
    )
```

```python
import jax
import jax.numpy as jnp
from jax import lax
from jax.experimental import pallas as pl
from jax.experimental.pallas import tpu as pltpu
from jax.sharding import PartitionSpec as P

HEAD_DIM = 64
EPSILON = 1e-06
MASKED_SCORE = -1e30
HIGHEST = lax.Precision.HIGHEST
SCORE_SCALE = 0.125
QUERY_COLS = 256
LANES = 128
GELU_SCALE = 0.7978845608028654
GELU_CUBIC = 0.044715
GAIN_ROWS = 16
VMEM_BYTES = 48 * 2**20


def dot_nt(left, right):
    return lax.dot_general(
        left, right, (((1,), (1,)), ((), ())), preferred_element_type=jnp.float32
    )


def dot_nn(left, right):
    return lax.dot_general(
        left, right, (((1,), (0,)), ((), ())), preferred_element_type=jnp.float32
    )


def dot_tn(left, right):
    return lax.dot_general(
        left, right, (((0,), (0,)), ((), ())), preferred_element_type=jnp.float32
    )


def bias_base(bias_row, seq):
    return pltpu.roll(
        jnp.broadcast_to(bias_row, (LANES, 2 * seq)),
        2 * seq - (LANES - 1),
        1,
        stride=1,
        stride_axis=0,
    )


def masked_scores(keys, query_block, base_ref, start, seq, cols, length):
    scores = dot_nt(keys, query_block) * SCORE_SCALE
    blocks = []
    for first in range(0, seq, LANES):
        offset = seq - LANES - first + start
        block = scores[first : first + LANES] + base_ref[:, offset : offset + cols]
        key_index = lax.broadcasted_iota(jnp.int32, block.shape, 0) + first
        blocks.append(jnp.where(key_index < length, block, MASKED_SCORE))
    return jnp.concatenate(blocks, axis=0)


def head_part(ref, start, cols, head):
    lane = lax.broadcasted_iota(jnp.int32, (cols, LANES), 1)
    return jnp.where(
        lane // HEAD_DIM == head, ref[start : start + cols, :], jnp.zeros((), jnp.bfloat16)
    )


def forward_kernel(length_ref, joined_ref, bias_ref, out_ref, total_ref, base_ref):
    query_ref, key_ref, value_ref = [
        joined_ref.at[:, i * LANES : (i + 1) * LANES] for i in range(3)
    ]
    seq = joined_ref.shape[0]
    cols = min(QUERY_COLS, seq)
    length = length_ref[0]
    values_t = value_ref[...].T
    keys = key_ref[...]
    starts = range(0, seq, cols)
    outs = {}
    for head in range(LANES // HEAD_DIM):
        base_ref[...] = bias_base(bias_ref[0, head : head + 1, :], seq)
        for start in starts:
            query_block = head_part(query_ref, start, cols, head)
            scores = masked_scores(keys, query_block, base_ref, start, seq, cols, length)
            top = jnp.max(scores, axis=0, keepdims=True)
            exponent = jnp.exp(scores - top)
            total = jnp.sum(exponent, axis=0, keepdims=True)
            probs = (exponent * (1.0 / total)).astype(jnp.bfloat16)
            total_ref[0, head : head + 1, start : start + cols] = top + jnp.log(total)
            outs[start, head] = dot_nn(
                values_t[head * HEAD_DIM : (head + 1) * HEAD_DIM], probs
            )
    for start in starts:
        joined = jnp.concatenate(
            [outs[start, head] for head in range(LANES // HEAD_DIM)], axis=0
        )
        out_ref[start : start + cols, :] = joined.T.astype(jnp.bfloat16)


def attend_forward(length, joined, bias_rows):
    seq = joined.shape[0]
    width = joined.shape[1] // 3
    pairs = width // LANES
    heads = LANES // HEAD_DIM
    column = pl.BlockSpec((seq, LANES), lambda i: (0, i))
    return pl.pallas_call(
        forward_kernel,
        grid=(pairs,),
        in_specs=[
            pl.BlockSpec(memory_space=pltpu.SMEM),
            pl.BlockSpec((seq, 3 * LANES), lambda i: (0, i)),
            pl.BlockSpec((1, heads, 2 * seq), lambda i: (i, 0, 0)),
        ],
        out_specs=[column, pl.BlockSpec((1, heads, seq), lambda i: (i, 0, 0))],
        out_shape=[
            jax.ShapeDtypeStruct((seq, width), jnp.bfloat16),
            jax.ShapeDtypeStruct((pairs, heads, seq), jnp.float32),
        ],
        scratch_shapes=[pltpu.VMEM((LANES, 2 * seq), jnp.float32)],
        cost_estimate=pl.CostEstimate(
            flops=16 * seq * seq * width,
            transcendentals=seq * seq * width // HEAD_DIM,
            bytes_accessed=8 * seq * width,
        ),
        name="attend_forward",
    )(length, joined, bias_rows)


def diagonal_sums(acc_ref, seq):
    period = 2 * seq
    folded = acc_ref[0:8, :]
    for first in range(8, LANES, 8):
        folded = folded + pltpu.roll(acc_ref[first : first + 8, :], period - first, 1)
    row = lax.broadcasted_iota(jnp.int32, folded.shape, 0)
    for bit in (1, 2, 4):
        folded = jnp.where((row & bit) != 0, pltpu.roll(folded, period - bit, 1), folded)
    return pltpu.roll(jnp.sum(folded, axis=0, keepdims=True), LANES - 1, 1)


def backward_kernel(
    length_ref,
    joined_ref,
    grad_ref,
    total_ref,
    bias_ref,
    joined_grad_ref,
    bias_grad_ref,
    base_ref,
    acc_ref,
):
    query_ref, key_ref, value_ref = [
        joined_ref.at[:, i * LANES : (i + 1) * LANES] for i in range(3)
    ]
    seq = joined_ref.shape[0]
    cols = min(QUERY_COLS, seq)
    length = length_ref[0]
    keys = key_ref[...]
    values = value_ref[...]
    keys_t = keys.T
    starts = range(0, seq, cols)
    key_acc = jnp.zeros((seq, LANES), jnp.float32)
    value_acc = jnp.zeros((seq, LANES), jnp.float32)
    query_parts = {}
    for head in range(LANES // HEAD_DIM):
        base_ref[...] = bias_base(bias_ref[0, head : head + 1, :], seq)
        acc_ref[...] = jnp.zeros_like(acc_ref)
        for start in starts:
            query_block = head_part(query_ref, start, cols, head)
            grad_block = head_part(grad_ref, start, cols, head)
            scores = masked_scores(keys, query_block, base_ref, start, seq, cols, length)
            probs = jnp.exp(scores - total_ref[0, head : head + 1, start : start + cols])
            probs_grad = dot_nt(values, grad_block)
            mean_grad = jnp.sum(probs * probs_grad, axis=0, keepdims=True)
            score_grad = (probs * (probs_grad - mean_grad)).astype(jnp.bfloat16)
            value_acc = value_acc + dot_nn(probs.astype(jnp.bfloat16), grad_block)
            key_acc = key_acc + dot_nn(score_grad, query_block)
            query_parts[start, head] = dot_nn(
                keys_t[head * HEAD_DIM : (head + 1) * HEAD_DIM], score_grad
            )
            for first in range(0, seq, LANES):
                offset = seq - LANES - first + start
                acc_ref[:, offset : offset + cols] += score_grad[
                    first : first + LANES
                ].astype(jnp.float32)
        bias_grad_ref[0, head : head + 1, :] = diagonal_sums(acc_ref, seq)
    joined_grad_ref[:, LANES : 2 * LANES] = (key_acc * SCORE_SCALE).astype(jnp.bfloat16)
    joined_grad_ref[:, 2 * LANES :] = value_acc.astype(jnp.bfloat16)
    for start in starts:
        joined = jnp.concatenate(
            [query_parts[start, head] for head in range(LANES // HEAD_DIM)], axis=0
        )
        joined_grad_ref[start : start + cols, :LANES] = (joined * SCORE_SCALE).T.astype(
            jnp.bfloat16
        )


def attend_backward(length, joined, attended_grad, totals, bias_rows):
    seq, width = attended_grad.shape
    pairs = width // LANES
    heads = LANES // HEAD_DIM
    column = pl.BlockSpec((seq, LANES), lambda i: (0, i))
    triple = pl.BlockSpec((seq, 3 * LANES), lambda i: (0, i))
    vector = pl.BlockSpec((1, heads, 2 * seq), lambda i: (i, 0, 0))
    return pl.pallas_call(
        backward_kernel,
        grid=(pairs,),
        in_specs=[
            pl.BlockSpec(memory_space=pltpu.SMEM),
            triple,
            column,
            pl.BlockSpec((1, heads, seq), lambda i: (i, 0, 0)),
            vector,
        ],
        out_specs=[triple, vector],
        out_shape=[
            jax.ShapeDtypeStruct((seq, 3 * width), jnp.bfloat16),
            jax.ShapeDtypeStruct((pairs, heads, 2 * seq), jnp.float32),
        ],
        scratch_shapes=[
            pltpu.VMEM((LANES, 2 * seq), jnp.float32),
            pltpu.VMEM((LANES, 2 * seq), jnp.float32),
        ],
        cost_estimate=pl.CostEstimate(
            flops=40 * seq * seq * width,
            transcendentals=seq * seq * width // HEAD_DIM,
            bytes_accessed=14 * seq * width,
        ),
        name="attend_backward",
    )(length, joined, attended_grad, totals, bias_rows)


def assemble_kernel(place_ref, *refs):
    parts, (weight_ref, out_ref, gain_ref) = refs[:-3], refs[-3:]
    rows = weight_ref.shape[0]
    pairs = weight_ref.shape[1] // (3 * LANES)
    wanted = pl.program_id(1) ^ place_ref[1]
    for index, part_ref in enumerate(parts):

        @pl.when(wanted == index)
        def _(part_ref=part_ref):
            for kind in range(3):
                for pair in range(pairs):
                    first = (3 * pair + kind) * LANES
                    weight_ref[:, first : first + LANES] = part_ref[
                        0, kind * rows : (kind + 1) * rows, pair * LANES : (pair + 1) * LANES
                    ]
            out_ref[...] = part_ref[0, 3 * rows : 4 * rows, :]
            gain_ref[0] = part_ref[0, 4 * rows :, :]


def assemble(place, parts):
    outer, block_rows, cols = parts[0].shape
    inner = len(parts)
    rows = (block_rows - GAIN_ROWS) // 4
    block = pl.BlockSpec(
        (1, block_rows, cols), lambda i, j, place_ref: (i ^ place_ref[0], 0, 0)
    )
    return pl.pallas_call(
        assemble_kernel,
        grid_spec=pltpu.PrefetchScalarGridSpec(
            num_scalar_prefetch=1,
            grid=(outer, inner),
            in_specs=[block] * inner,
            out_specs=[
                pl.BlockSpec((rows, 3 * cols), lambda i, j, place_ref: (i * inner + j, 0)),
                pl.BlockSpec((rows, cols), lambda i, j, place_ref: (i * inner + j, 0)),
                pl.BlockSpec(
                    (1, GAIN_ROWS, cols), lambda i, j, place_ref: (i * inner + j, 0, 0)
                ),
            ],
        ),
        out_shape=[
            jax.ShapeDtypeStruct((outer * inner * rows, 3 * cols), jnp.bfloat16),
            jax.ShapeDtypeStruct((outer * inner * rows, cols), jnp.bfloat16),
            jax.ShapeDtypeStruct((outer * inner, GAIN_ROWS, cols), jnp.bfloat16),
        ],
        name="assemble",
    )(place, *parts)


def gelu_parts(gate_pre):
    inner = jnp.tanh(GELU_SCALE * (gate_pre + GELU_CUBIC * gate_pre * gate_pre * gate_pre))
    gelu = 0.5 * gate_pre * (1.0 + inner)
    slope = 0.5 * (1.0 + inner) + 0.5 * gate_pre * (1.0 - inner * inner) * GELU_SCALE * (
        1.0 + 3.0 * GELU_CUBIC * gate_pre * gate_pre
    )
    return gelu, slope


def expert_forward_kernel(
    side_ref, near_ref, far_ref, gate_near, up_near, gate_far, up_far, hidden_ref, slope_ref, gelu_ref
):
    near = near_ref[...]
    far = far_ref[...]
    gate_pre = dot_nn(near, gate_near[...]) + dot_nn(far, gate_far[...])
    up_pre = dot_nn(near, up_near[...]) + dot_nn(far, up_far[...])
    gelu, slope = gelu_parts(gate_pre)
    hidden_ref[...] = (gelu * up_pre).astype(jnp.bfloat16)
    slope_ref[...] = slope * up_pre
    gelu_ref[...] = gelu


def slot_block(slots):
    return 288 if slots % 288 == 0 else slots


def expert_forward(side, near, far, weights, hidden_cols):
    slots, half = near.shape
    rows = slot_block(slots)
    row_spec = pl.BlockSpec((rows, half), lambda i, side_ref: (i, 0))
    wide_spec = pl.BlockSpec((rows, hidden_cols), lambda i, side_ref: (i, 0))

    def weight_spec(other, column):
        return pl.BlockSpec(
            (half, hidden_cols),
            lambda i, side_ref: (side_ref[0] ^ other, column),
            pipeline_mode=pl.Buffered(1),
        )

    return pl.pallas_call(
        expert_forward_kernel,
        grid_spec=pltpu.PrefetchScalarGridSpec(
            num_scalar_prefetch=1,
            grid=(slots // rows,),
            in_specs=[
                row_spec,
                row_spec,
                weight_spec(0, 0),
                weight_spec(0, 1),
                weight_spec(1, 0),
                weight_spec(1, 1),
            ],
            out_specs=[wide_spec] * 3,
        ),
        out_shape=[
            jax.ShapeDtypeStruct((slots, hidden_cols), jnp.bfloat16),
            jax.ShapeDtypeStruct((slots, hidden_cols), jnp.float32),
            jax.ShapeDtypeStruct((slots, hidden_cols), jnp.float32),
        ],
        compiler_params=pltpu.CompilerParams(vmem_limit_bytes=VMEM_BYTES),
        cost_estimate=pl.CostEstimate(
            flops=8 * slots * half * hidden_cols,
            transcendentals=slots * hidden_cols,
            bytes_accessed=10 * slots * hidden_cols + 8 * half * hidden_cols,
        ),
        name="expert_forward",
    )(side, near, far, weights, weights, weights, weights)


def expert_backward_kernel(
    side_ref,
    near_ref,
    far_ref,
    slope_ref,
    gelu_ref,
    down_near,
    down_far,
    gate_near,
    up_near,
    gate_far,
    up_far,
    pre_grad_ref,
    stay_ref,
    away_ref,
):
    cols = slope_ref.shape[1]
    hidden_grad = dot_nn(near_ref[...], down_near[...]) + dot_nn(far_ref[...], down_far[...])
    gate_grad = (hidden_grad * slope_ref[...]).astype(jnp.bfloat16)
    up_grad = (hidden_grad * gelu_ref[...]).astype(jnp.bfloat16)
    pre_grad_ref[:, :cols] = gate_grad
    pre_grad_ref[:, cols:] = up_grad
    away_ref[...] = (dot_nt(gate_grad, gate_far[...]) + dot_nt(up_grad, up_far[...])).astype(
        jnp.bfloat16
    )
    stay_ref[...] = dot_nt(gate_grad, gate_near[...]) + dot_nt(up_grad, up_near[...])


def expert_backward(side, near, far, slope, gelu, down, weights):
    slots, half = near.shape
    hidden_cols = slope.shape[1]
    rows = slot_block(slots)
    row_spec = pl.BlockSpec((rows, half), lambda i, side_ref: (i, 0))
    wide_spec = pl.BlockSpec((rows, hidden_cols), lambda i, side_ref: (i, 0))

    def weight_spec(other, column):
        return pl.BlockSpec(
            (half, hidden_cols),
            lambda i, side_ref: (side_ref[0] ^ other, column),
            pipeline_mode=pl.Buffered(1),
        )

    return pl.pallas_call(
        expert_backward_kernel,
        grid_spec=pltpu.PrefetchScalarGridSpec(
            num_scalar_prefetch=1,
            grid=(slots // rows,),
            in_specs=[
                row_spec,
                row_spec,
                wide_spec,
                wide_spec,
                weight_spec(0, 0),
                weight_spec(1, 0),
                weight_spec(0, 0),
                weight_spec(0, 1),
                weight_spec(1, 0),
                weight_spec(1, 1),
            ],
            out_specs=[
                pl.BlockSpec((rows, 2 * hidden_cols), lambda i, side_ref: (i, 0)),
                row_spec,
                row_spec,
            ],
        ),
        out_shape=[
            jax.ShapeDtypeStruct((slots, 2 * hidden_cols), jnp.bfloat16),
            jax.ShapeDtypeStruct((slots, half), jnp.float32),
            jax.ShapeDtypeStruct((slots, half), jnp.bfloat16),
        ],
        compiler_params=pltpu.CompilerParams(vmem_limit_bytes=VMEM_BYTES),
        cost_estimate=pl.CostEstimate(
            flops=12 * slots * half * hidden_cols,
            transcendentals=0,
            bytes_accessed=12 * slots * hidden_cols + 12 * half * hidden_cols,
        ),
        name="expert_backward",
    )(side, near, far, slope, gelu, down, down, weights, weights, weights, weights)


def on_device(
    tokens,
    cotangent,
    lengths,
    bucket_table,
    routes,
    gate_values,
    qkv_weight,
    out_weight,
    norm_gains,
    rel_bias,
    gate_weight,
    up_weight,
    down_weight,
):
    tok_rows, width = tokens.shape
    half = width // 2
    dp_count = lax.axis_size("dp")
    tensor_count = lax.axis_size("tensor")
    seq = tok_rows * tensor_count
    expert_count, shard_rows, hidden_cols = gate_weight.shape
    head_cols = qkv_weight.shape[2]
    head_count, bucket_count = rel_bias.shape
    capacity = 9 * seq // 64
    group_size = dp_count // expert_count
    slot_count = (capacity + group_size - 1) // group_size
    total_slots = dp_count * slot_count
    dp_index = lax.axis_index("dp")
    tensor_index = lax.axis_index("tensor")
    first_tensor = tensor_index == 0
    length = lengths[dp_index]
    length_row = length[None]
    group_valid = jnp.arange(seq, dtype=jnp.int32) < length
    own_valid = lax.dynamic_slice_in_dim(group_valid, tensor_index * tok_rows, tok_rows, 0)
    own_valid = own_valid.astype(jnp.float32)[:, None]

    def swap(block):
        return lax.ppermute(block, "tensor", [(0, 1), (1, 0)])

    def chain(block, earlier):
        return lax.optimization_barrier((block, earlier))

    def ordered(own, other, axis):
        return jnp.where(
            first_tensor,
            jnp.concatenate([own, other], axis=axis),
            jnp.concatenate([other, own], axis=axis),
        )

    def own_part(block, axis):
        size = block.shape[axis] // 2
        return lax.dynamic_slice_in_dim(block, tensor_index * size, size, axis)

    def other_part(block, axis):
        size = block.shape[axis] // 2
        return lax.dynamic_slice_in_dim(block, (1 - tensor_index) * size, size, axis)

    def exchange(block):
        return lax.all_to_all(block, "dp", split_axis=0, concat_axis=0, tiled=True)

    def home_order(weight):
        return jnp.repeat(weight, group_size, axis=0)

    def fetch(weight):
        return exchange(home_order(weight)).reshape(dp_count * shard_rows, weight.shape[2])

    def send_grad(grad):
        return exchange(grad.reshape(dp_count, shard_rows, grad.shape[1]))

    def route(rows):
        arrived = exchange(rows.reshape(dp_count, slot_count, rows.shape[1]))
        return arrived.reshape(total_slots, rows.shape[1])

    spare = slot_count - shard_rows
    fold = shard_rows // spare

    def pack(rows):
        blocks = rows.reshape(dp_count, slot_count, half)
        tail = blocks[:, shard_rows:].reshape(dp_count, spare, fold, half // fold)
        tail = tail.transpose(0, 2, 1, 3).reshape(dp_count, shard_rows, half // fold)
        return jnp.concatenate([blocks[:, :shard_rows], tail], axis=2)

    def unpack(packed):
        tail = packed[:, :, half:].reshape(dp_count, fold, spare, half // fold)
        tail = tail.transpose(0, 2, 1, 3).reshape(dp_count, spare, half)
        return jnp.concatenate([packed[:, :, :half], tail], axis=1).reshape(total_slots, half)

    def regroup(arrived):
        return jnp.sum(
            arrived.astype(jnp.float32).reshape(
                expert_count, group_size, shard_rows, arrived.shape[2]
            ),
            axis=1,
        )

    gain_pad = jnp.pad(norm_gains, ((0, GAIN_ROWS - 2), (0, head_cols - shard_rows)))
    layer_shard = jnp.concatenate(
        [qkv_weight.reshape(3 * shard_rows, head_cols), out_weight, gain_pad], axis=0
    )
    pairs = head_cols // LANES
    pair_expert = routes.reshape(-1)
    pair_valid = jnp.repeat(group_valid, 2)
    chosen = (
        pair_expert[:, None] == jnp.arange(expert_count, dtype=jnp.int32)[None, :]
    ) & pair_valid[:, None]
    pair_index = jnp.arange(2 * seq, dtype=jnp.int32)
    before = (pair_index[:, None] > pair_index[None, :]).astype(jnp.bfloat16)
    earlier_pairs = dot_nn(before, chosen.astype(jnp.bfloat16))
    position = jnp.sum(jnp.where(chosen, earlier_pairs, 0.0), axis=1).astype(jnp.int32)
    kept_pair = pair_valid & (position < capacity)
    device = pair_expert * group_size + position // slot_count
    pair_slot = jnp.where(
        kept_pair, device * slot_count + position % slot_count, total_slots
    ).reshape(seq, 2)
    slot_index = jnp.arange(total_slots, dtype=jnp.int32)
    first_hit = pair_slot[:, 0][None, :] == slot_index[:, None]
    second_hit = pair_slot[:, 1][None, :] == slot_index[:, None]
    no_gate = jnp.zeros((), jnp.bfloat16)
    pick = (first_hit | second_hit).astype(jnp.bfloat16)
    pick_gate = jnp.where(
        first_hit,
        gate_values[:, 0][None, :],
        jnp.where(second_hit, gate_values[:, 1][None, :], no_gate),
    )

    tokens_other = swap(tokens)
    mix_grad = lax.optimization_barrier(
        (own_valid * cotangent.astype(jnp.float32)).astype(jnp.bfloat16)
    )
    mix_other = swap(other_part(mix_grad, 1))
    out_grad_cols = dot_nn(
        pick_gate, ordered(own_part(mix_grad, 1), mix_other, 0)
    ).astype(jnp.bfloat16)
    residual, out_grad_cols = chain(tokens, out_grad_cols)
    gate_up = jnp.concatenate(
        [home_order(gate_weight), home_order(up_weight), pack(out_grad_cols)], axis=2
    )
    if dp_count == 16:
        across = [
            lax.ppermute(layer_shard, "dp", [(i, i ^ (4 * k)) for i in range(16)])
            for k in range(1, 4)
        ]
        gate_up, across = chain(gate_up, across)
        near = jnp.stack([layer_shard, *across])
        side = lax.ppermute(near, "dp", [(i, i ^ 2) for i in range(16)])
        core = [(i, i ^ 1) for i in range(16)]
        parts = [near, lax.ppermute(near, "dp", core), side, lax.ppermute(side, "dp", core)]
        place = jnp.stack([dp_index // 4, dp_index % 4])
        projection, out_all, gain_rows = assemble(place, parts)
    else:
        layer_all = lax.all_gather(layer_shard, "dp", axis=0, tiled=False)
        gate_up, layer_all = chain(gate_up, layer_all)
        projection = (
            layer_all[:, : 3 * shard_rows]
            .reshape(dp_count, 3, shard_rows, pairs, LANES)
            .transpose(0, 2, 3, 1, 4)
            .reshape(width, 3 * head_cols)
        )
        out_all = layer_all[:, 3 * shard_rows : 4 * shard_rows].reshape(width, head_cols)
        gain_rows = layer_all[:, 4 * shard_rows :]
    arrived = exchange(gate_up)
    gate_up_all = arrived.reshape(width, arrived.shape[2])
    slot_grad_half = unpack(arrived[:, :, 2 * hidden_cols :])

    distance = jnp.arange(2 * seq, dtype=jnp.int32)
    table_reversed = jnp.concatenate(
        [bucket_table[::-1], jnp.full((1,), bucket_count, jnp.int32)]
    )
    hot = (
        jnp.arange(bucket_count, dtype=jnp.int32)[:, None] == table_reversed[None, :]
    ).astype(jnp.float32)
    bias_rows = jnp.dot(rel_bias.astype(jnp.float32), hot, precision=HIGHEST).reshape(
        head_count // 2, 2, 2 * seq
    )
    gains_all = jnp.transpose(gain_rows[:, :2, :shard_rows], (1, 0, 2)).reshape(2, width)
    gain_one = gains_all[0].astype(jnp.float32)
    gain_two = gains_all[1].astype(jnp.float32)
    inputs_all = ordered(tokens, tokens_other, 0).astype(jnp.float32)
    scale_all = lax.rsqrt(jnp.mean(inputs_all * inputs_all, axis=-1, keepdims=True) + EPSILON)
    norm_one_all = (inputs_all * scale_all * gain_one).astype(jnp.bfloat16)
    joined = dot_nn(norm_one_all, projection).astype(jnp.bfloat16)
    attended, totals = attend_forward(length_row, joined, bias_rows)
    branch = dot_nt(attended, out_all)
    branch_other = swap(other_part(branch, 0).astype(jnp.bfloat16))
    inputs = residual.astype(jnp.float32)
    mid = inputs + own_valid * (own_part(branch, 0) + branch_other.astype(jnp.float32))
    mid_scale = lax.rsqrt(jnp.mean(mid * mid, axis=-1, keepdims=True) + EPSILON)
    norm_two = (mid * mid_scale * gain_two).astype(jnp.bfloat16)
    norm_two_cols = ordered(own_part(norm_two, 1), swap(other_part(norm_two, 1)), 0)
    expert_rows, slot_grad_half = chain(
        dot_nn(pick, norm_two_cols).astype(jnp.bfloat16), slot_grad_half
    )
    slot_grad_other = swap(slot_grad_half)
    down_late, (expert_half, slot_grad_other) = chain(
        down_weight, (route(expert_rows), slot_grad_other)
    )
    down_all = fetch(down_late)
    expert_other = swap(expert_half)

    side = tensor_index[None]
    hidden, slope, gelu = expert_forward(
        side, expert_half, expert_other, gate_up_all, hidden_cols
    )
    slot_grad = ordered(slot_grad_half, slot_grad_other, 1)
    down_grad, down_all = chain(dot_tn(slot_grad, hidden).astype(jnp.bfloat16), down_all)
    down_back = send_grad(down_grad)
    pre_grad, slot_back_stay, slot_back_away = expert_backward(
        side, slot_grad_half, slot_grad_other, slope, gelu, down_all, gate_up_all
    )
    hidden_late, slot_back_away = chain(hidden, slot_back_away)
    slot_back_other = swap(slot_back_away)
    expert_out_part = dot_nt(hidden_late, down_all)
    expert_out_away, slot_back_other = chain(
        other_part(expert_out_part, 1).astype(jnp.bfloat16), slot_back_other
    )
    slot_back_half = (
        slot_back_stay + slot_back_other.astype(jnp.float32)
    ).astype(jnp.bfloat16)
    expert_out_half = (
        own_part(expert_out_part, 1) + swap(expert_out_away).astype(jnp.float32)
    ).astype(jnp.bfloat16)
    slot_back_half, down_back = chain(slot_back_half, down_back)
    last, slot_back = chain(
        jnp.concatenate(
            [
                dot_tn(ordered(expert_half, expert_other, 1), pre_grad)
                .astype(jnp.bfloat16)
                .reshape(dp_count, shard_rows, 2 * hidden_cols),
                pack(expert_out_half),
            ],
            axis=2,
        ),
        route(slot_back_half),
    )
    arrived_back = exchange(last)

    back_cols = dot_tn(pick, slot_back)
    norm_two_grad = ordered(
        own_part(back_cols, 0), swap(other_part(back_cols, 0).astype(jnp.bfloat16)).astype(jnp.float32), 1
    )
    mid_unit = mid * mid_scale
    mid_inner = norm_two_grad * gain_two
    mid_grad = own_valid * cotangent.astype(jnp.float32) + mid_scale * (
        mid_inner - mid_unit * jnp.mean(mid_inner * mid_unit, axis=-1, keepdims=True)
    )
    gain_two_grad = jnp.sum(norm_two_grad * mid_unit, axis=0)
    branch_grad = (own_valid * mid_grad).astype(jnp.bfloat16)
    branch_grad_all = ordered(branch_grad, swap(branch_grad), 0)

    attended_grad = dot_nn(branch_grad_all, out_all).astype(jnp.bfloat16)
    joined_grad, bias_sums = attend_backward(
        length_row, joined, attended_grad, totals, bias_rows
    )
    bias_grad = jnp.dot(
        bias_sums.reshape(head_count, 2 * seq), hot.T, precision=HIGHEST
    )
    norm_one_part = dot_nt(joined_grad, projection)
    layer_part = jnp.concatenate(
        [
            dot_tn(norm_one_all, joined_grad).astype(jnp.bfloat16),
            dot_tn(branch_grad_all, attended).astype(jnp.bfloat16),
        ],
        axis=1,
    )
    gain_one_grad = jnp.sum(norm_one_part * (inputs_all * scale_all), axis=0)
    norm_one_grad = own_part(norm_one_part, 0) + swap(
        other_part(norm_one_part, 0).astype(jnp.bfloat16)
    ).astype(jnp.float32)
    scale = lax.rsqrt(jnp.mean(inputs * inputs, axis=-1, keepdims=True) + EPSILON)
    unit = inputs * scale
    inner = norm_one_grad * gain_one
    input_grad = mid_grad + scale * (
        inner - unit * jnp.mean(inner * unit, axis=-1, keepdims=True)
    )
    gain_part = jnp.concatenate([gain_one_grad, gain_two_grad]).reshape(-1, LANES)
    small = jnp.concatenate(
        [gain_part + swap(gain_part), bias_grad.reshape(-1, LANES)], axis=0
    )

    def partner(block, offset):
        return lax.ppermute(block, "dp", [(i, i ^ offset) for i in range(dp_count)])

    row_size = layer_part.shape[1]
    small = jnp.pad(small.reshape(-1), (0, -small.size % row_size)).reshape(-1, row_size)
    small_rows = small.shape[0]

    def with_small(block):
        high = lax.reduce_precision(small, 8, 7)
        rows = jnp.concatenate([high, small - high], axis=0).astype(jnp.bfloat16)
        rows = jnp.pad(rows, ((0, -rows.shape[0] % 8), (0, 0)))
        return jnp.concatenate([block, rows], axis=0)

    def small_of(block, first):
        rows = block[first : first + 2 * small_rows].astype(jnp.float32)
        return rows[:small_rows] + rows[small_rows:]

    if dp_count == 16:
        blocks = layer_part.reshape(dp_count, shard_rows, row_size)
        for step in (1, 2):
            pieces = blocks.reshape(-1, 2, shard_rows, row_size)
            bit = (dp_index // step) % 2
            away = lax.dynamic_index_in_dim(pieces, 1 - bit, 1, keepdims=False)
            stay = lax.dynamic_index_in_dim(pieces, bit, 1, keepdims=False)
            if step == 1:
                came = partner(away, step)
                small = small + partner(small, step)
            else:
                came = partner(with_small(away.reshape(-1, row_size)), step)
                came = chain(came, input_grad)[0]
                small = small + small_of(came, away.shape[0] * shard_rows)
                came = came[: away.shape[0] * shard_rows].reshape(away.shape)
            blocks = (stay.astype(jnp.float32) + came.astype(jnp.float32)).astype(jnp.bfloat16)
        outer = dp_index // 4
        leaving = [
            with_small(lax.dynamic_index_in_dim(blocks, outer ^ k, 0, keepdims=False))
            for k in range(1, 4)
        ]
        stay = lax.dynamic_index_in_dim(blocks, outer, 0, keepdims=False)
        arrived_back = chain(arrived_back, leaving)[0]
        came = [partner(piece, 4 * k) for k, piece in zip(range(1, 4), leaving, strict=True)]
    else:
        step = 1
        while step < dp_count:
            small = small + partner(small, step)
            step *= 2
    returned = unpack(arrived_back[:, :, 2 * hidden_cols :])
    mix_cols = dot_tn(pick_gate, returned)
    mix_away = other_part(mix_cols, 0).astype(jnp.bfloat16)
    arrived_back = chain(arrived_back, mix_away)[0]
    gate_grad = regroup(arrived_back[:, :, :hidden_cols])
    up_grad = regroup(arrived_back[:, :, hidden_cols : 2 * hidden_cols])
    mix_own = ordered(own_part(mix_cols, 0), swap(mix_away).astype(jnp.float32), 1)
    mixed = (mid + own_valid * mix_own).astype(jnp.bfloat16)
    if dp_count == 16:
        came = chain(came, (gate_grad, up_grad, mixed))[0]
        small = small + sum(small_of(piece, shard_rows) for piece in came)
        layer_grad = stay.astype(jnp.float32) + sum(
            piece[:shard_rows].astype(jnp.float32) for piece in came
        )
    else:
        layer_grad = lax.psum_scatter(
            layer_part, "dp", scatter_dimension=0, tiled=True
        ).astype(jnp.float32)
    qkv_grad = (
        layer_grad[:, : 3 * head_cols]
        .reshape(shard_rows, pairs, 3, LANES)
        .transpose(2, 0, 1, 3)
        .reshape(3, shard_rows, head_cols)
    )
    out_grad = layer_grad[:, 3 * head_cols :]
    gain_size = 2 * width
    gain_sums = small.reshape(-1)[:gain_size].reshape(2, width)
    bias_out = small.reshape(-1)[gain_size : gain_size + head_count * bucket_count].reshape(
        head_count, bucket_count
    )
    gains_grad = lax.dynamic_slice_in_dim(gain_sums, dp_index * shard_rows, shard_rows, 1)
    return (
        mixed,
        input_grad,
        qkv_grad,
        out_grad,
        gains_grad,
        bias_out,
        gate_grad,
        up_grad,
        regroup(down_back),
    )


def solution(mesh):
    rows = P(("dp", "tensor"), None)
    shard = P("dp", "tensor")
    stacked = P(None, "dp", "tensor")
    return jax.shard_map(
        on_device,
        mesh=mesh,
        in_specs=(
            rows,
            rows,
            P(),
            P(),
            P("dp", None),
            P("dp", None),
            stacked,
            shard,
            P(None, "dp"),
            P("tensor", None),
            stacked,
            stacked,
            stacked,
        ),
        out_specs=(
            rows,
            rows,
            stacked,
            shard,
            P(None, "dp"),
            P("tensor", None),
            stacked,
            stacked,
            stacked,
        ),
        check_vma=False,
    )
```

```python
import jax
import jax.numpy as jnp
from jax import lax
from jax.experimental import pallas as pl
from jax.experimental.pallas import tpu as pltpu
from jax.sharding import PartitionSpec as P

HEAD_DIM = 64
EPSILON = 1e-06
MASKED_SCORE = -1e30
HIGHEST = lax.Precision.HIGHEST
SCORE_SCALE = 0.125
QUERY_COLS = 256
LANES = 128
GELU_SCALE = 0.7978845608028654
GELU_CUBIC = 0.044715
GAIN_ROWS = 16
VMEM_BYTES = 48 * 2**20


def dot_nt(left, right):
    return lax.dot_general(
        left, right, (((1,), (1,)), ((), ())), preferred_element_type=jnp.float32
    )


def dot_nn(left, right):
    return lax.dot_general(
        left, right, (((1,), (0,)), ((), ())), preferred_element_type=jnp.float32
    )


def dot_tn(left, right):
    return lax.dot_general(
        left, right, (((0,), (0,)), ((), ())), preferred_element_type=jnp.float32
    )


def bias_base(bias_row, seq):
    return pltpu.roll(
        jnp.broadcast_to(bias_row, (LANES, 2 * seq)),
        2 * seq - (LANES - 1),
        1,
        stride=1,
        stride_axis=0,
    )


def masked_scores(keys, query_block, base_ref, start, seq, cols, length):
    scores = dot_nt(keys, query_block) * SCORE_SCALE
    blocks = []
    for first in range(0, seq, LANES):
        offset = seq - LANES - first + start
        block = scores[first : first + LANES] + base_ref[:, offset : offset + cols]
        key_index = lax.broadcasted_iota(jnp.int32, block.shape, 0) + first
        blocks.append(jnp.where(key_index < length, block, MASKED_SCORE))
    return jnp.concatenate(blocks, axis=0)


def head_part(ref, start, cols, head):
    lane = lax.broadcasted_iota(jnp.int32, (cols, LANES), 1)
    return jnp.where(
        lane // HEAD_DIM == head, ref[start : start + cols, :], jnp.zeros((), jnp.bfloat16)
    )


def forward_kernel(length_ref, joined_ref, bias_ref, out_ref, total_ref, base_ref):
    query_ref, key_ref, value_ref = [
        joined_ref.at[:, i * LANES : (i + 1) * LANES] for i in range(3)
    ]
    seq = joined_ref.shape[0]
    cols = min(QUERY_COLS, seq)
    length = length_ref[0]
    values_t = value_ref[...].T
    keys = key_ref[...]
    starts = range(0, seq, cols)
    outs = {}
    for head in range(LANES // HEAD_DIM):
        base_ref[...] = bias_base(bias_ref[0, head : head + 1, :], seq)
        for start in starts:
            query_block = head_part(query_ref, start, cols, head)
            scores = masked_scores(keys, query_block, base_ref, start, seq, cols, length)
            top = jnp.max(scores, axis=0, keepdims=True)
            exponent = jnp.exp(scores - top)
            total = jnp.sum(exponent, axis=0, keepdims=True)
            probs = (exponent * (1.0 / total)).astype(jnp.bfloat16)
            total_ref[0, head : head + 1, start : start + cols] = top + jnp.log(total)
            outs[start, head] = dot_nn(
                values_t[head * HEAD_DIM : (head + 1) * HEAD_DIM], probs
            )
    for start in starts:
        joined = jnp.concatenate(
            [outs[start, head] for head in range(LANES // HEAD_DIM)], axis=0
        )
        out_ref[start : start + cols, :] = joined.T.astype(jnp.bfloat16)


def attend_forward(length, joined, bias_rows):
    seq = joined.shape[0]
    width = joined.shape[1] // 3
    pairs = width // LANES
    heads = LANES // HEAD_DIM
    column = pl.BlockSpec((seq, LANES), lambda i: (0, i))
    return pl.pallas_call(
        forward_kernel,
        grid=(pairs,),
        in_specs=[
            pl.BlockSpec(memory_space=pltpu.SMEM),
            pl.BlockSpec((seq, 3 * LANES), lambda i: (0, i)),
            pl.BlockSpec((1, heads, 2 * seq), lambda i: (i, 0, 0)),
        ],
        out_specs=[column, pl.BlockSpec((1, heads, seq), lambda i: (i, 0, 0))],
        out_shape=[
            jax.ShapeDtypeStruct((seq, width), jnp.bfloat16),
            jax.ShapeDtypeStruct((pairs, heads, seq), jnp.float32),
        ],
        scratch_shapes=[pltpu.VMEM((LANES, 2 * seq), jnp.float32)],
        cost_estimate=pl.CostEstimate(
            flops=16 * seq * seq * width,
            transcendentals=seq * seq * width // HEAD_DIM,
            bytes_accessed=8 * seq * width,
        ),
        name="attend_forward",
    )(length, joined, bias_rows)


def diagonal_sums(acc_ref, seq):
    period = 2 * seq
    folded = acc_ref[0:8, :]
    for first in range(8, LANES, 8):
        folded = folded + pltpu.roll(acc_ref[first : first + 8, :], period - first, 1)
    row = lax.broadcasted_iota(jnp.int32, folded.shape, 0)
    for bit in (1, 2, 4):
        folded = jnp.where((row & bit) != 0, pltpu.roll(folded, period - bit, 1), folded)
    return pltpu.roll(jnp.sum(folded, axis=0, keepdims=True), LANES - 1, 1)


def backward_kernel(
    length_ref,
    joined_ref,
    grad_ref,
    total_ref,
    bias_ref,
    joined_grad_ref,
    bias_grad_ref,
    base_ref,
    acc_ref,
):
    query_ref, key_ref, value_ref = [
        joined_ref.at[:, i * LANES : (i + 1) * LANES] for i in range(3)
    ]
    seq = joined_ref.shape[0]
    cols = min(QUERY_COLS, seq)
    length = length_ref[0]
    keys = key_ref[...]
    values = value_ref[...]
    keys_t = keys.T
    starts = range(0, seq, cols)
    key_acc = jnp.zeros((seq, LANES), jnp.float32)
    value_acc = jnp.zeros((seq, LANES), jnp.float32)
    query_parts = {}
    for head in range(LANES // HEAD_DIM):
        base_ref[...] = bias_base(bias_ref[0, head : head + 1, :], seq)
        acc_ref[...] = jnp.zeros_like(acc_ref)
        for start in starts:
            query_block = head_part(query_ref, start, cols, head)
            grad_block = head_part(grad_ref, start, cols, head)
            scores = masked_scores(keys, query_block, base_ref, start, seq, cols, length)
            probs = jnp.exp(scores - total_ref[0, head : head + 1, start : start + cols])
            probs_grad = dot_nt(values, grad_block)
            mean_grad = jnp.sum(probs * probs_grad, axis=0, keepdims=True)
            score_grad = (probs * (probs_grad - mean_grad)).astype(jnp.bfloat16)
            value_acc = value_acc + dot_nn(probs.astype(jnp.bfloat16), grad_block)
            key_acc = key_acc + dot_nn(score_grad, query_block)
            query_parts[start, head] = dot_nn(
                keys_t[head * HEAD_DIM : (head + 1) * HEAD_DIM], score_grad
            )
            for first in range(0, seq, LANES):
                offset = seq - LANES - first + start
                acc_ref[:, offset : offset + cols] += score_grad[
                    first : first + LANES
                ].astype(jnp.float32)
        bias_grad_ref[0, head : head + 1, :] = diagonal_sums(acc_ref, seq)
    joined_grad_ref[:, LANES : 2 * LANES] = (key_acc * SCORE_SCALE).astype(jnp.bfloat16)
    joined_grad_ref[:, 2 * LANES :] = value_acc.astype(jnp.bfloat16)
    for start in starts:
        joined = jnp.concatenate(
            [query_parts[start, head] for head in range(LANES // HEAD_DIM)], axis=0
        )
        joined_grad_ref[start : start + cols, :LANES] = (joined * SCORE_SCALE).T.astype(
            jnp.bfloat16
        )


def attend_backward(length, joined, attended_grad, totals, bias_rows):
    seq, width = attended_grad.shape
    pairs = width // LANES
    heads = LANES // HEAD_DIM
    column = pl.BlockSpec((seq, LANES), lambda i: (0, i))
    triple = pl.BlockSpec((seq, 3 * LANES), lambda i: (0, i))
    vector = pl.BlockSpec((1, heads, 2 * seq), lambda i: (i, 0, 0))
    return pl.pallas_call(
        backward_kernel,
        grid=(pairs,),
        in_specs=[
            pl.BlockSpec(memory_space=pltpu.SMEM),
            triple,
            column,
            pl.BlockSpec((1, heads, seq), lambda i: (i, 0, 0)),
            vector,
        ],
        out_specs=[triple, vector],
        out_shape=[
            jax.ShapeDtypeStruct((seq, 3 * width), jnp.bfloat16),
            jax.ShapeDtypeStruct((pairs, heads, 2 * seq), jnp.float32),
        ],
        scratch_shapes=[
            pltpu.VMEM((LANES, 2 * seq), jnp.float32),
            pltpu.VMEM((LANES, 2 * seq), jnp.float32),
        ],
        cost_estimate=pl.CostEstimate(
            flops=40 * seq * seq * width,
            transcendentals=seq * seq * width // HEAD_DIM,
            bytes_accessed=14 * seq * width,
        ),
        name="attend_backward",
    )(length, joined, attended_grad, totals, bias_rows)


def assemble_kernel(place_ref, *refs):
    parts, (weight_ref, out_ref, gain_ref) = refs[:-3], refs[-3:]
    rows = weight_ref.shape[0] // len(parts)
    pairs = weight_ref.shape[1] // (3 * LANES)
    for index, part_ref in enumerate(parts):
        inner = index ^ place_ref[1]
        block = pl.ds(pl.multiple_of(inner * rows, rows), rows)
        for kind in range(3):
            for pair in range(pairs):
                first = (3 * pair + kind) * LANES
                weight_ref[block, first : first + LANES] = part_ref[
                    0, kind * rows : (kind + 1) * rows, pair * LANES : (pair + 1) * LANES
                ]
        out_ref[block, :] = part_ref[0, 3 * rows : 4 * rows, :]
        gain_ref[pl.ds(inner, 1)] = part_ref[:, 4 * rows :, :]


def assemble(place, parts):
    outer, block_rows, cols = parts[0].shape
    inner = len(parts)
    rows = (block_rows - GAIN_ROWS) // 4
    block = pl.BlockSpec((1, block_rows, cols), lambda i, place_ref: (i ^ place_ref[0], 0, 0))
    return pl.pallas_call(
        assemble_kernel,
        grid_spec=pltpu.PrefetchScalarGridSpec(
            num_scalar_prefetch=1,
            grid=(outer,),
            in_specs=[block] * inner,
            out_specs=[
                pl.BlockSpec((inner * rows, 3 * cols), lambda i, place_ref: (i, 0)),
                pl.BlockSpec((inner * rows, cols), lambda i, place_ref: (i, 0)),
                pl.BlockSpec((inner, GAIN_ROWS, cols), lambda i, place_ref: (i, 0, 0)),
            ],
        ),
        out_shape=[
            jax.ShapeDtypeStruct((outer * inner * rows, 3 * cols), jnp.bfloat16),
            jax.ShapeDtypeStruct((outer * inner * rows, cols), jnp.bfloat16),
            jax.ShapeDtypeStruct((outer * inner, GAIN_ROWS, cols), jnp.bfloat16),
        ],
        name="assemble",
    )(place, *parts)


def gelu_parts(gate_pre):
    inner = jnp.tanh(GELU_SCALE * (gate_pre + GELU_CUBIC * gate_pre * gate_pre * gate_pre))
    gelu = 0.5 * gate_pre * (1.0 + inner)
    slope = 0.5 * (1.0 + inner) + 0.5 * gate_pre * (1.0 - inner * inner) * GELU_SCALE * (
        1.0 + 3.0 * GELU_CUBIC * gate_pre * gate_pre
    )
    return gelu, slope


def expert_forward_kernel(
    side_ref, near_ref, far_ref, gate_near, up_near, gate_far, up_far, hidden_ref, slope_ref, gelu_ref
):
    near = near_ref[...]
    far = far_ref[...]
    gate_pre = dot_nn(near, gate_near[...]) + dot_nn(far, gate_far[...])
    up_pre = dot_nn(near, up_near[...]) + dot_nn(far, up_far[...])
    gelu, slope = gelu_parts(gate_pre)
    hidden_ref[...] = (gelu * up_pre).astype(jnp.bfloat16)
    slope_ref[...] = slope * up_pre
    gelu_ref[...] = gelu


def slot_block(slots):
    return 288 if slots % 288 == 0 else slots


def expert_forward(side, near, far, weights, hidden_cols):
    slots, half = near.shape
    rows = slot_block(slots)
    row_spec = pl.BlockSpec((rows, half), lambda i, side_ref: (i, 0))
    wide_spec = pl.BlockSpec((rows, hidden_cols), lambda i, side_ref: (i, 0))

    def weight_spec(other, column):
        return pl.BlockSpec(
            (half, hidden_cols),
            lambda i, side_ref: (side_ref[0] ^ other, column),
            pipeline_mode=pl.Buffered(1),
        )

    return pl.pallas_call(
        expert_forward_kernel,
        grid_spec=pltpu.PrefetchScalarGridSpec(
            num_scalar_prefetch=1,
            grid=(slots // rows,),
            in_specs=[
                row_spec,
                row_spec,
                weight_spec(0, 0),
                weight_spec(0, 1),
                weight_spec(1, 0),
                weight_spec(1, 1),
            ],
            out_specs=[wide_spec] * 3,
        ),
        out_shape=[
            jax.ShapeDtypeStruct((slots, hidden_cols), jnp.bfloat16),
            jax.ShapeDtypeStruct((slots, hidden_cols), jnp.float32),
            jax.ShapeDtypeStruct((slots, hidden_cols), jnp.float32),
        ],
        compiler_params=pltpu.CompilerParams(vmem_limit_bytes=VMEM_BYTES),
        cost_estimate=pl.CostEstimate(
            flops=8 * slots * half * hidden_cols,
            transcendentals=slots * hidden_cols,
            bytes_accessed=10 * slots * hidden_cols + 8 * half * hidden_cols,
        ),
        name="expert_forward",
    )(side, near, far, weights, weights, weights, weights)


def expert_backward_kernel(
    side_ref,
    near_ref,
    far_ref,
    slope_ref,
    gelu_ref,
    down_near,
    down_far,
    gate_near,
    up_near,
    gate_far,
    up_far,
    pre_grad_ref,
    stay_ref,
    away_ref,
):
    cols = slope_ref.shape[1]
    hidden_grad = dot_nn(near_ref[...], down_near[...]) + dot_nn(far_ref[...], down_far[...])
    gate_grad = (hidden_grad * slope_ref[...]).astype(jnp.bfloat16)
    up_grad = (hidden_grad * gelu_ref[...]).astype(jnp.bfloat16)
    pre_grad_ref[:, :cols] = gate_grad
    pre_grad_ref[:, cols:] = up_grad
    away_ref[...] = (dot_nt(gate_grad, gate_far[...]) + dot_nt(up_grad, up_far[...])).astype(
        jnp.bfloat16
    )
    stay_ref[...] = dot_nt(gate_grad, gate_near[...]) + dot_nt(up_grad, up_near[...])


def expert_backward(side, near, far, slope, gelu, down, weights):
    slots, half = near.shape
    hidden_cols = slope.shape[1]
    rows = slot_block(slots)
    row_spec = pl.BlockSpec((rows, half), lambda i, side_ref: (i, 0))
    wide_spec = pl.BlockSpec((rows, hidden_cols), lambda i, side_ref: (i, 0))

    def weight_spec(other, column):
        return pl.BlockSpec(
            (half, hidden_cols),
            lambda i, side_ref: (side_ref[0] ^ other, column),
            pipeline_mode=pl.Buffered(1),
        )

    return pl.pallas_call(
        expert_backward_kernel,
        grid_spec=pltpu.PrefetchScalarGridSpec(
            num_scalar_prefetch=1,
            grid=(slots // rows,),
            in_specs=[
                row_spec,
                row_spec,
                wide_spec,
                wide_spec,
                weight_spec(0, 0),
                weight_spec(1, 0),
                weight_spec(0, 0),
                weight_spec(0, 1),
                weight_spec(1, 0),
                weight_spec(1, 1),
            ],
            out_specs=[
                pl.BlockSpec((rows, 2 * hidden_cols), lambda i, side_ref: (i, 0)),
                row_spec,
                row_spec,
            ],
        ),
        out_shape=[
            jax.ShapeDtypeStruct((slots, 2 * hidden_cols), jnp.bfloat16),
            jax.ShapeDtypeStruct((slots, half), jnp.float32),
            jax.ShapeDtypeStruct((slots, half), jnp.bfloat16),
        ],
        compiler_params=pltpu.CompilerParams(vmem_limit_bytes=VMEM_BYTES),
        cost_estimate=pl.CostEstimate(
            flops=12 * slots * half * hidden_cols,
            transcendentals=0,
            bytes_accessed=12 * slots * hidden_cols + 12 * half * hidden_cols,
        ),
        name="expert_backward",
    )(side, near, far, slope, gelu, down, down, weights, weights, weights, weights)


def on_device(
    tokens,
    cotangent,
    lengths,
    bucket_table,
    routes,
    gate_values,
    qkv_weight,
    out_weight,
    norm_gains,
    rel_bias,
    gate_weight,
    up_weight,
    down_weight,
):
    tok_rows, width = tokens.shape
    half = width // 2
    dp_count = lax.axis_size("dp")
    tensor_count = lax.axis_size("tensor")
    seq = tok_rows * tensor_count
    expert_count, shard_rows, hidden_cols = gate_weight.shape
    head_cols = qkv_weight.shape[2]
    head_count, bucket_count = rel_bias.shape
    capacity = 9 * seq // 64
    group_size = dp_count // expert_count
    slot_count = (capacity + group_size - 1) // group_size
    total_slots = dp_count * slot_count
    dp_index = lax.axis_index("dp")
    tensor_index = lax.axis_index("tensor")
    first_tensor = tensor_index == 0
    length = lengths[dp_index]
    length_row = length[None]
    group_valid = jnp.arange(seq, dtype=jnp.int32) < length
    own_valid = lax.dynamic_slice_in_dim(group_valid, tensor_index * tok_rows, tok_rows, 0)
    own_valid = own_valid.astype(jnp.float32)[:, None]

    def swap(block):
        return lax.ppermute(block, "tensor", [(0, 1), (1, 0)])

    def partner(block, offset):
        return lax.ppermute(block, "dp", [(i, i ^ offset) for i in range(dp_count)])

    def chain(block, earlier):
        return lax.optimization_barrier((block, earlier))

    def ordered(own, other, axis):
        return jnp.where(
            first_tensor,
            jnp.concatenate([own, other], axis=axis),
            jnp.concatenate([other, own], axis=axis),
        )

    def own_part(block, axis):
        size = block.shape[axis] // 2
        return lax.dynamic_slice_in_dim(block, tensor_index * size, size, axis)

    def other_part(block, axis):
        size = block.shape[axis] // 2
        return lax.dynamic_slice_in_dim(block, (1 - tensor_index) * size, size, axis)

    def exchange(block):
        return lax.all_to_all(block, "dp", split_axis=0, concat_axis=0, tiled=True)

    def home_order(weight):
        return jnp.repeat(weight, group_size, axis=0)

    def fetch(weight):
        return exchange(home_order(weight)).reshape(dp_count * shard_rows, weight.shape[2])

    def send_grad(grad):
        return exchange(grad.reshape(dp_count, shard_rows, grad.shape[1]))

    def route(rows):
        arrived = exchange(rows.reshape(dp_count, slot_count, rows.shape[1]))
        return arrived.reshape(total_slots, rows.shape[1])

    spare = slot_count - shard_rows
    fold = shard_rows // spare

    def pack(rows):
        blocks = rows.reshape(dp_count, slot_count, half)
        tail = blocks[:, shard_rows:].reshape(dp_count, spare, fold, half // fold)
        tail = tail.transpose(0, 2, 1, 3).reshape(dp_count, shard_rows, half // fold)
        return jnp.concatenate([blocks[:, :shard_rows], tail], axis=2)

    def unpack(packed):
        tail = packed[:, :, half:].reshape(dp_count, fold, spare, half // fold)
        tail = tail.transpose(0, 2, 1, 3).reshape(dp_count, spare, half)
        return jnp.concatenate([packed[:, :, :half], tail], axis=1).reshape(total_slots, half)

    def regroup(arrived):
        return jnp.sum(
            arrived.astype(jnp.float32).reshape(
                expert_count, group_size, shard_rows, arrived.shape[2]
            ),
            axis=1,
        )

    gain_pad = jnp.pad(norm_gains, ((0, GAIN_ROWS - 2), (0, head_cols - shard_rows)))
    layer_shard = jnp.concatenate(
        [qkv_weight.reshape(3 * shard_rows, head_cols), out_weight, gain_pad], axis=0
    )
    pairs = head_cols // LANES
    pair_expert = routes.reshape(-1)
    pair_valid = jnp.repeat(group_valid, 2)
    chosen = (
        pair_expert[:, None] == jnp.arange(expert_count, dtype=jnp.int32)[None, :]
    ) & pair_valid[:, None]
    pair_index = jnp.arange(2 * seq, dtype=jnp.int32)
    before = (pair_index[:, None] > pair_index[None, :]).astype(jnp.bfloat16)
    earlier_pairs = dot_nn(before, chosen.astype(jnp.bfloat16))
    position = jnp.sum(jnp.where(chosen, earlier_pairs, 0.0), axis=1).astype(jnp.int32)
    kept_pair = pair_valid & (position < capacity)
    device = pair_expert * group_size + position // slot_count
    pair_slot = jnp.where(
        kept_pair, device * slot_count + position % slot_count, total_slots
    ).reshape(seq, 2)
    slot_index = jnp.arange(total_slots, dtype=jnp.int32)
    first_hit = pair_slot[:, 0][None, :] == slot_index[:, None]
    second_hit = pair_slot[:, 1][None, :] == slot_index[:, None]
    no_gate = jnp.zeros((), jnp.bfloat16)
    pick = (first_hit | second_hit).astype(jnp.bfloat16)
    pick_gate = jnp.where(
        first_hit,
        gate_values[:, 0][None, :],
        jnp.where(second_hit, gate_values[:, 1][None, :], no_gate),
    )

    mix_grad = lax.optimization_barrier(
        (own_valid * cotangent.astype(jnp.float32)).astype(jnp.bfloat16)
    )
    mix_away = other_part(mix_grad, 1)
    mix_other = swap(mix_away)
    tokens_other = swap(chain(tokens, mix_away)[0])
    out_grad_cols = dot_nn(
        pick_gate, ordered(own_part(mix_grad, 1), mix_other, 0)
    ).astype(jnp.bfloat16)
    residual, out_grad_cols = chain(tokens, out_grad_cols)
    gate_up = jnp.concatenate([home_order(gate_weight), home_order(up_weight)], axis=2)
    if dp_count == 16:
        across = [partner(layer_shard, 4 * k) for k in range(1, 4)]
        gate_up = chain(gate_up, across)[0]
        near = jnp.stack([layer_shard, *across])
        side = partner(near, 2)
        parts = [near, partner(near, 1), side, partner(side, 1)]
        place = jnp.stack([dp_index // 4, dp_index % 4])
        projection, out_all, gain_rows = assemble(place, parts)
    else:
        layer_all = lax.all_gather(layer_shard, "dp", axis=0, tiled=False)
        gate_up = chain(gate_up, layer_all)[0]
        projection = (
            layer_all[:, : 3 * shard_rows]
            .reshape(dp_count, 3, shard_rows, pairs, LANES)
            .transpose(0, 2, 3, 1, 4)
            .reshape(width, 3 * head_cols)
        )
        out_all = layer_all[:, 3 * shard_rows : 4 * shard_rows].reshape(width, head_cols)
        gain_rows = layer_all[:, 4 * shard_rows :]
    gate_up_all = exchange(gate_up).reshape(width, 2 * hidden_cols)

    distance = jnp.arange(2 * seq, dtype=jnp.int32)
    table_reversed = jnp.concatenate(
        [bucket_table[::-1], jnp.full((1,), bucket_count, jnp.int32)]
    )
    hot = (
        jnp.arange(bucket_count, dtype=jnp.int32)[:, None] == table_reversed[None, :]
    ).astype(jnp.float32)
    bias_rows = jnp.dot(rel_bias.astype(jnp.float32), hot, precision=HIGHEST).reshape(
        head_count // 2, 2, 2 * seq
    )
    gains_all = jnp.transpose(gain_rows[:, :2, :shard_rows], (1, 0, 2)).reshape(2, width)
    gain_one = gains_all[0].astype(jnp.float32)
    gain_two = gains_all[1].astype(jnp.float32)
    inputs_all = ordered(tokens, tokens_other, 0).astype(jnp.float32)
    scale_all = lax.rsqrt(jnp.mean(inputs_all * inputs_all, axis=-1, keepdims=True) + EPSILON)
    norm_one_all = (inputs_all * scale_all * gain_one).astype(jnp.bfloat16)
    joined = dot_nn(norm_one_all, projection).astype(jnp.bfloat16)
    attended, totals = attend_forward(length_row, joined, bias_rows)
    branch = dot_nt(attended, out_all)
    branch_other = swap(other_part(branch, 0).astype(jnp.bfloat16))
    inputs = residual.astype(jnp.float32)
    mid = inputs + own_valid * (own_part(branch, 0) + branch_other.astype(jnp.float32))
    mid_scale = lax.rsqrt(jnp.mean(mid * mid, axis=-1, keepdims=True) + EPSILON)
    norm_two = (mid * mid_scale * gain_two).astype(jnp.bfloat16)
    norm_two_cols = ordered(own_part(norm_two, 1), swap(other_part(norm_two, 1)), 0)
    slot_rows, gate_up_all = chain(
        jnp.concatenate(
            [dot_nn(pick, norm_two_cols).astype(jnp.bfloat16), out_grad_cols], axis=1
        ),
        gate_up_all,
    )
    down_late, slot_rows = chain(down_weight, route(slot_rows))
    down_all = fetch(down_late)
    expert_half = slot_rows[:, :half]
    expert_other = swap(expert_half)
    slot_grad_half = chain(slot_rows[:, half:], expert_other)[0]
    slot_grad_other = swap(slot_grad_half)

    side = tensor_index[None]
    hidden, slope, gelu = expert_forward(
        side, expert_half, expert_other, gate_up_all, hidden_cols
    )
    slot_grad = ordered(slot_grad_half, slot_grad_other, 1)
    down_grad, down_all = chain(dot_tn(slot_grad, hidden).astype(jnp.bfloat16), down_all)
    down_back = send_grad(down_grad)
    pre_grad, slot_back_stay, slot_back_away = expert_backward(
        side, slot_grad_half, slot_grad_other, slope, gelu, down_all, gate_up_all
    )
    hidden_late, slot_back_away = chain(hidden, slot_back_away)
    slot_back_other = swap(slot_back_away)
    expert_out_part = dot_nt(hidden_late, down_all)
    expert_out_away, slot_back_other = chain(
        other_part(expert_out_part, 1).astype(jnp.bfloat16), slot_back_other
    )
    slot_back_half = (
        slot_back_stay + slot_back_other.astype(jnp.float32)
    ).astype(jnp.bfloat16)
    expert_out_half = (
        own_part(expert_out_part, 1) + swap(expert_out_away).astype(jnp.float32)
    ).astype(jnp.bfloat16)
    slot_back_half, down_back = chain(slot_back_half, down_back)
    last, slot_back = chain(
        jnp.concatenate(
            [
                dot_tn(ordered(expert_half, expert_other, 1), pre_grad)
                .astype(jnp.bfloat16)
                .reshape(dp_count, shard_rows, 2 * hidden_cols),
                pack(expert_out_half),
            ],
            axis=2,
        ),
        route(slot_back_half),
    )
    arrived_back = exchange(last)

    back_cols = dot_tn(pick, slot_back)
    norm_two_grad = ordered(
        own_part(back_cols, 0), swap(other_part(back_cols, 0).astype(jnp.bfloat16)).astype(jnp.float32), 1
    )
    mid_unit = mid * mid_scale
    mid_inner = norm_two_grad * gain_two
    mid_grad = own_valid * cotangent.astype(jnp.float32) + mid_scale * (
        mid_inner - mid_unit * jnp.mean(mid_inner * mid_unit, axis=-1, keepdims=True)
    )
    gain_two_grad = jnp.sum(norm_two_grad * mid_unit, axis=0)
    branch_grad = (own_valid * mid_grad).astype(jnp.bfloat16)
    branch_grad_all = ordered(branch_grad, swap(branch_grad), 0)

    attended_grad = dot_nn(branch_grad_all, out_all).astype(jnp.bfloat16)
    joined_grad, bias_sums = attend_backward(
        length_row, joined, attended_grad, totals, bias_rows
    )
    bias_grad = jnp.dot(
        bias_sums.reshape(head_count, 2 * seq), hot.T, precision=HIGHEST
    )
    norm_one_part = dot_nt(joined_grad, projection)
    layer_part = jnp.concatenate(
        [
            dot_tn(norm_one_all, joined_grad).astype(jnp.bfloat16),
            dot_tn(branch_grad_all, attended).astype(jnp.bfloat16),
        ],
        axis=1,
    )
    gain_one_grad = jnp.sum(norm_one_part * (inputs_all * scale_all), axis=0)
    norm_one_grad = own_part(norm_one_part, 0) + swap(
        other_part(norm_one_part, 0).astype(jnp.bfloat16)
    ).astype(jnp.float32)
    scale = lax.rsqrt(jnp.mean(inputs * inputs, axis=-1, keepdims=True) + EPSILON)
    unit = inputs * scale
    inner = norm_one_grad * gain_one
    input_grad = mid_grad + scale * (
        inner - unit * jnp.mean(inner * unit, axis=-1, keepdims=True)
    )
    gain_part = jnp.concatenate([gain_one_grad, gain_two_grad]).reshape(-1, LANES)
    small = jnp.concatenate(
        [gain_part + swap(gain_part), bias_grad.reshape(-1, LANES)], axis=0
    )

    row_size = layer_part.shape[1]
    small = jnp.pad(small.reshape(-1), (0, -small.size % row_size)).reshape(-1, row_size)
    small_rows = small.shape[0]

    def with_small(block):
        high = lax.reduce_precision(small, 8, 7)
        rows = jnp.concatenate([high, small - high], axis=0).astype(jnp.bfloat16)
        rows = jnp.pad(rows, ((0, -rows.shape[0] % 8), (0, 0)))
        return jnp.concatenate([block, rows], axis=0)

    def small_of(block, first):
        rows = block[first : first + 2 * small_rows].astype(jnp.float32)
        return rows[:small_rows] + rows[small_rows:]

    if dp_count == 16:
        blocks = layer_part.reshape(dp_count, shard_rows, row_size)
        for step in (1, 2):
            pieces = blocks.reshape(-1, 2, shard_rows, row_size)
            bit = (dp_index // step) % 2
            away = lax.dynamic_index_in_dim(pieces, 1 - bit, 1, keepdims=False)
            stay = lax.dynamic_index_in_dim(pieces, bit, 1, keepdims=False)
            if step == 1:
                came = partner(away, step)
                small = small + partner(small, step)
            else:
                came = partner(with_small(away.reshape(-1, row_size)), step)
                came = chain(came, input_grad)[0]
                small = small + small_of(came, away.shape[0] * shard_rows)
                came = came[: away.shape[0] * shard_rows].reshape(away.shape)
            blocks = (stay.astype(jnp.float32) + came.astype(jnp.float32)).astype(jnp.bfloat16)
        outer = dp_index // 4
        leaving = [
            with_small(lax.dynamic_index_in_dim(blocks, outer ^ k, 0, keepdims=False))
            for k in range(1, 4)
        ]
        stay = lax.dynamic_index_in_dim(blocks, outer, 0, keepdims=False)
        arrived_back = chain(arrived_back, leaving)[0]
        came = [partner(piece, 4 * k) for k, piece in zip(range(1, 4), leaving, strict=True)]
    else:
        step = 1
        while step < dp_count:
            small = small + partner(small, step)
            step *= 2
    returned = unpack(arrived_back[:, :, 2 * hidden_cols :])
    mix_cols = dot_tn(pick_gate, returned)
    mix_away = other_part(mix_cols, 0).astype(jnp.bfloat16)
    arrived_back = chain(arrived_back, mix_away)[0]
    gate_grad = regroup(arrived_back[:, :, :hidden_cols])
    up_grad = regroup(arrived_back[:, :, hidden_cols : 2 * hidden_cols])
    mix_own = ordered(own_part(mix_cols, 0), swap(mix_away).astype(jnp.float32), 1)
    mixed = (mid + own_valid * mix_own).astype(jnp.bfloat16)
    if dp_count == 16:
        came = chain(came, (gate_grad, up_grad, mixed))[0]
        small = small + sum(small_of(piece, shard_rows) for piece in came)
        layer_grad = stay.astype(jnp.float32) + sum(
            piece[:shard_rows].astype(jnp.float32) for piece in came
        )
    else:
        layer_grad = lax.psum_scatter(
            layer_part, "dp", scatter_dimension=0, tiled=True
        ).astype(jnp.float32)
    qkv_grad = (
        layer_grad[:, : 3 * head_cols]
        .reshape(shard_rows, pairs, 3, LANES)
        .transpose(2, 0, 1, 3)
        .reshape(3, shard_rows, head_cols)
    )
    out_grad = layer_grad[:, 3 * head_cols :]
    gain_size = 2 * width
    gain_sums = small.reshape(-1)[:gain_size].reshape(2, width)
    bias_out = small.reshape(-1)[gain_size : gain_size + head_count * bucket_count].reshape(
        head_count, bucket_count
    )
    gains_grad = lax.dynamic_slice_in_dim(gain_sums, dp_index * shard_rows, shard_rows, 1)
    return (
        mixed,
        input_grad,
        qkv_grad,
        out_grad,
        gains_grad,
        bias_out,
        gate_grad,
        up_grad,
        regroup(down_back),
    )


def solution(mesh):
    rows = P(("dp", "tensor"), None)
    shard = P("dp", "tensor")
    stacked = P(None, "dp", "tensor")
    return jax.shard_map(
        on_device,
        mesh=mesh,
        in_specs=(
            rows,
            rows,
            P(),
            P(),
            P("dp", None),
            P("dp", None),
            stacked,
            shard,
            P(None, "dp"),
            P("tensor", None),
            stacked,
            stacked,
            stacked,
        ),
        out_specs=(
            rows,
            rows,
            stacked,
            shard,
            P(None, "dp"),
            P("tensor", None),
            stacked,
            stacked,
            stacked,
        ),
        check_vma=False,
    )
```

```python
import jax
import jax.numpy as jnp
from jax import lax
from jax.experimental import pallas as pl
from jax.experimental.pallas import tpu as pltpu
from jax.sharding import PartitionSpec as P

HEAD_DIM = 64
EPSILON = 1e-06
MASKED_SCORE = -1e30
HIGHEST = lax.Precision.HIGHEST
SCORE_SCALE = 0.125
QUERY_COLS = 256
LANES = 128
GELU_SCALE = 0.7978845608028654
GELU_CUBIC = 0.044715
GAIN_ROWS = 16
VMEM_BYTES = 48 * 2**20


def dot_nt(left, right):
    return lax.dot_general(
        left, right, (((1,), (1,)), ((), ())), preferred_element_type=jnp.float32
    )


def dot_nn(left, right):
    return lax.dot_general(
        left, right, (((1,), (0,)), ((), ())), preferred_element_type=jnp.float32
    )


def dot_tn(left, right):
    return lax.dot_general(
        left, right, (((0,), (0,)), ((), ())), preferred_element_type=jnp.float32
    )


def bias_base(bias_row, seq):
    return pltpu.roll(
        jnp.broadcast_to(bias_row, (LANES, 2 * seq)),
        2 * seq - (LANES - 1),
        1,
        stride=1,
        stride_axis=0,
    )


def masked_scores(keys, query_block, base_ref, start, seq, cols, length):
    scores = dot_nt(keys, query_block) * SCORE_SCALE
    blocks = []
    for first in range(0, seq, LANES):
        offset = seq - LANES - first + start
        block = scores[first : first + LANES] + base_ref[:, offset : offset + cols]
        key_index = lax.broadcasted_iota(jnp.int32, block.shape, 0) + first
        blocks.append(jnp.where(key_index < length, block, MASKED_SCORE))
    return jnp.concatenate(blocks, axis=0)


def head_part(ref, start, cols, head):
    lane = lax.broadcasted_iota(jnp.int32, (cols, LANES), 1)
    return jnp.where(
        lane // HEAD_DIM == head, ref[start : start + cols, :], jnp.zeros((), jnp.bfloat16)
    )


def forward_kernel(length_ref, joined_ref, bias_ref, out_ref, total_ref, base_ref):
    query_ref, key_ref, value_ref = [
        joined_ref.at[:, i * LANES : (i + 1) * LANES] for i in range(3)
    ]
    seq = joined_ref.shape[0]
    cols = min(QUERY_COLS, seq)
    length = length_ref[0]
    values_t = value_ref[...].T
    keys = key_ref[...]
    starts = range(0, seq, cols)
    outs = {}
    for head in range(LANES // HEAD_DIM):
        base_ref[...] = bias_base(bias_ref[0, head : head + 1, :], seq)
        for start in starts:
            query_block = head_part(query_ref, start, cols, head)
            scores = masked_scores(keys, query_block, base_ref, start, seq, cols, length)
            top = jnp.max(scores, axis=0, keepdims=True)
            exponent = jnp.exp(scores - top)
            total = jnp.sum(exponent, axis=0, keepdims=True)
            probs = (exponent * (1.0 / total)).astype(jnp.bfloat16)
            total_ref[0, head : head + 1, start : start + cols] = top + jnp.log(total)
            outs[start, head] = dot_nn(
                values_t[head * HEAD_DIM : (head + 1) * HEAD_DIM], probs
            )
    for start in starts:
        joined = jnp.concatenate(
            [outs[start, head] for head in range(LANES // HEAD_DIM)], axis=0
        )
        out_ref[start : start + cols, :] = joined.T.astype(jnp.bfloat16)


def attend_forward(length, joined, bias_rows):
    seq = joined.shape[0]
    width = joined.shape[1] // 3
    pairs = width // LANES
    heads = LANES // HEAD_DIM
    column = pl.BlockSpec((seq, LANES), lambda i: (0, i))
    return pl.pallas_call(
        forward_kernel,
        grid=(pairs,),
        in_specs=[
            pl.BlockSpec(memory_space=pltpu.SMEM),
            pl.BlockSpec((seq, 3 * LANES), lambda i: (0, i)),
            pl.BlockSpec((1, heads, 2 * seq), lambda i: (i, 0, 0)),
        ],
        out_specs=[column, pl.BlockSpec((1, heads, seq), lambda i: (i, 0, 0))],
        out_shape=[
            jax.ShapeDtypeStruct((seq, width), jnp.bfloat16),
            jax.ShapeDtypeStruct((pairs, heads, seq), jnp.float32),
        ],
        scratch_shapes=[pltpu.VMEM((LANES, 2 * seq), jnp.float32)],
        cost_estimate=pl.CostEstimate(
            flops=16 * seq * seq * width,
            transcendentals=seq * seq * width // HEAD_DIM,
            bytes_accessed=8 * seq * width,
        ),
        name="attend_forward",
    )(length, joined, bias_rows)


def diagonal_sums(acc_ref, seq):
    period = 2 * seq
    folded = acc_ref[0:8, :]
    for first in range(8, LANES, 8):
        folded = folded + pltpu.roll(acc_ref[first : first + 8, :], period - first, 1)
    row = lax.broadcasted_iota(jnp.int32, folded.shape, 0)
    for bit in (1, 2, 4):
        folded = jnp.where((row & bit) != 0, pltpu.roll(folded, period - bit, 1), folded)
    return pltpu.roll(jnp.sum(folded, axis=0, keepdims=True), LANES - 1, 1)


def backward_kernel(
    length_ref,
    joined_ref,
    grad_ref,
    total_ref,
    bias_ref,
    joined_grad_ref,
    bias_grad_ref,
    base_ref,
    acc_ref,
):
    query_ref, key_ref, value_ref = [
        joined_ref.at[:, i * LANES : (i + 1) * LANES] for i in range(3)
    ]
    seq = joined_ref.shape[0]
    cols = min(QUERY_COLS, seq)
    length = length_ref[0]
    keys = key_ref[...]
    values = value_ref[...]
    keys_t = keys.T
    starts = range(0, seq, cols)
    key_acc = jnp.zeros((seq, LANES), jnp.float32)
    value_acc = jnp.zeros((seq, LANES), jnp.float32)
    query_parts = {}
    for head in range(LANES // HEAD_DIM):
        base_ref[...] = bias_base(bias_ref[0, head : head + 1, :], seq)
        acc_ref[...] = jnp.zeros_like(acc_ref)
        for start in starts:
            query_block = head_part(query_ref, start, cols, head)
            grad_block = head_part(grad_ref, start, cols, head)
            scores = masked_scores(keys, query_block, base_ref, start, seq, cols, length)
            probs = jnp.exp(scores - total_ref[0, head : head + 1, start : start + cols])
            probs_grad = dot_nt(values, grad_block)
            mean_grad = jnp.sum(probs * probs_grad, axis=0, keepdims=True)
            score_grad = (probs * (probs_grad - mean_grad)).astype(jnp.bfloat16)
            value_acc = value_acc + dot_nn(probs.astype(jnp.bfloat16), grad_block)
            key_acc = key_acc + dot_nn(score_grad, query_block)
            query_parts[start, head] = dot_nn(
                keys_t[head * HEAD_DIM : (head + 1) * HEAD_DIM], score_grad
            )
            for first in range(0, seq, LANES):
                offset = seq - LANES - first + start
                acc_ref[:, offset : offset + cols] += score_grad[
                    first : first + LANES
                ].astype(jnp.float32)
        bias_grad_ref[0, head : head + 1, :] = diagonal_sums(acc_ref, seq)
    joined_grad_ref[:, LANES : 2 * LANES] = (key_acc * SCORE_SCALE).astype(jnp.bfloat16)
    joined_grad_ref[:, 2 * LANES :] = value_acc.astype(jnp.bfloat16)
    for start in starts:
        joined = jnp.concatenate(
            [query_parts[start, head] for head in range(LANES // HEAD_DIM)], axis=0
        )
        joined_grad_ref[start : start + cols, :LANES] = (joined * SCORE_SCALE).T.astype(
            jnp.bfloat16
        )


def attend_backward(length, joined, attended_grad, totals, bias_rows):
    seq, width = attended_grad.shape
    pairs = width // LANES
    heads = LANES // HEAD_DIM
    column = pl.BlockSpec((seq, LANES), lambda i: (0, i))
    triple = pl.BlockSpec((seq, 3 * LANES), lambda i: (0, i))
    vector = pl.BlockSpec((1, heads, 2 * seq), lambda i: (i, 0, 0))
    return pl.pallas_call(
        backward_kernel,
        grid=(pairs,),
        in_specs=[
            pl.BlockSpec(memory_space=pltpu.SMEM),
            triple,
            column,
            pl.BlockSpec((1, heads, seq), lambda i: (i, 0, 0)),
            vector,
        ],
        out_specs=[triple, vector],
        out_shape=[
            jax.ShapeDtypeStruct((seq, 3 * width), jnp.bfloat16),
            jax.ShapeDtypeStruct((pairs, heads, 2 * seq), jnp.float32),
        ],
        scratch_shapes=[
            pltpu.VMEM((LANES, 2 * seq), jnp.float32),
            pltpu.VMEM((LANES, 2 * seq), jnp.float32),
        ],
        cost_estimate=pl.CostEstimate(
            flops=40 * seq * seq * width,
            transcendentals=seq * seq * width // HEAD_DIM,
            bytes_accessed=14 * seq * width,
        ),
        name="attend_backward",
    )(length, joined, attended_grad, totals, bias_rows)


def assemble_kernel(place_ref, *refs):
    parts, (weight_ref, out_ref, gain_ref) = refs[:-3], refs[-3:]
    rows = weight_ref.shape[0] // len(parts)
    pairs = weight_ref.shape[1] // (3 * LANES)
    for index, part_ref in enumerate(parts):
        inner = index ^ place_ref[1]
        block = pl.ds(pl.multiple_of(inner * rows, rows), rows)
        for kind in range(3):
            for pair in range(pairs):
                first = (3 * pair + kind) * LANES
                weight_ref[block, first : first + LANES] = part_ref[
                    0, kind * rows : (kind + 1) * rows, pair * LANES : (pair + 1) * LANES
                ]
        out_ref[block, :] = part_ref[0, 3 * rows : 4 * rows, :]
        gain_ref[pl.ds(inner, 1)] = part_ref[:, 4 * rows :, :]


def assemble(place, parts):
    outer, block_rows, cols = parts[0].shape
    inner = len(parts)
    rows = (block_rows - GAIN_ROWS) // 4
    block = pl.BlockSpec((1, block_rows, cols), lambda i, place_ref: (i ^ place_ref[0], 0, 0))
    return pl.pallas_call(
        assemble_kernel,
        grid_spec=pltpu.PrefetchScalarGridSpec(
            num_scalar_prefetch=1,
            grid=(outer,),
            in_specs=[block] * inner,
            out_specs=[
                pl.BlockSpec((inner * rows, 3 * cols), lambda i, place_ref: (i, 0)),
                pl.BlockSpec((inner * rows, cols), lambda i, place_ref: (i, 0)),
                pl.BlockSpec((inner, GAIN_ROWS, cols), lambda i, place_ref: (i, 0, 0)),
            ],
        ),
        out_shape=[
            jax.ShapeDtypeStruct((outer * inner * rows, 3 * cols), jnp.bfloat16),
            jax.ShapeDtypeStruct((outer * inner * rows, cols), jnp.bfloat16),
            jax.ShapeDtypeStruct((outer * inner, GAIN_ROWS, cols), jnp.bfloat16),
        ],
        name="assemble",
    )(place, *parts)


def gelu_parts(gate_pre):
    inner = jnp.tanh(GELU_SCALE * (gate_pre + GELU_CUBIC * gate_pre * gate_pre * gate_pre))
    gelu = 0.5 * gate_pre * (1.0 + inner)
    slope = 0.5 * (1.0 + inner) + 0.5 * gate_pre * (1.0 - inner * inner) * GELU_SCALE * (
        1.0 + 3.0 * GELU_CUBIC * gate_pre * gate_pre
    )
    return gelu, slope


def expert_forward_kernel(
    side_ref, near_ref, far_ref, gate_near, up_near, gate_far, up_far, hidden_ref, slope_ref, gelu_ref
):
    near = near_ref[...]
    far = far_ref[...]
    gate_pre = dot_nn(near, gate_near[...]) + dot_nn(far, gate_far[...])
    up_pre = dot_nn(near, up_near[...]) + dot_nn(far, up_far[...])
    gelu, slope = gelu_parts(gate_pre)
    hidden_ref[...] = (gelu * up_pre).astype(jnp.bfloat16)
    slope_ref[...] = slope * up_pre
    gelu_ref[...] = gelu


def slot_block(slots):
    return 288 if slots % 288 == 0 else slots


def expert_forward(side, near, far, weights, hidden_cols):
    slots, half = near.shape
    rows = slot_block(slots)
    row_spec = pl.BlockSpec((rows, half), lambda i, side_ref: (i, 0))
    wide_spec = pl.BlockSpec((rows, hidden_cols), lambda i, side_ref: (i, 0))

    def weight_spec(other, column):
        return pl.BlockSpec(
            (half, hidden_cols),
            lambda i, side_ref: (side_ref[0] ^ other, column),
            pipeline_mode=pl.Buffered(1),
        )

    return pl.pallas_call(
        expert_forward_kernel,
        grid_spec=pltpu.PrefetchScalarGridSpec(
            num_scalar_prefetch=1,
            grid=(slots // rows,),
            in_specs=[
                row_spec,
                row_spec,
                weight_spec(0, 0),
                weight_spec(0, 1),
                weight_spec(1, 0),
                weight_spec(1, 1),
            ],
            out_specs=[wide_spec] * 3,
        ),
        out_shape=[
            jax.ShapeDtypeStruct((slots, hidden_cols), jnp.bfloat16),
            jax.ShapeDtypeStruct((slots, hidden_cols), jnp.float32),
            jax.ShapeDtypeStruct((slots, hidden_cols), jnp.float32),
        ],
        compiler_params=pltpu.CompilerParams(vmem_limit_bytes=VMEM_BYTES),
        cost_estimate=pl.CostEstimate(
            flops=8 * slots * half * hidden_cols,
            transcendentals=slots * hidden_cols,
            bytes_accessed=10 * slots * hidden_cols + 8 * half * hidden_cols,
        ),
        name="expert_forward",
    )(side, near, far, weights, weights, weights, weights)


def expert_backward_kernel(
    side_ref,
    near_ref,
    far_ref,
    slope_ref,
    gelu_ref,
    down_near,
    down_far,
    gate_near,
    up_near,
    gate_far,
    up_far,
    pre_grad_ref,
    stay_ref,
    away_ref,
):
    cols = slope_ref.shape[1]
    hidden_grad = dot_nn(near_ref[...], down_near[...]) + dot_nn(far_ref[...], down_far[...])
    gate_grad = (hidden_grad * slope_ref[...]).astype(jnp.bfloat16)
    up_grad = (hidden_grad * gelu_ref[...]).astype(jnp.bfloat16)
    pre_grad_ref[:, :cols] = gate_grad
    pre_grad_ref[:, cols:] = up_grad
    away_ref[...] = (dot_nt(gate_grad, gate_far[...]) + dot_nt(up_grad, up_far[...])).astype(
        jnp.bfloat16
    )
    stay_ref[...] = dot_nt(gate_grad, gate_near[...]) + dot_nt(up_grad, up_near[...])


def expert_backward(side, near, far, slope, gelu, down, weights):
    slots, half = near.shape
    hidden_cols = slope.shape[1]
    rows = slot_block(slots)
    row_spec = pl.BlockSpec((rows, half), lambda i, side_ref: (i, 0))
    wide_spec = pl.BlockSpec((rows, hidden_cols), lambda i, side_ref: (i, 0))

    def weight_spec(other, column):
        return pl.BlockSpec(
            (half, hidden_cols),
            lambda i, side_ref: (side_ref[0] ^ other, column),
            pipeline_mode=pl.Buffered(1),
        )

    return pl.pallas_call(
        expert_backward_kernel,
        grid_spec=pltpu.PrefetchScalarGridSpec(
            num_scalar_prefetch=1,
            grid=(slots // rows,),
            in_specs=[
                row_spec,
                row_spec,
                wide_spec,
                wide_spec,
                weight_spec(0, 0),
                weight_spec(1, 0),
                weight_spec(0, 0),
                weight_spec(0, 1),
                weight_spec(1, 0),
                weight_spec(1, 1),
            ],
            out_specs=[
                pl.BlockSpec((rows, 2 * hidden_cols), lambda i, side_ref: (i, 0)),
                row_spec,
                row_spec,
            ],
        ),
        out_shape=[
            jax.ShapeDtypeStruct((slots, 2 * hidden_cols), jnp.bfloat16),
            jax.ShapeDtypeStruct((slots, half), jnp.float32),
            jax.ShapeDtypeStruct((slots, half), jnp.bfloat16),
        ],
        compiler_params=pltpu.CompilerParams(vmem_limit_bytes=VMEM_BYTES),
        cost_estimate=pl.CostEstimate(
            flops=12 * slots * half * hidden_cols,
            transcendentals=0,
            bytes_accessed=12 * slots * hidden_cols + 12 * half * hidden_cols,
        ),
        name="expert_backward",
    )(side, near, far, slope, gelu, down, down, weights, weights, weights, weights)


def finish_kernel(place_ref, stay_ref, *refs):
    arrivals, small_ref, qkv_ref, out_ref, gain_ref, bias_ref = refs[:3], *refs[3:]
    kinds, rows, cols = qkv_ref.shape
    small_rows = small_ref.shape[0]
    total = stay_ref[...].astype(jnp.float32)
    small = small_ref[...]
    for arrival in arrivals:
        total = total + arrival[:rows].astype(jnp.float32)
        extra = arrival[rows : rows + 2 * small_rows].astype(jnp.float32)
        small = small + extra[:small_rows] + extra[small_rows:]
    for kind in range(kinds):
        for pair in range(cols // LANES):
            first = (kinds * pair + kind) * LANES
            qkv_ref[kind, :, pair * LANES : (pair + 1) * LANES] = total[:, first : first + LANES]
    out_ref[...] = total[:, kinds * cols :]
    width = small.shape[1] // 2
    gains = jnp.concatenate([small[:1, :width], small[:1, width:]], axis=0)
    gain_ref[...] = pltpu.roll(gains, width - place_ref[0] * rows, 1)[:, :rows]
    heads, buckets = bias_ref.shape
    for head in range(heads):
        bias_ref[head : head + 1, :] = small[1:2, head * buckets : (head + 1) * buckets]


def finish(place, stay, arrivals, small, cols, bias_shape):
    rows = stay.shape[0]
    whole = pl.BlockSpec(memory_space=pltpu.VMEM)
    return pl.pallas_call(
        finish_kernel,
        in_specs=[pl.BlockSpec(memory_space=pltpu.SMEM), *[whole] * 5],
        out_specs=[whole] * 4,
        out_shape=[
            jax.ShapeDtypeStruct((3, rows, cols), jnp.float32),
            jax.ShapeDtypeStruct((rows, cols), jnp.float32),
            jax.ShapeDtypeStruct((2, rows), jnp.float32),
            jax.ShapeDtypeStruct(bias_shape, jnp.float32),
        ],
        name="finish",
    )(place, stay, *arrivals, small)


def on_device(
    tokens,
    cotangent,
    lengths,
    bucket_table,
    routes,
    gate_values,
    qkv_weight,
    out_weight,
    norm_gains,
    rel_bias,
    gate_weight,
    up_weight,
    down_weight,
):
    tok_rows, width = tokens.shape
    half = width // 2
    dp_count = lax.axis_size("dp")
    tensor_count = lax.axis_size("tensor")
    seq = tok_rows * tensor_count
    expert_count, shard_rows, hidden_cols = gate_weight.shape
    head_cols = qkv_weight.shape[2]
    head_count, bucket_count = rel_bias.shape
    capacity = 9 * seq // 64
    group_size = dp_count // expert_count
    slot_count = (capacity + group_size - 1) // group_size
    total_slots = dp_count * slot_count
    dp_index = lax.axis_index("dp")
    tensor_index = lax.axis_index("tensor")
    first_tensor = tensor_index == 0
    length = lengths[dp_index]
    length_row = length[None]
    group_valid = jnp.arange(seq, dtype=jnp.int32) < length
    own_valid = lax.dynamic_slice_in_dim(group_valid, tensor_index * tok_rows, tok_rows, 0)
    own_valid = own_valid.astype(jnp.float32)[:, None]

    def swap(block):
        return lax.ppermute(block, "tensor", [(0, 1), (1, 0)])

    def partner(block, offset):
        return lax.ppermute(block, "dp", [(i, i ^ offset) for i in range(dp_count)])

    def chain(block, earlier):
        return lax.optimization_barrier((block, earlier))

    def ordered(own, other, axis):
        return jnp.where(
            first_tensor,
            jnp.concatenate([own, other], axis=axis),
            jnp.concatenate([other, own], axis=axis),
        )

    def own_part(block, axis):
        size = block.shape[axis] // 2
        return lax.dynamic_slice_in_dim(block, tensor_index * size, size, axis)

    def other_part(block, axis):
        size = block.shape[axis] // 2
        return lax.dynamic_slice_in_dim(block, (1 - tensor_index) * size, size, axis)

    def exchange(block):
        return lax.all_to_all(block, "dp", split_axis=0, concat_axis=0, tiled=True)

    def home_order(weight):
        return jnp.repeat(weight, group_size, axis=0)

    def fetch(weight):
        return exchange(home_order(weight)).reshape(dp_count * shard_rows, weight.shape[2])

    def send_grad(grad):
        return exchange(grad.reshape(dp_count, shard_rows, grad.shape[1]))

    def route(rows):
        arrived = exchange(rows.reshape(dp_count, slot_count, rows.shape[1]))
        return arrived.reshape(total_slots, rows.shape[1])

    spare = slot_count - shard_rows
    fold = shard_rows // spare

    def pack(rows):
        blocks = rows.reshape(dp_count, slot_count, half)
        tail = blocks[:, shard_rows:].reshape(dp_count, spare, fold, half // fold)
        tail = tail.transpose(0, 2, 1, 3).reshape(dp_count, shard_rows, half // fold)
        return jnp.concatenate([blocks[:, :shard_rows], tail], axis=2)

    def unpack(packed):
        tail = packed[:, :, half:].reshape(dp_count, fold, spare, half // fold)
        tail = tail.transpose(0, 2, 1, 3).reshape(dp_count, spare, half)
        return jnp.concatenate([packed[:, :, :half], tail], axis=1).reshape(total_slots, half)

    def regroup(arrived):
        return jnp.sum(
            arrived.astype(jnp.float32).reshape(
                expert_count, group_size, shard_rows, arrived.shape[2]
            ),
            axis=1,
        )

    gain_pad = jnp.pad(norm_gains, ((0, GAIN_ROWS - 2), (0, head_cols - shard_rows)))
    layer_shard = jnp.concatenate(
        [qkv_weight.reshape(3 * shard_rows, head_cols), out_weight, gain_pad], axis=0
    )
    pairs = head_cols // LANES
    pair_expert = routes.reshape(-1)
    pair_valid = jnp.repeat(group_valid, 2)
    chosen = (
        pair_expert[:, None] == jnp.arange(expert_count, dtype=jnp.int32)[None, :]
    ) & pair_valid[:, None]
    pair_index = jnp.arange(2 * seq, dtype=jnp.int32)
    before = (pair_index[:, None] > pair_index[None, :]).astype(jnp.bfloat16)
    earlier_pairs = dot_nn(before, chosen.astype(jnp.bfloat16))
    position = jnp.sum(jnp.where(chosen, earlier_pairs, 0.0), axis=1).astype(jnp.int32)
    kept_pair = pair_valid & (position < capacity)
    device = pair_expert * group_size + position // slot_count
    pair_slot = jnp.where(
        kept_pair, device * slot_count + position % slot_count, total_slots
    ).reshape(seq, 2)
    slot_index = jnp.arange(total_slots, dtype=jnp.int32)
    first_hit = pair_slot[:, 0][None, :] == slot_index[:, None]
    second_hit = pair_slot[:, 1][None, :] == slot_index[:, None]
    no_gate = jnp.zeros((), jnp.bfloat16)
    pick = (first_hit | second_hit).astype(jnp.bfloat16)
    pick_gate = jnp.where(
        first_hit,
        gate_values[:, 0][None, :],
        jnp.where(second_hit, gate_values[:, 1][None, :], no_gate),
    )

    mix_grad = lax.optimization_barrier(
        (own_valid * cotangent.astype(jnp.float32)).astype(jnp.bfloat16)
    )
    mix_away = other_part(mix_grad, 1)
    mix_other = swap(mix_away)
    tokens_other = swap(chain(tokens, mix_away)[0])
    out_grad_cols = dot_nn(
        pick_gate, ordered(own_part(mix_grad, 1), mix_other, 0)
    ).astype(jnp.bfloat16)
    residual, out_grad_cols = chain(tokens, out_grad_cols)
    gate_up = jnp.concatenate([home_order(gate_weight), home_order(up_weight)], axis=2)
    if dp_count == 16:
        across = [partner(layer_shard, 4 * k) for k in range(1, 4)]
        gate_up = chain(gate_up, across)[0]
        near = jnp.stack([layer_shard, *across])
        side = partner(near, 2)
        parts = [near, partner(near, 1), side, partner(side, 1)]
        place = jnp.stack([dp_index // 4, dp_index % 4])
        projection, out_all, gain_rows = assemble(place, parts)
    else:
        layer_all = lax.all_gather(layer_shard, "dp", axis=0, tiled=False)
        gate_up = chain(gate_up, layer_all)[0]
        projection = (
            layer_all[:, : 3 * shard_rows]
            .reshape(dp_count, 3, shard_rows, pairs, LANES)
            .transpose(0, 2, 3, 1, 4)
            .reshape(width, 3 * head_cols)
        )
        out_all = layer_all[:, 3 * shard_rows : 4 * shard_rows].reshape(width, head_cols)
        gain_rows = layer_all[:, 4 * shard_rows :]
    gate_up_all = exchange(gate_up).reshape(width, 2 * hidden_cols)

    distance = jnp.arange(2 * seq, dtype=jnp.int32)
    table_reversed = jnp.concatenate(
        [bucket_table[::-1], jnp.full((1,), bucket_count, jnp.int32)]
    )
    hot = (
        jnp.arange(bucket_count, dtype=jnp.int32)[:, None] == table_reversed[None, :]
    ).astype(jnp.float32)
    bias_rows = jnp.dot(rel_bias.astype(jnp.float32), hot, precision=HIGHEST).reshape(
        head_count // 2, 2, 2 * seq
    )
    gains_all = jnp.transpose(gain_rows[:, :2, :shard_rows], (1, 0, 2)).reshape(2, width)
    gain_one = gains_all[0].astype(jnp.float32)
    gain_two = gains_all[1].astype(jnp.float32)
    inputs_all = ordered(tokens, tokens_other, 0).astype(jnp.float32)
    scale_all = lax.rsqrt(jnp.mean(inputs_all * inputs_all, axis=-1, keepdims=True) + EPSILON)
    norm_one_all = (inputs_all * scale_all * gain_one).astype(jnp.bfloat16)
    joined = dot_nn(norm_one_all, projection).astype(jnp.bfloat16)
    attended, totals = attend_forward(length_row, joined, bias_rows)
    branch = dot_nt(attended, out_all)
    branch_other = swap(other_part(branch, 0).astype(jnp.bfloat16))
    inputs = residual.astype(jnp.float32)
    mid = inputs + own_valid * (own_part(branch, 0) + branch_other.astype(jnp.float32))
    mid_scale = lax.rsqrt(jnp.mean(mid * mid, axis=-1, keepdims=True) + EPSILON)
    norm_two = (mid * mid_scale * gain_two).astype(jnp.bfloat16)
    norm_two_cols = ordered(own_part(norm_two, 1), swap(other_part(norm_two, 1)), 0)
    slot_rows, gate_up_all = chain(
        jnp.concatenate(
            [dot_nn(pick, norm_two_cols).astype(jnp.bfloat16), out_grad_cols], axis=1
        ),
        gate_up_all,
    )
    down_late, slot_rows = chain(down_weight, route(slot_rows))
    down_all = fetch(down_late)
    expert_half = slot_rows[:, :half]
    expert_other = swap(expert_half)
    slot_grad_half = chain(slot_rows[:, half:], expert_other)[0]
    slot_grad_other = swap(slot_grad_half)

    side = tensor_index[None]
    hidden, slope, gelu = expert_forward(
        side, expert_half, expert_other, gate_up_all, hidden_cols
    )
    slot_grad = ordered(slot_grad_half, slot_grad_other, 1)
    down_grad, down_all = chain(dot_tn(slot_grad, hidden).astype(jnp.bfloat16), down_all)
    down_back = send_grad(down_grad)
    pre_grad, slot_back_stay, slot_back_away = expert_backward(
        side, slot_grad_half, slot_grad_other, slope, gelu, down_all, gate_up_all
    )
    hidden_late, slot_back_away = chain(hidden, slot_back_away)
    slot_back_other = swap(slot_back_away)
    expert_out_part = dot_nt(hidden_late, down_all)
    expert_out_away, slot_back_other = chain(
        other_part(expert_out_part, 1).astype(jnp.bfloat16), slot_back_other
    )
    slot_back_half = (
        slot_back_stay + slot_back_other.astype(jnp.float32)
    ).astype(jnp.bfloat16)
    expert_out_half = (
        own_part(expert_out_part, 1) + swap(expert_out_away).astype(jnp.float32)
    ).astype(jnp.bfloat16)
    slot_back_half, down_back = chain(slot_back_half, down_back)
    last, slot_back = chain(
        jnp.concatenate(
            [
                dot_tn(ordered(expert_half, expert_other, 1), pre_grad)
                .astype(jnp.bfloat16)
                .reshape(dp_count, shard_rows, 2 * hidden_cols),
                pack(expert_out_half),
            ],
            axis=2,
        ),
        route(slot_back_half),
    )
    arrived_back = exchange(last)

    back_cols = dot_tn(pick, slot_back)
    norm_two_grad = ordered(
        own_part(back_cols, 0), swap(other_part(back_cols, 0).astype(jnp.bfloat16)).astype(jnp.float32), 1
    )
    mid_unit = mid * mid_scale
    mid_inner = norm_two_grad * gain_two
    mid_grad = own_valid * cotangent.astype(jnp.float32) + mid_scale * (
        mid_inner - mid_unit * jnp.mean(mid_inner * mid_unit, axis=-1, keepdims=True)
    )
    gain_two_grad = jnp.sum(norm_two_grad * mid_unit, axis=0)
    branch_grad = (own_valid * mid_grad).astype(jnp.bfloat16)
    branch_grad_all = ordered(branch_grad, swap(branch_grad), 0)

    attended_grad = dot_nn(branch_grad_all, out_all).astype(jnp.bfloat16)
    joined_grad, bias_sums = attend_backward(
        length_row, joined, attended_grad, totals, bias_rows
    )
    bias_grad = jnp.dot(
        bias_sums.reshape(head_count, 2 * seq), hot.T, precision=HIGHEST
    )
    norm_one_part = dot_nt(joined_grad, projection)
    layer_part = jnp.concatenate(
        [
            dot_tn(norm_one_all, joined_grad).astype(jnp.bfloat16),
            dot_tn(branch_grad_all, attended).astype(jnp.bfloat16),
        ],
        axis=1,
    )
    gain_one_grad = jnp.sum(norm_one_part * (inputs_all * scale_all), axis=0)
    norm_one_grad = own_part(norm_one_part, 0) + swap(
        other_part(norm_one_part, 0).astype(jnp.bfloat16)
    ).astype(jnp.float32)
    scale = lax.rsqrt(jnp.mean(inputs * inputs, axis=-1, keepdims=True) + EPSILON)
    unit = inputs * scale
    inner = norm_one_grad * gain_one
    input_grad = mid_grad + scale * (
        inner - unit * jnp.mean(inner * unit, axis=-1, keepdims=True)
    )
    gain_part = jnp.concatenate([gain_one_grad, gain_two_grad]).reshape(-1, LANES)
    small = jnp.concatenate(
        [gain_part + swap(gain_part), bias_grad.reshape(-1, LANES)], axis=0
    )

    row_size = layer_part.shape[1]
    small = jnp.pad(small.reshape(-1), (0, -small.size % row_size)).reshape(-1, row_size)
    small_rows = small.shape[0]

    def with_small(block):
        high = lax.reduce_precision(small, 8, 7)
        rows = jnp.concatenate([high, small - high], axis=0).astype(jnp.bfloat16)
        rows = jnp.pad(rows, ((0, -rows.shape[0] % 8), (0, 0)))
        return jnp.concatenate([block, rows], axis=0)

    def small_of(block, first):
        rows = block[first : first + 2 * small_rows].astype(jnp.float32)
        return rows[:small_rows] + rows[small_rows:]

    if dp_count == 16:
        blocks = layer_part.reshape(dp_count, shard_rows, row_size)
        for step in (1, 2):
            pieces = blocks.reshape(-1, 2, shard_rows, row_size)
            bit = (dp_index // step) % 2
            away = lax.dynamic_index_in_dim(pieces, 1 - bit, 1, keepdims=False)
            stay = lax.dynamic_index_in_dim(pieces, bit, 1, keepdims=False)
            if step == 1:
                came = partner(away, step)
                small = small + partner(small, step)
            else:
                came = partner(with_small(away.reshape(-1, row_size)), step)
                came = chain(came, input_grad)[0]
                small = small + small_of(came, away.shape[0] * shard_rows)
                came = came[: away.shape[0] * shard_rows].reshape(away.shape)
            blocks = (stay.astype(jnp.float32) + came.astype(jnp.float32)).astype(jnp.bfloat16)
        outer = dp_index // 4
        leaving = [
            with_small(lax.dynamic_index_in_dim(blocks, outer ^ k, 0, keepdims=False))
            for k in range(1, 4)
        ]
        stay = lax.dynamic_index_in_dim(blocks, outer, 0, keepdims=False)
        arrived_back = chain(arrived_back, leaving)[0]
        came = [partner(piece, 4 * k) for k, piece in zip(range(1, 4), leaving, strict=True)]
    else:
        step = 1
        while step < dp_count:
            small = small + partner(small, step)
            step *= 2
    returned = unpack(arrived_back[:, :, 2 * hidden_cols :])
    mix_cols = dot_tn(pick_gate, returned)
    mix_away = other_part(mix_cols, 0).astype(jnp.bfloat16)
    mix_other = swap(mix_away)
    arrived_back = chain(arrived_back, mix_away)[0]
    gate_grad = regroup(arrived_back[:, :, :hidden_cols])
    up_grad = regroup(arrived_back[:, :, hidden_cols : 2 * hidden_cols])
    mix_own = ordered(own_part(mix_cols, 0), mix_other.astype(jnp.float32), 1)
    mixed = (mid + own_valid * mix_own).astype(jnp.bfloat16)
    if dp_count == 16:
        came = chain(came, (gate_grad, up_grad, mixed))[0]
        qkv_grad, out_grad, gains_grad, bias_out = finish(
            dp_index[None], stay, came, small, head_cols, bias_grad.shape
        )
    else:
        layer_grad = lax.psum_scatter(
            layer_part, "dp", scatter_dimension=0, tiled=True
        ).astype(jnp.float32)
        qkv_grad = (
            layer_grad[:, : 3 * head_cols]
            .reshape(shard_rows, pairs, 3, LANES)
            .transpose(2, 0, 1, 3)
            .reshape(3, shard_rows, head_cols)
        )
        out_grad = layer_grad[:, 3 * head_cols :]
        gain_sums = small[:1].reshape(2, width)
        gains_grad = lax.dynamic_slice_in_dim(gain_sums, dp_index * shard_rows, shard_rows, 1)
        bias_out = small[1, : head_count * bucket_count].reshape(head_count, bucket_count)
    return (
        mixed,
        input_grad,
        qkv_grad,
        out_grad,
        gains_grad,
        bias_out,
        gate_grad,
        up_grad,
        regroup(down_back),
    )


def solution(mesh):
    rows = P(("dp", "tensor"), None)
    shard = P("dp", "tensor")
    stacked = P(None, "dp", "tensor")
    return jax.shard_map(
        on_device,
        mesh=mesh,
        in_specs=(
            rows,
            rows,
            P(),
            P(),
            P("dp", None),
            P("dp", None),
            stacked,
            shard,
            P(None, "dp"),
            P("tensor", None),
            stacked,
            stacked,
            stacked,
        ),
        out_specs=(
            rows,
            rows,
            stacked,
            shard,
            P(None, "dp"),
            P("tensor", None),
            stacked,
            stacked,
            stacked,
        ),
        check_vma=False,
    )
```

```python
import jax
import jax.numpy as jnp
from jax import lax
from jax.experimental import pallas as pl
from jax.experimental.pallas import tpu as pltpu
from jax.sharding import PartitionSpec as P

HEAD_DIM = 64
EPSILON = 1e-06
MASKED_SCORE = -1e30
HIGHEST = lax.Precision.HIGHEST
SCORE_SCALE = 0.125
QUERY_COLS = 256
LANES = 128
GELU_SCALE = 0.7978845608028654
GELU_CUBIC = 0.044715
GAIN_ROWS = 8
VMEM_BYTES = 48 * 2**20


def dot_nt(left, right):
    return lax.dot_general(
        left, right, (((1,), (1,)), ((), ())), preferred_element_type=jnp.float32
    )


def dot_nn(left, right):
    return lax.dot_general(
        left, right, (((1,), (0,)), ((), ())), preferred_element_type=jnp.float32
    )


def dot_tn(left, right):
    return lax.dot_general(
        left, right, (((0,), (0,)), ((), ())), preferred_element_type=jnp.float32
    )


def bias_base(bias_row, seq):
    return pltpu.roll(
        jnp.broadcast_to(bias_row, (LANES, 2 * seq)),
        2 * seq - (LANES - 1),
        1,
        stride=1,
        stride_axis=0,
    )


def masked_scores(keys, query_block, base_ref, start, seq, cols, length):
    scores = dot_nt(keys, query_block) * SCORE_SCALE
    blocks = []
    for first in range(0, seq, LANES):
        offset = seq - LANES - first + start
        block = scores[first : first + LANES] + base_ref[:, offset : offset + cols]
        key_index = lax.broadcasted_iota(jnp.int32, block.shape, 0) + first
        blocks.append(jnp.where(key_index < length, block, MASKED_SCORE))
    return jnp.concatenate(blocks, axis=0)


def head_part(ref, start, cols, head):
    lane = lax.broadcasted_iota(jnp.int32, (cols, LANES), 1)
    return jnp.where(
        lane // HEAD_DIM == head, ref[start : start + cols, :], jnp.zeros((), jnp.bfloat16)
    )


def forward_kernel(length_ref, joined_ref, bias_ref, out_ref, total_ref, base_ref):
    query_ref, key_ref, value_ref = [
        joined_ref.at[:, i * LANES : (i + 1) * LANES] for i in range(3)
    ]
    seq = joined_ref.shape[0]
    cols = min(QUERY_COLS, seq)
    length = length_ref[0]
    values_t = value_ref[...].T
    keys = key_ref[...]
    starts = range(0, seq, cols)
    outs = {}
    for head in range(LANES // HEAD_DIM):
        base_ref[...] = bias_base(bias_ref[0, head : head + 1, :], seq)
        for start in starts:
            query_block = head_part(query_ref, start, cols, head)
            scores = masked_scores(keys, query_block, base_ref, start, seq, cols, length)
            top = jnp.max(scores, axis=0, keepdims=True)
            exponent = jnp.exp(scores - top)
            total = jnp.sum(exponent, axis=0, keepdims=True)
            probs = (exponent * (1.0 / total)).astype(jnp.bfloat16)
            total_ref[0, head : head + 1, start : start + cols] = top + jnp.log(total)
            outs[start, head] = dot_nn(
                values_t[head * HEAD_DIM : (head + 1) * HEAD_DIM], probs
            )
    for start in starts:
        joined = jnp.concatenate(
            [outs[start, head] for head in range(LANES // HEAD_DIM)], axis=0
        )
        out_ref[start : start + cols, :] = joined.T.astype(jnp.bfloat16)


def attend_forward(length, joined, bias_rows):
    seq = joined.shape[0]
    width = joined.shape[1] // 3
    pairs = width // LANES
    heads = LANES // HEAD_DIM
    column = pl.BlockSpec((seq, LANES), lambda i: (0, i))
    return pl.pallas_call(
        forward_kernel,
        grid=(pairs,),
        in_specs=[
            pl.BlockSpec(memory_space=pltpu.SMEM),
            pl.BlockSpec((seq, 3 * LANES), lambda i: (0, i)),
            pl.BlockSpec((1, heads, 2 * seq), lambda i: (i, 0, 0)),
        ],
        out_specs=[column, pl.BlockSpec((1, heads, seq), lambda i: (i, 0, 0))],
        out_shape=[
            jax.ShapeDtypeStruct((seq, width), jnp.bfloat16),
            jax.ShapeDtypeStruct((pairs, heads, seq), jnp.float32),
        ],
        scratch_shapes=[pltpu.VMEM((LANES, 2 * seq), jnp.float32)],
        cost_estimate=pl.CostEstimate(
            flops=16 * seq * seq * width,
            transcendentals=seq * seq * width // HEAD_DIM,
            bytes_accessed=8 * seq * width,
        ),
        name="attend_forward",
    )(length, joined, bias_rows)


def diagonal_sums(acc_ref, seq):
    period = 2 * seq
    folded = acc_ref[0:8, :]
    for first in range(8, LANES, 8):
        folded = folded + pltpu.roll(acc_ref[first : first + 8, :], period - first, 1)
    row = lax.broadcasted_iota(jnp.int32, folded.shape, 0)
    for bit in (1, 2, 4):
        folded = jnp.where((row & bit) != 0, pltpu.roll(folded, period - bit, 1), folded)
    return pltpu.roll(jnp.sum(folded, axis=0, keepdims=True), LANES - 1, 1)


def backward_kernel(
    length_ref,
    joined_ref,
    grad_ref,
    total_ref,
    bias_ref,
    joined_grad_ref,
    bias_grad_ref,
    base_ref,
    acc_ref,
):
    query_ref, key_ref, value_ref = [
        joined_ref.at[:, i * LANES : (i + 1) * LANES] for i in range(3)
    ]
    seq = joined_ref.shape[0]
    cols = min(QUERY_COLS, seq)
    length = length_ref[0]
    keys = key_ref[...]
    values = value_ref[...]
    keys_t = keys.T
    starts = range(0, seq, cols)
    key_acc = jnp.zeros((seq, LANES), jnp.float32)
    value_acc = jnp.zeros((seq, LANES), jnp.float32)
    query_parts = {}
    for head in range(LANES // HEAD_DIM):
        base_ref[...] = bias_base(bias_ref[0, head : head + 1, :], seq)
        acc_ref[...] = jnp.zeros_like(acc_ref)
        for start in starts:
            query_block = head_part(query_ref, start, cols, head)
            grad_block = head_part(grad_ref, start, cols, head)
            scores = masked_scores(keys, query_block, base_ref, start, seq, cols, length)
            probs = jnp.exp(scores - total_ref[0, head : head + 1, start : start + cols])
            probs_grad = dot_nt(values, grad_block)
            mean_grad = jnp.sum(probs * probs_grad, axis=0, keepdims=True)
            score_grad = (probs * (probs_grad - mean_grad)).astype(jnp.bfloat16)
            value_acc = value_acc + dot_nn(probs.astype(jnp.bfloat16), grad_block)
            key_acc = key_acc + dot_nn(score_grad, query_block)
            query_parts[start, head] = dot_nn(
                keys_t[head * HEAD_DIM : (head + 1) * HEAD_DIM], score_grad
            )
            for first in range(0, seq, LANES):
                offset = seq - LANES - first + start
                acc_ref[:, offset : offset + cols] += score_grad[
                    first : first + LANES
                ].astype(jnp.float32)
        bias_grad_ref[0, head : head + 1, :] = diagonal_sums(acc_ref, seq)
    joined_grad_ref[:, LANES : 2 * LANES] = (key_acc * SCORE_SCALE).astype(jnp.bfloat16)
    joined_grad_ref[:, 2 * LANES :] = value_acc.astype(jnp.bfloat16)
    for start in starts:
        joined = jnp.concatenate(
            [query_parts[start, head] for head in range(LANES // HEAD_DIM)], axis=0
        )
        joined_grad_ref[start : start + cols, :LANES] = (joined * SCORE_SCALE).T.astype(
            jnp.bfloat16
        )


def attend_backward(length, joined, attended_grad, totals, bias_rows):
    seq, width = attended_grad.shape
    pairs = width // LANES
    heads = LANES // HEAD_DIM
    column = pl.BlockSpec((seq, LANES), lambda i: (0, i))
    triple = pl.BlockSpec((seq, 3 * LANES), lambda i: (0, i))
    vector = pl.BlockSpec((1, heads, 2 * seq), lambda i: (i, 0, 0))
    return pl.pallas_call(
        backward_kernel,
        grid=(pairs,),
        in_specs=[
            pl.BlockSpec(memory_space=pltpu.SMEM),
            triple,
            column,
            pl.BlockSpec((1, heads, seq), lambda i: (i, 0, 0)),
            vector,
        ],
        out_specs=[triple, vector],
        out_shape=[
            jax.ShapeDtypeStruct((seq, 3 * width), jnp.bfloat16),
            jax.ShapeDtypeStruct((pairs, heads, 2 * seq), jnp.float32),
        ],
        scratch_shapes=[
            pltpu.VMEM((LANES, 2 * seq), jnp.float32),
            pltpu.VMEM((LANES, 2 * seq), jnp.float32),
        ],
        cost_estimate=pl.CostEstimate(
            flops=40 * seq * seq * width,
            transcendentals=seq * seq * width // HEAD_DIM,
            bytes_accessed=14 * seq * width,
        ),
        name="attend_backward",
    )(length, joined, attended_grad, totals, bias_rows)


def assemble_kernel(place_ref, *refs):
    parts, (weight_ref, out_ref, gain_ref) = refs[:-3], refs[-3:]
    rows = weight_ref.shape[0] // len(parts)
    pairs = weight_ref.shape[1] // (3 * LANES)
    for index, part_ref in enumerate(parts):
        inner = index ^ place_ref[1]
        block = pl.ds(pl.multiple_of(inner * rows, rows), rows)
        for kind in range(3):
            for pair in range(pairs):
                first = (3 * pair + kind) * LANES
                weight_ref[block, first : first + LANES] = part_ref[
                    0, kind * rows : (kind + 1) * rows, pair * LANES : (pair + 1) * LANES
                ]
        out_ref[block, :] = part_ref[0, 3 * rows : 4 * rows, :]
        gain_ref[pl.ds(inner, 1)] = part_ref[:, 4 * rows :, :]


def assemble(place, parts):
    outer, block_rows, cols = parts[0].shape
    inner = len(parts)
    rows = (block_rows - GAIN_ROWS) // 4
    block = pl.BlockSpec((1, block_rows, cols), lambda i, place_ref: (i ^ place_ref[0], 0, 0))
    return pl.pallas_call(
        assemble_kernel,
        grid_spec=pltpu.PrefetchScalarGridSpec(
            num_scalar_prefetch=1,
            grid=(outer,),
            in_specs=[block] * inner,
            out_specs=[
                pl.BlockSpec((inner * rows, 3 * cols), lambda i, place_ref: (i, 0)),
                pl.BlockSpec((inner * rows, cols), lambda i, place_ref: (i, 0)),
                pl.BlockSpec((inner, GAIN_ROWS, cols), lambda i, place_ref: (i, 0, 0)),
            ],
        ),
        out_shape=[
            jax.ShapeDtypeStruct((outer * inner * rows, 3 * cols), jnp.bfloat16),
            jax.ShapeDtypeStruct((outer * inner * rows, cols), jnp.bfloat16),
            jax.ShapeDtypeStruct((outer * inner, GAIN_ROWS, cols), jnp.bfloat16),
        ],
        name="assemble",
    )(place, *parts)


def gelu_parts(gate_pre):
    inner = jnp.tanh(GELU_SCALE * (gate_pre + GELU_CUBIC * gate_pre * gate_pre * gate_pre))
    gelu = 0.5 * gate_pre * (1.0 + inner)
    slope = 0.5 * (1.0 + inner) + 0.5 * gate_pre * (1.0 - inner * inner) * GELU_SCALE * (
        1.0 + 3.0 * GELU_CUBIC * gate_pre * gate_pre
    )
    return gelu, slope


def expert_forward_kernel(
    side_ref, near_ref, far_ref, gate_near, up_near, gate_far, up_far, hidden_ref, slope_ref, gelu_ref
):
    near = near_ref[...]
    far = far_ref[...]
    gate_pre = dot_nn(near, gate_near[...]) + dot_nn(far, gate_far[...])
    up_pre = dot_nn(near, up_near[...]) + dot_nn(far, up_far[...])
    gelu, slope = gelu_parts(gate_pre)
    hidden_ref[...] = (gelu * up_pre).astype(jnp.bfloat16)
    slope_ref[...] = slope * up_pre
    gelu_ref[...] = gelu


def slot_block(slots):
    return 288 if slots % 288 == 0 else slots


def expert_forward(side, near, far, weights, hidden_cols):
    slots, half = near.shape
    rows = slot_block(slots)
    row_spec = pl.BlockSpec((rows, half), lambda i, side_ref: (i, 0))
    wide_spec = pl.BlockSpec((rows, hidden_cols), lambda i, side_ref: (i, 0))

    def weight_spec(other, column):
        return pl.BlockSpec(
            (half, hidden_cols),
            lambda i, side_ref: (side_ref[0] ^ other, column),
            pipeline_mode=pl.Buffered(1),
        )

    return pl.pallas_call(
        expert_forward_kernel,
        grid_spec=pltpu.PrefetchScalarGridSpec(
            num_scalar_prefetch=1,
            grid=(slots // rows,),
            in_specs=[
                row_spec,
                row_spec,
                weight_spec(0, 0),
                weight_spec(0, 1),
                weight_spec(1, 0),
                weight_spec(1, 1),
            ],
            out_specs=[wide_spec] * 3,
        ),
        out_shape=[
            jax.ShapeDtypeStruct((slots, hidden_cols), jnp.bfloat16),
            jax.ShapeDtypeStruct((slots, hidden_cols), jnp.float32),
            jax.ShapeDtypeStruct((slots, hidden_cols), jnp.float32),
        ],
        compiler_params=pltpu.CompilerParams(vmem_limit_bytes=VMEM_BYTES),
        cost_estimate=pl.CostEstimate(
            flops=8 * slots * half * hidden_cols,
            transcendentals=slots * hidden_cols,
            bytes_accessed=10 * slots * hidden_cols + 8 * half * hidden_cols,
        ),
        name="expert_forward",
    )(side, near, far, weights, weights, weights, weights)


def expert_backward_kernel(
    side_ref,
    near_ref,
    far_ref,
    slope_ref,
    gelu_ref,
    down_near,
    down_far,
    gate_near,
    up_near,
    gate_far,
    up_far,
    pre_grad_ref,
    stay_ref,
    away_ref,
):
    cols = slope_ref.shape[1]
    hidden_grad = dot_nn(near_ref[...], down_near[...]) + dot_nn(far_ref[...], down_far[...])
    gate_grad = (hidden_grad * slope_ref[...]).astype(jnp.bfloat16)
    up_grad = (hidden_grad * gelu_ref[...]).astype(jnp.bfloat16)
    pre_grad_ref[:, :cols] = gate_grad
    pre_grad_ref[:, cols:] = up_grad
    away_ref[...] = (dot_nt(gate_grad, gate_far[...]) + dot_nt(up_grad, up_far[...])).astype(
        jnp.bfloat16
    )
    stay_ref[...] = dot_nt(gate_grad, gate_near[...]) + dot_nt(up_grad, up_near[...])


def expert_backward(side, near, far, slope, gelu, down, weights):
    slots, half = near.shape
    hidden_cols = slope.shape[1]
    rows = slot_block(slots)
    row_spec = pl.BlockSpec((rows, half), lambda i, side_ref: (i, 0))
    wide_spec = pl.BlockSpec((rows, hidden_cols), lambda i, side_ref: (i, 0))

    def weight_spec(other, column):
        return pl.BlockSpec(
            (half, hidden_cols),
            lambda i, side_ref: (side_ref[0] ^ other, column),
            pipeline_mode=pl.Buffered(1),
        )

    return pl.pallas_call(
        expert_backward_kernel,
        grid_spec=pltpu.PrefetchScalarGridSpec(
            num_scalar_prefetch=1,
            grid=(slots // rows,),
            in_specs=[
                row_spec,
                row_spec,
                wide_spec,
                wide_spec,
                weight_spec(0, 0),
                weight_spec(1, 0),
                weight_spec(0, 0),
                weight_spec(0, 1),
                weight_spec(1, 0),
                weight_spec(1, 1),
            ],
            out_specs=[
                pl.BlockSpec((rows, 2 * hidden_cols), lambda i, side_ref: (i, 0)),
                row_spec,
                row_spec,
            ],
        ),
        out_shape=[
            jax.ShapeDtypeStruct((slots, 2 * hidden_cols), jnp.bfloat16),
            jax.ShapeDtypeStruct((slots, half), jnp.float32),
            jax.ShapeDtypeStruct((slots, half), jnp.bfloat16),
        ],
        compiler_params=pltpu.CompilerParams(vmem_limit_bytes=VMEM_BYTES),
        cost_estimate=pl.CostEstimate(
            flops=12 * slots * half * hidden_cols,
            transcendentals=0,
            bytes_accessed=12 * slots * hidden_cols + 12 * half * hidden_cols,
        ),
        name="expert_backward",
    )(side, near, far, slope, gelu, down, down, weights, weights, weights, weights)


def finish_kernel(place_ref, stay_ref, *refs):
    arrivals, small_ref, qkv_ref, out_ref, gain_ref, bias_ref = refs[:3], *refs[3:]
    kinds, rows, cols = qkv_ref.shape
    small_rows = small_ref.shape[0]
    total = stay_ref[...].astype(jnp.float32)
    small = small_ref[...]
    for arrival in arrivals:
        total = total + arrival[:rows].astype(jnp.float32)
        extra = arrival[rows : rows + 2 * small_rows].astype(jnp.float32)
        small = small + extra[:small_rows] + extra[small_rows:]
    for kind in range(kinds):
        for pair in range(cols // LANES):
            first = (kinds * pair + kind) * LANES
            qkv_ref[kind, :, pair * LANES : (pair + 1) * LANES] = total[:, first : first + LANES]
    out_ref[...] = total[:, kinds * cols :]
    width = small.shape[1] // 2
    gains = jnp.concatenate([small[:1, :width], small[:1, width:]], axis=0)
    shift = lax.rem(width - place_ref[0] * rows, width)
    gain_ref[...] = pltpu.roll(gains, shift, 1)[:, :rows]
    heads, buckets = bias_ref.shape
    for head in range(heads):
        bias_ref[head : head + 1, :] = small[1:2, head * buckets : (head + 1) * buckets]


def finish(place, stay, arrivals, small, cols, bias_shape):
    rows = stay.shape[0]
    whole = pl.BlockSpec(memory_space=pltpu.VMEM)
    return pl.pallas_call(
        finish_kernel,
        in_specs=[pl.BlockSpec(memory_space=pltpu.SMEM), *[whole] * 5],
        out_specs=[whole] * 4,
        out_shape=[
            jax.ShapeDtypeStruct((3, rows, cols), jnp.float32),
            jax.ShapeDtypeStruct((rows, cols), jnp.float32),
            jax.ShapeDtypeStruct((2, rows), jnp.float32),
            jax.ShapeDtypeStruct(bias_shape, jnp.float32),
        ],
        name="finish",
    )(place, stay, *arrivals, small)


def on_device(
    tokens,
    cotangent,
    lengths,
    bucket_table,
    routes,
    gate_values,
    qkv_weight,
    out_weight,
    norm_gains,
    rel_bias,
    gate_weight,
    up_weight,
    down_weight,
):
    tok_rows, width = tokens.shape
    half = width // 2
    dp_count = lax.axis_size("dp")
    tensor_count = lax.axis_size("tensor")
    seq = tok_rows * tensor_count
    expert_count, shard_rows, hidden_cols = gate_weight.shape
    head_cols = qkv_weight.shape[2]
    head_count, bucket_count = rel_bias.shape
    capacity = 9 * seq // 64
    group_size = dp_count // expert_count
    slot_count = (capacity + group_size - 1) // group_size
    total_slots = dp_count * slot_count
    dp_index = lax.axis_index("dp")
    tensor_index = lax.axis_index("tensor")
    first_tensor = tensor_index == 0
    length = lengths[dp_index]
    length_row = length[None]
    group_valid = jnp.arange(seq, dtype=jnp.int32) < length
    own_valid = lax.dynamic_slice_in_dim(group_valid, tensor_index * tok_rows, tok_rows, 0)
    own_valid = own_valid.astype(jnp.float32)[:, None]

    def swap(block):
        return lax.ppermute(block, "tensor", [(0, 1), (1, 0)])

    def partner(block, offset):
        return lax.ppermute(block, "dp", [(i, i ^ offset) for i in range(dp_count)])

    def chain(block, earlier):
        return lax.optimization_barrier((block, earlier))

    def ordered(own, other, axis):
        return jnp.where(
            first_tensor,
            jnp.concatenate([own, other], axis=axis),
            jnp.concatenate([other, own], axis=axis),
        )

    def own_part(block, axis):
        size = block.shape[axis] // 2
        return lax.dynamic_slice_in_dim(block, tensor_index * size, size, axis)

    def other_part(block, axis):
        size = block.shape[axis] // 2
        return lax.dynamic_slice_in_dim(block, (1 - tensor_index) * size, size, axis)

    def exchange(block):
        return lax.all_to_all(block, "dp", split_axis=0, concat_axis=0, tiled=True)

    def home_order(weight):
        return jnp.repeat(weight, group_size, axis=0)

    def fetch(weight):
        return exchange(home_order(weight)).reshape(dp_count * shard_rows, weight.shape[2])

    def send_grad(grad):
        return exchange(grad.reshape(dp_count, shard_rows, grad.shape[1]))

    def route(rows):
        arrived = exchange(rows.reshape(dp_count, slot_count, rows.shape[1]))
        return arrived.reshape(total_slots, rows.shape[1])

    spare = slot_count - shard_rows
    fold = shard_rows // spare

    def pack(rows):
        blocks = rows.reshape(dp_count, slot_count, half)
        tail = blocks[:, shard_rows:].reshape(dp_count, spare, fold, half // fold)
        tail = tail.transpose(0, 2, 1, 3).reshape(dp_count, shard_rows, half // fold)
        return jnp.concatenate([blocks[:, :shard_rows], tail], axis=2)

    def unpack(packed):
        tail = packed[:, :, half:].reshape(dp_count, fold, spare, half // fold)
        tail = tail.transpose(0, 2, 1, 3).reshape(dp_count, spare, half)
        return jnp.concatenate([packed[:, :, :half], tail], axis=1).reshape(total_slots, half)

    def regroup(arrived):
        return jnp.sum(
            arrived.astype(jnp.float32).reshape(
                expert_count, group_size, shard_rows, arrived.shape[2]
            ),
            axis=1,
        )

    gain_pad = jnp.pad(norm_gains, ((0, GAIN_ROWS - 2), (0, head_cols - shard_rows)))
    layer_shard = jnp.concatenate(
        [qkv_weight.reshape(3 * shard_rows, head_cols), out_weight, gain_pad], axis=0
    )
    pairs = head_cols // LANES
    pair_expert = routes.reshape(-1)
    pair_valid = jnp.repeat(group_valid, 2)
    chosen = (
        pair_expert[:, None] == jnp.arange(expert_count, dtype=jnp.int32)[None, :]
    ) & pair_valid[:, None]
    pair_index = jnp.arange(2 * seq, dtype=jnp.int32)
    before = (pair_index[:, None] > pair_index[None, :]).astype(jnp.bfloat16)
    earlier_pairs = dot_nn(before, chosen.astype(jnp.bfloat16))
    position = jnp.sum(jnp.where(chosen, earlier_pairs, 0.0), axis=1).astype(jnp.int32)
    kept_pair = pair_valid & (position < capacity)
    device = pair_expert * group_size + position // slot_count
    pair_slot = jnp.where(
        kept_pair, device * slot_count + position % slot_count, total_slots
    ).reshape(seq, 2)
    slot_index = jnp.arange(total_slots, dtype=jnp.int32)
    first_hit = pair_slot[:, 0][None, :] == slot_index[:, None]
    second_hit = pair_slot[:, 1][None, :] == slot_index[:, None]
    no_gate = jnp.zeros((), jnp.bfloat16)
    pick = (first_hit | second_hit).astype(jnp.bfloat16)
    pick_gate = jnp.where(
        first_hit,
        gate_values[:, 0][None, :],
        jnp.where(second_hit, gate_values[:, 1][None, :], no_gate),
    )

    mix_grad = lax.optimization_barrier(
        (own_valid * cotangent.astype(jnp.float32)).astype(jnp.bfloat16)
    )
    mix_away = other_part(mix_grad, 1)
    mix_other = swap(mix_away)
    tokens_other = swap(chain(tokens, mix_away)[0])
    out_grad_cols = dot_nn(
        pick_gate, ordered(own_part(mix_grad, 1), mix_other, 0)
    ).astype(jnp.bfloat16)
    residual, out_grad_cols = chain(tokens, out_grad_cols)
    gate_up = jnp.concatenate([home_order(gate_weight), home_order(up_weight)], axis=2)
    if dp_count == 16:
        across = [partner(layer_shard, 4 * k) for k in range(1, 4)]
        gate_up = chain(gate_up, across)[0]
        near = jnp.stack([layer_shard, *across])
        side = partner(near, 2)
        parts = [near, partner(near, 1), side, partner(side, 1)]
        place = jnp.stack([dp_index // 4, dp_index % 4])
        projection, out_all, gain_rows = assemble(place, parts)
    else:
        layer_all = lax.all_gather(layer_shard, "dp", axis=0, tiled=False)
        gate_up = chain(gate_up, layer_all)[0]
        projection = (
            layer_all[:, : 3 * shard_rows]
            .reshape(dp_count, 3, shard_rows, pairs, LANES)
            .transpose(0, 2, 3, 1, 4)
            .reshape(width, 3 * head_cols)
        )
        out_all = layer_all[:, 3 * shard_rows : 4 * shard_rows].reshape(width, head_cols)
        gain_rows = layer_all[:, 4 * shard_rows :]
    gate_up_all = exchange(gate_up).reshape(width, 2 * hidden_cols)

    distance = jnp.arange(2 * seq, dtype=jnp.int32)
    table_reversed = jnp.concatenate(
        [bucket_table[::-1], jnp.full((1,), bucket_count, jnp.int32)]
    )
    hot = (
        jnp.arange(bucket_count, dtype=jnp.int32)[:, None] == table_reversed[None, :]
    ).astype(jnp.float32)
    bias_rows = jnp.dot(rel_bias.astype(jnp.float32), hot, precision=HIGHEST).reshape(
        head_count // 2, 2, 2 * seq
    )
    gains_all = jnp.transpose(gain_rows[:, :2, :shard_rows], (1, 0, 2)).reshape(2, width)
    gain_one = gains_all[0].astype(jnp.float32)
    gain_two = gains_all[1].astype(jnp.float32)
    inputs_all = ordered(tokens, tokens_other, 0).astype(jnp.float32)
    scale_all = lax.rsqrt(jnp.mean(inputs_all * inputs_all, axis=-1, keepdims=True) + EPSILON)
    norm_one_all = (inputs_all * scale_all * gain_one).astype(jnp.bfloat16)
    joined = dot_nn(norm_one_all, projection).astype(jnp.bfloat16)
    attended, totals = attend_forward(length_row, joined, bias_rows)
    branch = dot_nt(attended, out_all)
    branch_other = swap(other_part(branch, 0).astype(jnp.bfloat16))
    inputs = residual.astype(jnp.float32)
    mid = inputs + own_valid * (own_part(branch, 0) + branch_other.astype(jnp.float32))
    mid_scale = lax.rsqrt(jnp.mean(mid * mid, axis=-1, keepdims=True) + EPSILON)
    norm_two = (mid * mid_scale * gain_two).astype(jnp.bfloat16)
    norm_two_cols = ordered(own_part(norm_two, 1), swap(other_part(norm_two, 1)), 0)
    slot_rows, gate_up_all = chain(
        jnp.concatenate(
            [dot_nn(pick, norm_two_cols).astype(jnp.bfloat16), out_grad_cols], axis=1
        ),
        gate_up_all,
    )
    down_late, slot_rows = chain(down_weight, route(slot_rows))
    down_all = fetch(down_late)
    expert_half = slot_rows[:, :half]
    expert_other = swap(expert_half)
    slot_grad_half = chain(slot_rows[:, half:], expert_other)[0]
    slot_grad_other = swap(slot_grad_half)

    side = tensor_index[None]
    hidden, slope, gelu = expert_forward(
        side, expert_half, expert_other, gate_up_all, hidden_cols
    )
    slot_grad = ordered(slot_grad_half, slot_grad_other, 1)
    down_grad, down_all = chain(dot_tn(slot_grad, hidden).astype(jnp.bfloat16), down_all)
    down_back = send_grad(down_grad)
    pre_grad, slot_back_stay, slot_back_away = expert_backward(
        side, slot_grad_half, slot_grad_other, slope, gelu, down_all, gate_up_all
    )
    hidden_late, slot_back_away = chain(hidden, slot_back_away)
    slot_back_other = swap(slot_back_away)
    expert_out_part = dot_nt(hidden_late, down_all)
    expert_out_away, slot_back_other = chain(
        other_part(expert_out_part, 1).astype(jnp.bfloat16), slot_back_other
    )
    slot_back_half = (
        slot_back_stay + slot_back_other.astype(jnp.float32)
    ).astype(jnp.bfloat16)
    expert_out_half = (
        own_part(expert_out_part, 1) + swap(expert_out_away).astype(jnp.float32)
    ).astype(jnp.bfloat16)
    slot_back_half, down_back = chain(slot_back_half, down_back)
    last, slot_back = chain(
        jnp.concatenate(
            [
                dot_tn(ordered(expert_half, expert_other, 1), pre_grad)
                .astype(jnp.bfloat16)
                .reshape(dp_count, shard_rows, 2 * hidden_cols),
                pack(expert_out_half),
            ],
            axis=2,
        ),
        route(slot_back_half),
    )
    arrived_back = exchange(last)

    back_cols = dot_tn(pick, slot_back)
    norm_two_grad = ordered(
        own_part(back_cols, 0), swap(other_part(back_cols, 0).astype(jnp.bfloat16)).astype(jnp.float32), 1
    )
    mid_unit = mid * mid_scale
    mid_inner = norm_two_grad * gain_two
    mid_grad = own_valid * cotangent.astype(jnp.float32) + mid_scale * (
        mid_inner - mid_unit * jnp.mean(mid_inner * mid_unit, axis=-1, keepdims=True)
    )
    gain_two_grad = jnp.sum(norm_two_grad * mid_unit, axis=0)
    branch_grad = (own_valid * mid_grad).astype(jnp.bfloat16)
    branch_grad_all = ordered(branch_grad, swap(branch_grad), 0)

    attended_grad = dot_nn(branch_grad_all, out_all).astype(jnp.bfloat16)
    joined_grad, bias_sums = attend_backward(
        length_row, joined, attended_grad, totals, bias_rows
    )
    bias_grad = jnp.dot(
        bias_sums.reshape(head_count, 2 * seq), hot.T, precision=HIGHEST
    )
    norm_one_part = dot_nt(joined_grad, projection)
    layer_part = jnp.concatenate(
        [
            dot_tn(norm_one_all, joined_grad).astype(jnp.bfloat16),
            dot_tn(branch_grad_all, attended).astype(jnp.bfloat16),
        ],
        axis=1,
    )
    gain_one_grad = jnp.sum(norm_one_part * (inputs_all * scale_all), axis=0)
    norm_one_grad = own_part(norm_one_part, 0) + swap(
        other_part(norm_one_part, 0).astype(jnp.bfloat16)
    ).astype(jnp.float32)
    scale = lax.rsqrt(jnp.mean(inputs * inputs, axis=-1, keepdims=True) + EPSILON)
    unit = inputs * scale
    inner = norm_one_grad * gain_one
    input_grad = mid_grad + scale * (
        inner - unit * jnp.mean(inner * unit, axis=-1, keepdims=True)
    )
    gain_part = jnp.concatenate([gain_one_grad, gain_two_grad]).reshape(-1, LANES)
    small = jnp.concatenate(
        [gain_part + swap(gain_part), bias_grad.reshape(-1, LANES)], axis=0
    )

    row_size = layer_part.shape[1]
    small = jnp.pad(small.reshape(-1), (0, -small.size % row_size)).reshape(-1, row_size)
    small_rows = small.shape[0]

    def with_small(block):
        high = lax.reduce_precision(small, 8, 7)
        rows = jnp.concatenate([high, small - high], axis=0).astype(jnp.bfloat16)
        rows = jnp.pad(rows, ((0, -rows.shape[0] % 8), (0, 0)))
        return jnp.concatenate([block, rows], axis=0)

    def small_of(block, first):
        rows = block[first : first + 2 * small_rows].astype(jnp.float32)
        return rows[:small_rows] + rows[small_rows:]

    if dp_count == 16:
        blocks = layer_part.reshape(dp_count, shard_rows, row_size)
        for step in (1, 2):
            pieces = blocks.reshape(-1, 2, shard_rows, row_size)
            bit = (dp_index // step) % 2
            away = lax.dynamic_index_in_dim(pieces, 1 - bit, 1, keepdims=False)
            stay = lax.dynamic_index_in_dim(pieces, bit, 1, keepdims=False)
            if step == 1:
                came = partner(away, step)
                small = small + partner(small, step)
            else:
                down_out = regroup(down_back)
                ready = with_small(away.reshape(-1, row_size))
                came = partner(chain(ready, (down_out, input_grad))[0], step)
                small = small + small_of(came, away.shape[0] * shard_rows)
                came = came[: away.shape[0] * shard_rows].reshape(away.shape)
            blocks = (stay.astype(jnp.float32) + came.astype(jnp.float32)).astype(jnp.bfloat16)
        outer = dp_index // 4
        leaving = [
            with_small(lax.dynamic_index_in_dim(blocks, outer ^ k, 0, keepdims=False))
            for k in range(1, 4)
        ]
        stay = lax.dynamic_index_in_dim(blocks, outer, 0, keepdims=False)
        arrived_back = chain(arrived_back, leaving)[0]
        came = [partner(piece, 4 * k) for k, piece in zip(range(1, 4), leaving, strict=True)]
    else:
        step = 1
        while step < dp_count:
            small = small + partner(small, step)
            step *= 2
    returned = unpack(arrived_back[:, :, 2 * hidden_cols :])
    mix_cols = dot_tn(pick_gate, returned)
    mix_away = other_part(mix_cols, 0).astype(jnp.bfloat16)
    mix_other = swap(mix_away)
    arrived_back = chain(arrived_back, mix_away)[0]
    gate_grad = regroup(arrived_back[:, :, :hidden_cols])
    up_grad = regroup(arrived_back[:, :, hidden_cols : 2 * hidden_cols])
    mix_own = ordered(own_part(mix_cols, 0), mix_other.astype(jnp.float32), 1)
    mixed = (mid + own_valid * mix_own).astype(jnp.bfloat16)
    if dp_count == 16:
        came = chain(came, (gate_grad, up_grad, mixed))[0]
        qkv_grad, out_grad, gains_grad, bias_out = finish(
            dp_index[None], stay, came, small, head_cols, bias_grad.shape
        )
    else:
        layer_grad = lax.psum_scatter(
            layer_part, "dp", scatter_dimension=0, tiled=True
        ).astype(jnp.float32)
        qkv_grad = (
            layer_grad[:, : 3 * head_cols]
            .reshape(shard_rows, pairs, 3, LANES)
            .transpose(2, 0, 1, 3)
            .reshape(3, shard_rows, head_cols)
        )
        out_grad = layer_grad[:, 3 * head_cols :]
        gain_sums = small[:1].reshape(2, width)
        gains_grad = lax.dynamic_slice_in_dim(gain_sums, dp_index * shard_rows, shard_rows, 1)
        bias_out = small[1, : head_count * bucket_count].reshape(head_count, bucket_count)
    return (
        mixed,
        input_grad,
        qkv_grad,
        out_grad,
        gains_grad,
        bias_out,
        gate_grad,
        up_grad,
        down_out if dp_count == 16 else regroup(down_back),
    )


def solution(mesh):
    rows = P(("dp", "tensor"), None)
    shard = P("dp", "tensor")
    stacked = P(None, "dp", "tensor")
    return jax.shard_map(
        on_device,
        mesh=mesh,
        in_specs=(
            rows,
            rows,
            P(),
            P(),
            P("dp", None),
            P("dp", None),
            stacked,
            shard,
            P(None, "dp"),
            P("tensor", None),
            stacked,
            stacked,
            stacked,
        ),
        out_specs=(
            rows,
            rows,
            stacked,
            shard,
            P(None, "dp"),
            P("tensor", None),
            stacked,
            stacked,
            stacked,
        ),
        check_vma=False,
    )
```

```python
import jax
import jax.numpy as jnp
from jax import lax
from jax.experimental import pallas as pl
from jax.experimental.pallas import tpu as pltpu
from jax.sharding import PartitionSpec as P

HEAD_DIM = 64
EPSILON = 1e-06
MASKED_SCORE = -1e30
HIGHEST = lax.Precision.HIGHEST
SCORE_SCALE = 0.125
QUERY_COLS = 256
LANES = 128
GELU_SCALE = 0.7978845608028654
GELU_CUBIC = 0.044715
GAIN_ROWS = 8
VMEM_BYTES = 48 * 2**20


def dot_nt(left, right):
    return lax.dot_general(
        left, right, (((1,), (1,)), ((), ())), preferred_element_type=jnp.float32
    )


def dot_nn(left, right):
    return lax.dot_general(
        left, right, (((1,), (0,)), ((), ())), preferred_element_type=jnp.float32
    )


def dot_tn(left, right):
    return lax.dot_general(
        left, right, (((0,), (0,)), ((), ())), preferred_element_type=jnp.float32
    )


def bias_base(bias_row, seq):
    return pltpu.roll(
        jnp.broadcast_to(bias_row, (LANES, 2 * seq)),
        2 * seq - (LANES - 1),
        1,
        stride=1,
        stride_axis=0,
    )


def masked_scores(keys, query_block, base_ref, start, seq, cols, length):
    scores = dot_nt(keys, query_block) * SCORE_SCALE
    blocks = []
    for first in range(0, seq, LANES):
        offset = seq - LANES - first + start
        block = scores[first : first + LANES] + base_ref[:, offset : offset + cols]
        key_index = lax.broadcasted_iota(jnp.int32, block.shape, 0) + first
        blocks.append(jnp.where(key_index < length, block, MASKED_SCORE))
    return jnp.concatenate(blocks, axis=0)


def head_part(ref, start, cols, head):
    lane = lax.broadcasted_iota(jnp.int32, (cols, LANES), 1)
    return jnp.where(
        lane // HEAD_DIM == head, ref[start : start + cols, :], jnp.zeros((), jnp.bfloat16)
    )


def forward_kernel(length_ref, joined_ref, bias_ref, out_ref, total_ref, base_ref):
    query_ref, key_ref, value_ref = [
        joined_ref.at[:, i * LANES : (i + 1) * LANES] for i in range(3)
    ]
    seq = joined_ref.shape[0]
    cols = min(QUERY_COLS, seq)
    length = length_ref[0]
    values_t = value_ref[...].T
    keys = key_ref[...]
    starts = range(0, seq, cols)
    outs = {}
    for head in range(LANES // HEAD_DIM):
        base_ref[...] = bias_base(bias_ref[0, head : head + 1, :], seq)
        for start in starts:
            query_block = head_part(query_ref, start, cols, head)
            scores = masked_scores(keys, query_block, base_ref, start, seq, cols, length)
            top = jnp.max(scores, axis=0, keepdims=True)
            exponent = jnp.exp(scores - top)
            total = jnp.sum(exponent, axis=0, keepdims=True)
            probs = (exponent * (1.0 / total)).astype(jnp.bfloat16)
            total_ref[0, head : head + 1, start : start + cols] = top + jnp.log(total)
            outs[start, head] = dot_nn(
                values_t[head * HEAD_DIM : (head + 1) * HEAD_DIM], probs
            )
    for start in starts:
        joined = jnp.concatenate(
            [outs[start, head] for head in range(LANES // HEAD_DIM)], axis=0
        )
        out_ref[start : start + cols, :] = joined.T.astype(jnp.bfloat16)


def attend_forward(length, joined, bias_rows):
    seq = joined.shape[0]
    width = joined.shape[1] // 3
    pairs = width // LANES
    heads = LANES // HEAD_DIM
    column = pl.BlockSpec((seq, LANES), lambda i: (0, i))
    return pl.pallas_call(
        forward_kernel,
        grid=(pairs,),
        in_specs=[
            pl.BlockSpec(memory_space=pltpu.SMEM),
            pl.BlockSpec((seq, 3 * LANES), lambda i: (0, i)),
            pl.BlockSpec((1, heads, 2 * seq), lambda i: (i, 0, 0)),
        ],
        out_specs=[column, pl.BlockSpec((1, heads, seq), lambda i: (i, 0, 0))],
        out_shape=[
            jax.ShapeDtypeStruct((seq, width), jnp.bfloat16),
            jax.ShapeDtypeStruct((pairs, heads, seq), jnp.float32),
        ],
        scratch_shapes=[pltpu.VMEM((LANES, 2 * seq), jnp.float32)],
        cost_estimate=pl.CostEstimate(
            flops=16 * seq * seq * width,
            transcendentals=seq * seq * width // HEAD_DIM,
            bytes_accessed=8 * seq * width,
        ),
        name="attend_forward",
    )(length, joined, bias_rows)


def diagonal_sums(acc_ref, seq):
    period = 2 * seq
    folded = acc_ref[0:8, :]
    for first in range(8, LANES, 8):
        folded = folded + pltpu.roll(acc_ref[first : first + 8, :], period - first, 1)
    row = lax.broadcasted_iota(jnp.int32, folded.shape, 0)
    for bit in (1, 2, 4):
        folded = jnp.where((row & bit) != 0, pltpu.roll(folded, period - bit, 1), folded)
    return pltpu.roll(jnp.sum(folded, axis=0, keepdims=True), LANES - 1, 1)


def backward_kernel(
    length_ref,
    joined_ref,
    grad_ref,
    total_ref,
    bias_ref,
    joined_grad_ref,
    bias_grad_ref,
    base_ref,
    acc_ref,
):
    query_ref, key_ref, value_ref = [
        joined_ref.at[:, i * LANES : (i + 1) * LANES] for i in range(3)
    ]
    seq = joined_ref.shape[0]
    cols = min(QUERY_COLS, seq)
    length = length_ref[0]
    keys = key_ref[...]
    values = value_ref[...]
    keys_t = keys.T
    starts = range(0, seq, cols)
    key_acc = jnp.zeros((seq, LANES), jnp.float32)
    value_acc = jnp.zeros((seq, LANES), jnp.float32)
    query_parts = {}
    for head in range(LANES // HEAD_DIM):
        base_ref[...] = bias_base(bias_ref[0, head : head + 1, :], seq)
        acc_ref[...] = jnp.zeros_like(acc_ref)
        for start in starts:
            query_block = head_part(query_ref, start, cols, head)
            grad_block = head_part(grad_ref, start, cols, head)
            scores = masked_scores(keys, query_block, base_ref, start, seq, cols, length)
            probs = jnp.exp(scores - total_ref[0, head : head + 1, start : start + cols])
            probs_grad = dot_nt(values, grad_block)
            mean_grad = jnp.sum(probs * probs_grad, axis=0, keepdims=True)
            score_grad = (probs * (probs_grad - mean_grad)).astype(jnp.bfloat16)
            value_acc = value_acc + dot_nn(probs.astype(jnp.bfloat16), grad_block)
            key_acc = key_acc + dot_nn(score_grad, query_block)
            query_parts[start, head] = dot_nn(
                keys_t[head * HEAD_DIM : (head + 1) * HEAD_DIM], score_grad
            )
            for first in range(0, seq, LANES):
                offset = seq - LANES - first + start
                acc_ref[:, offset : offset + cols] += score_grad[
                    first : first + LANES
                ].astype(jnp.float32)
        bias_grad_ref[0, head : head + 1, :] = diagonal_sums(acc_ref, seq)
    joined_grad_ref[:, LANES : 2 * LANES] = (key_acc * SCORE_SCALE).astype(jnp.bfloat16)
    joined_grad_ref[:, 2 * LANES :] = value_acc.astype(jnp.bfloat16)
    for start in starts:
        joined = jnp.concatenate(
            [query_parts[start, head] for head in range(LANES // HEAD_DIM)], axis=0
        )
        joined_grad_ref[start : start + cols, :LANES] = (joined * SCORE_SCALE).T.astype(
            jnp.bfloat16
        )


def attend_backward(length, joined, attended_grad, totals, bias_rows):
    seq, width = attended_grad.shape
    pairs = width // LANES
    heads = LANES // HEAD_DIM
    column = pl.BlockSpec((seq, LANES), lambda i: (0, i))
    triple = pl.BlockSpec((seq, 3 * LANES), lambda i: (0, i))
    vector = pl.BlockSpec((1, heads, 2 * seq), lambda i: (i, 0, 0))
    return pl.pallas_call(
        backward_kernel,
        grid=(pairs,),
        in_specs=[
            pl.BlockSpec(memory_space=pltpu.SMEM),
            triple,
            column,
            pl.BlockSpec((1, heads, seq), lambda i: (i, 0, 0)),
            vector,
        ],
        out_specs=[triple, vector],
        out_shape=[
            jax.ShapeDtypeStruct((seq, 3 * width), jnp.bfloat16),
            jax.ShapeDtypeStruct((pairs, heads, 2 * seq), jnp.float32),
        ],
        scratch_shapes=[
            pltpu.VMEM((LANES, 2 * seq), jnp.float32),
            pltpu.VMEM((LANES, 2 * seq), jnp.float32),
        ],
        cost_estimate=pl.CostEstimate(
            flops=40 * seq * seq * width,
            transcendentals=seq * seq * width // HEAD_DIM,
            bytes_accessed=14 * seq * width,
        ),
        name="attend_backward",
    )(length, joined, attended_grad, totals, bias_rows)


def assemble_kernel(place_ref, *refs):
    parts, (weight_ref, out_ref, gain_ref) = refs[:-3], refs[-3:]
    rows = weight_ref.shape[0] // len(parts)
    pairs = weight_ref.shape[1] // (3 * LANES)
    for index, part_ref in enumerate(parts):
        inner = index ^ place_ref[1]
        block = pl.ds(pl.multiple_of(inner * rows, rows), rows)
        for kind in range(3):
            for pair in range(pairs):
                first = (3 * pair + kind) * LANES
                weight_ref[block, first : first + LANES] = part_ref[
                    0, kind * rows : (kind + 1) * rows, pair * LANES : (pair + 1) * LANES
                ]
        out_ref[block, :] = part_ref[0, 3 * rows : 4 * rows, :]
        gain_ref[pl.ds(inner, 1)] = part_ref[:, 4 * rows :, :]


def assemble(place, parts):
    outer, block_rows, cols = parts[0].shape
    inner = len(parts)
    rows = (block_rows - GAIN_ROWS) // 4
    block = pl.BlockSpec((1, block_rows, cols), lambda i, place_ref: (i ^ place_ref[0], 0, 0))
    return pl.pallas_call(
        assemble_kernel,
        grid_spec=pltpu.PrefetchScalarGridSpec(
            num_scalar_prefetch=1,
            grid=(outer,),
            in_specs=[block] * inner,
            out_specs=[
                pl.BlockSpec((inner * rows, 3 * cols), lambda i, place_ref: (i, 0)),
                pl.BlockSpec((inner * rows, cols), lambda i, place_ref: (i, 0)),
                pl.BlockSpec((inner, GAIN_ROWS, cols), lambda i, place_ref: (i, 0, 0)),
            ],
        ),
        out_shape=[
            jax.ShapeDtypeStruct((outer * inner * rows, 3 * cols), jnp.bfloat16),
            jax.ShapeDtypeStruct((outer * inner * rows, cols), jnp.bfloat16),
            jax.ShapeDtypeStruct((outer * inner, GAIN_ROWS, cols), jnp.bfloat16),
        ],
        name="assemble",
    )(place, *parts)


def gelu_parts(gate_pre):
    inner = jnp.tanh(GELU_SCALE * (gate_pre + GELU_CUBIC * gate_pre * gate_pre * gate_pre))
    gelu = 0.5 * gate_pre * (1.0 + inner)
    slope = 0.5 * (1.0 + inner) + 0.5 * gate_pre * (1.0 - inner * inner) * GELU_SCALE * (
        1.0 + 3.0 * GELU_CUBIC * gate_pre * gate_pre
    )
    return gelu, slope


def expert_forward_kernel(
    side_ref, near_ref, far_ref, gate_near, up_near, gate_far, up_far, hidden_ref, slope_ref, gelu_ref
):
    near = near_ref[...]
    far = far_ref[...]
    gate_pre = dot_nn(near, gate_near[...]) + dot_nn(far, gate_far[...])
    up_pre = dot_nn(near, up_near[...]) + dot_nn(far, up_far[...])
    gelu, slope = gelu_parts(gate_pre)
    hidden_ref[...] = (gelu * up_pre).astype(jnp.bfloat16)
    slope_ref[...] = slope * up_pre
    gelu_ref[...] = gelu


def slot_block(slots):
    return 288 if slots % 288 == 0 else slots


def expert_forward(side, near, far, weights, hidden_cols):
    slots, half = near.shape
    rows = slot_block(slots)
    row_spec = pl.BlockSpec((rows, half), lambda i, side_ref: (i, 0))
    wide_spec = pl.BlockSpec((rows, hidden_cols), lambda i, side_ref: (i, 0))

    def weight_spec(other, column):
        return pl.BlockSpec(
            (half, hidden_cols),
            lambda i, side_ref: (side_ref[0] ^ other, column),
            pipeline_mode=pl.Buffered(1),
        )

    return pl.pallas_call(
        expert_forward_kernel,
        grid_spec=pltpu.PrefetchScalarGridSpec(
            num_scalar_prefetch=1,
            grid=(slots // rows,),
            in_specs=[
                row_spec,
                row_spec,
                weight_spec(0, 0),
                weight_spec(0, 1),
                weight_spec(1, 0),
                weight_spec(1, 1),
            ],
            out_specs=[wide_spec] * 3,
        ),
        out_shape=[
            jax.ShapeDtypeStruct((slots, hidden_cols), jnp.bfloat16),
            jax.ShapeDtypeStruct((slots, hidden_cols), jnp.float32),
            jax.ShapeDtypeStruct((slots, hidden_cols), jnp.float32),
        ],
        compiler_params=pltpu.CompilerParams(vmem_limit_bytes=VMEM_BYTES),
        cost_estimate=pl.CostEstimate(
            flops=8 * slots * half * hidden_cols,
            transcendentals=slots * hidden_cols,
            bytes_accessed=10 * slots * hidden_cols + 8 * half * hidden_cols,
        ),
        name="expert_forward",
    )(side, near, far, weights, weights, weights, weights)


def expert_backward_kernel(
    side_ref,
    near_ref,
    far_ref,
    slope_ref,
    gelu_ref,
    down_near,
    down_far,
    gate_near,
    up_near,
    gate_far,
    up_far,
    pre_grad_ref,
    stay_ref,
    away_ref,
):
    cols = slope_ref.shape[1]
    hidden_grad = dot_nn(near_ref[...], down_near[...]) + dot_nn(far_ref[...], down_far[...])
    gate_grad = (hidden_grad * slope_ref[...]).astype(jnp.bfloat16)
    up_grad = (hidden_grad * gelu_ref[...]).astype(jnp.bfloat16)
    pre_grad_ref[:, :cols] = gate_grad
    pre_grad_ref[:, cols:] = up_grad
    away_ref[...] = (dot_nt(gate_grad, gate_far[...]) + dot_nt(up_grad, up_far[...])).astype(
        jnp.bfloat16
    )
    stay_ref[...] = dot_nt(gate_grad, gate_near[...]) + dot_nt(up_grad, up_near[...])


def expert_backward(side, near, far, slope, gelu, down, weights):
    slots, half = near.shape
    hidden_cols = slope.shape[1]
    rows = slot_block(slots)
    row_spec = pl.BlockSpec((rows, half), lambda i, side_ref: (i, 0))
    wide_spec = pl.BlockSpec((rows, hidden_cols), lambda i, side_ref: (i, 0))

    def weight_spec(other, column):
        return pl.BlockSpec(
            (half, hidden_cols),
            lambda i, side_ref: (side_ref[0] ^ other, column),
            pipeline_mode=pl.Buffered(1),
        )

    return pl.pallas_call(
        expert_backward_kernel,
        grid_spec=pltpu.PrefetchScalarGridSpec(
            num_scalar_prefetch=1,
            grid=(slots // rows,),
            in_specs=[
                row_spec,
                row_spec,
                wide_spec,
                wide_spec,
                weight_spec(0, 0),
                weight_spec(1, 0),
                weight_spec(0, 0),
                weight_spec(0, 1),
                weight_spec(1, 0),
                weight_spec(1, 1),
            ],
            out_specs=[
                pl.BlockSpec((rows, 2 * hidden_cols), lambda i, side_ref: (i, 0)),
                row_spec,
                row_spec,
            ],
        ),
        out_shape=[
            jax.ShapeDtypeStruct((slots, 2 * hidden_cols), jnp.bfloat16),
            jax.ShapeDtypeStruct((slots, half), jnp.float32),
            jax.ShapeDtypeStruct((slots, half), jnp.bfloat16),
        ],
        compiler_params=pltpu.CompilerParams(vmem_limit_bytes=VMEM_BYTES),
        cost_estimate=pl.CostEstimate(
            flops=12 * slots * half * hidden_cols,
            transcendentals=0,
            bytes_accessed=12 * slots * hidden_cols + 12 * half * hidden_cols,
        ),
        name="expert_backward",
    )(side, near, far, slope, gelu, down, down, weights, weights, weights, weights)


def finish_kernel(place_ref, stay_ref, *refs):
    arrivals = refs[:3]
    small_ref, qkv_ref, out_ref, gain_ref, bias_ref, total_ref = refs[3:]
    kinds, rows, cols = qkv_ref.shape
    row_size = stay_ref.shape[1]
    small_rows = small_ref.shape[0]
    total = stay_ref[...].astype(jnp.float32)
    small = small_ref[...]
    for arrival in arrivals:
        total = total + arrival[:, :row_size].astype(jnp.float32)
        extra = arrival[:, row_size:].astype(jnp.float32)
        small = small + extra[:small_rows] + extra[small_rows : 2 * small_rows]
    for kind in range(kinds):
        for pair in range(cols // LANES):
            first = (kinds * pair + kind) * LANES
            qkv_ref[kind, :, pair * LANES : (pair + 1) * LANES] = total[:, first : first + LANES]
    out_ref[...] = total[:, kinds * cols :]
    total_ref[...] = small
    norm_rows = row_size // LANES // 2
    first = place_ref[0] * rows
    for norm in range(2):
        row = total_ref[pl.ds(norm * norm_rows + first // LANES, 1), :]
        shift = lax.rem(LANES - lax.rem(first, LANES), LANES)
        gain_ref[norm : norm + 1, :] = pltpu.roll(row, shift, 1)[:, :rows]
    heads, buckets = bias_ref.shape
    for head in range(heads):
        row, lane = divmod(head * buckets, LANES)
        bias_ref[head : head + 1, :] = small[
            2 * norm_rows + row : 2 * norm_rows + row + 1, lane : lane + buckets
        ]


def finish(place, stay, arrivals, small, cols, bias_shape):
    rows = stay.shape[0]
    whole = pl.BlockSpec(memory_space=pltpu.VMEM)
    return pl.pallas_call(
        finish_kernel,
        in_specs=[pl.BlockSpec(memory_space=pltpu.SMEM), *[whole] * 5],
        out_specs=[whole] * 4,
        out_shape=[
            jax.ShapeDtypeStruct((3, rows, cols), jnp.float32),
            jax.ShapeDtypeStruct((rows, cols), jnp.float32),
            jax.ShapeDtypeStruct((2, rows), jnp.float32),
            jax.ShapeDtypeStruct(bias_shape, jnp.float32),
        ],
        scratch_shapes=[pltpu.VMEM(small.shape, jnp.float32)],
        name="finish",
    )(place, stay, *arrivals, small)


def on_device(
    tokens,
    cotangent,
    lengths,
    bucket_table,
    routes,
    gate_values,
    qkv_weight,
    out_weight,
    norm_gains,
    rel_bias,
    gate_weight,
    up_weight,
    down_weight,
):
    tok_rows, width = tokens.shape
    half = width // 2
    dp_count = lax.axis_size("dp")
    tensor_count = lax.axis_size("tensor")
    seq = tok_rows * tensor_count
    expert_count, shard_rows, hidden_cols = gate_weight.shape
    head_cols = qkv_weight.shape[2]
    head_count, bucket_count = rel_bias.shape
    capacity = 9 * seq // 64
    group_size = dp_count // expert_count
    slot_count = (capacity + group_size - 1) // group_size
    total_slots = dp_count * slot_count
    dp_index = lax.axis_index("dp")
    tensor_index = lax.axis_index("tensor")
    first_tensor = tensor_index == 0
    length = lengths[dp_index]
    length_row = length[None]
    group_valid = jnp.arange(seq, dtype=jnp.int32) < length
    own_valid = lax.dynamic_slice_in_dim(group_valid, tensor_index * tok_rows, tok_rows, 0)
    own_valid = own_valid.astype(jnp.float32)[:, None]

    def swap(block):
        return lax.ppermute(block, "tensor", [(0, 1), (1, 0)])

    def partner(block, offset):
        return lax.ppermute(block, "dp", [(i, i ^ offset) for i in range(dp_count)])

    def chain(block, earlier):
        return lax.optimization_barrier((block, earlier))

    def ordered(own, other, axis):
        return jnp.where(
            first_tensor,
            jnp.concatenate([own, other], axis=axis),
            jnp.concatenate([other, own], axis=axis),
        )

    def own_part(block, axis):
        size = block.shape[axis] // 2
        return lax.dynamic_slice_in_dim(block, tensor_index * size, size, axis)

    def other_part(block, axis):
        size = block.shape[axis] // 2
        return lax.dynamic_slice_in_dim(block, (1 - tensor_index) * size, size, axis)

    def exchange(block):
        return lax.all_to_all(block, "dp", split_axis=0, concat_axis=0, tiled=True)

    def home_order(weight):
        return jnp.repeat(weight, group_size, axis=0)

    def fetch(weight):
        return exchange(home_order(weight)).reshape(dp_count * shard_rows, weight.shape[2])

    def send_grad(grad):
        return exchange(grad.reshape(dp_count, shard_rows, grad.shape[1]))

    def route(rows):
        arrived = exchange(rows.reshape(dp_count, slot_count, rows.shape[1]))
        return arrived.reshape(total_slots, rows.shape[1])

    spare = slot_count - shard_rows
    fold = shard_rows // spare

    def pack(rows):
        blocks = rows.reshape(dp_count, slot_count, half)
        tail = blocks[:, shard_rows:].reshape(dp_count, spare, fold, half // fold)
        tail = tail.transpose(0, 2, 1, 3).reshape(dp_count, shard_rows, half // fold)
        return jnp.concatenate([blocks[:, :shard_rows], tail], axis=2)

    def unpack(packed):
        tail = packed[:, :, half:].reshape(dp_count, fold, spare, half // fold)
        tail = tail.transpose(0, 2, 1, 3).reshape(dp_count, spare, half)
        return jnp.concatenate([packed[:, :, :half], tail], axis=1).reshape(total_slots, half)

    def regroup(arrived):
        return jnp.sum(
            arrived.astype(jnp.float32).reshape(
                expert_count, group_size, shard_rows, arrived.shape[2]
            ),
            axis=1,
        )

    gain_pad = jnp.pad(norm_gains, ((0, GAIN_ROWS - 2), (0, head_cols - shard_rows)))
    layer_shard = jnp.concatenate(
        [qkv_weight.reshape(3 * shard_rows, head_cols), out_weight, gain_pad], axis=0
    )
    pairs = head_cols // LANES
    pair_expert = routes.reshape(-1)
    pair_valid = jnp.repeat(group_valid, 2)
    chosen = (
        pair_expert[:, None] == jnp.arange(expert_count, dtype=jnp.int32)[None, :]
    ) & pair_valid[:, None]
    pair_index = jnp.arange(2 * seq, dtype=jnp.int32)
    before = (pair_index[:, None] > pair_index[None, :]).astype(jnp.bfloat16)
    earlier_pairs = dot_nn(before, chosen.astype(jnp.bfloat16))
    position = jnp.sum(jnp.where(chosen, earlier_pairs, 0.0), axis=1).astype(jnp.int32)
    kept_pair = pair_valid & (position < capacity)
    device = pair_expert * group_size + position // slot_count
    pair_slot = jnp.where(
        kept_pair, device * slot_count + position % slot_count, total_slots
    ).reshape(seq, 2)
    slot_index = jnp.arange(total_slots, dtype=jnp.int32)
    first_hit = pair_slot[:, 0][None, :] == slot_index[:, None]
    second_hit = pair_slot[:, 1][None, :] == slot_index[:, None]
    no_gate = jnp.zeros((), jnp.bfloat16)
    pick = (first_hit | second_hit).astype(jnp.bfloat16)
    pick_gate = jnp.where(
        first_hit,
        gate_values[:, 0][None, :],
        jnp.where(second_hit, gate_values[:, 1][None, :], no_gate),
    )

    mix_grad = lax.optimization_barrier(
        (own_valid * cotangent.astype(jnp.float32)).astype(jnp.bfloat16)
    )
    mix_away = other_part(mix_grad, 1)
    mix_other = swap(mix_away)
    tokens_other = swap(chain(tokens, mix_away)[0])
    out_grad_cols = dot_nn(
        pick_gate, ordered(own_part(mix_grad, 1), mix_other, 0)
    ).astype(jnp.bfloat16)
    residual, out_grad_cols = chain(tokens, out_grad_cols)
    gate_up = jnp.concatenate([home_order(gate_weight), home_order(up_weight)], axis=2)
    if dp_count == 16:
        across = [partner(layer_shard, 4 * k) for k in range(1, 4)]
        gate_up = chain(gate_up, across)[0]
        near = jnp.stack([layer_shard, *across])
        side = partner(near, 2)
        parts = [near, partner(near, 1), side, partner(side, 1)]
        place = jnp.stack([dp_index // 4, dp_index % 4])
        projection, out_all, gain_rows = assemble(place, parts)
    else:
        layer_all = lax.all_gather(layer_shard, "dp", axis=0, tiled=False)
        gate_up = chain(gate_up, layer_all)[0]
        projection = (
            layer_all[:, : 3 * shard_rows]
            .reshape(dp_count, 3, shard_rows, pairs, LANES)
            .transpose(0, 2, 3, 1, 4)
            .reshape(width, 3 * head_cols)
        )
        out_all = layer_all[:, 3 * shard_rows : 4 * shard_rows].reshape(width, head_cols)
        gain_rows = layer_all[:, 4 * shard_rows :]
    gate_up_all = exchange(gate_up).reshape(width, 2 * hidden_cols)

    distance = jnp.arange(2 * seq, dtype=jnp.int32)
    table_reversed = jnp.concatenate(
        [bucket_table[::-1], jnp.full((1,), bucket_count, jnp.int32)]
    )
    hot = (
        jnp.arange(bucket_count, dtype=jnp.int32)[:, None] == table_reversed[None, :]
    ).astype(jnp.float32)
    bias_rows = jnp.dot(rel_bias.astype(jnp.float32), hot, precision=HIGHEST).reshape(
        head_count // 2, 2, 2 * seq
    )
    gains_all = jnp.transpose(gain_rows[:, :2, :shard_rows], (1, 0, 2)).reshape(2, width)
    gain_one = gains_all[0].astype(jnp.float32)
    gain_two = gains_all[1].astype(jnp.float32)
    inputs_all = ordered(tokens, tokens_other, 0).astype(jnp.float32)
    scale_all = lax.rsqrt(jnp.mean(inputs_all * inputs_all, axis=-1, keepdims=True) + EPSILON)
    norm_one_all = (inputs_all * scale_all * gain_one).astype(jnp.bfloat16)
    joined = dot_nn(norm_one_all, projection).astype(jnp.bfloat16)
    attended, totals = attend_forward(length_row, joined, bias_rows)
    branch = dot_nt(attended, out_all)
    branch_other = swap(other_part(branch, 0).astype(jnp.bfloat16))
    inputs = residual.astype(jnp.float32)
    mid = inputs + own_valid * (own_part(branch, 0) + branch_other.astype(jnp.float32))
    mid_scale = lax.rsqrt(jnp.mean(mid * mid, axis=-1, keepdims=True) + EPSILON)
    norm_two = (mid * mid_scale * gain_two).astype(jnp.bfloat16)
    norm_two_cols = ordered(own_part(norm_two, 1), swap(other_part(norm_two, 1)), 0)
    slot_rows, gate_up_all = chain(
        jnp.concatenate(
            [dot_nn(pick, norm_two_cols).astype(jnp.bfloat16), out_grad_cols], axis=1
        ),
        gate_up_all,
    )
    down_late, slot_rows = chain(down_weight, route(slot_rows))
    down_all = fetch(down_late)
    expert_half = slot_rows[:, :half]
    expert_other = swap(expert_half)
    slot_grad_half = chain(slot_rows[:, half:], expert_other)[0]
    slot_grad_other = swap(slot_grad_half)

    side = tensor_index[None]
    hidden, slope, gelu = expert_forward(
        side, expert_half, expert_other, gate_up_all, hidden_cols
    )
    slot_grad = ordered(slot_grad_half, slot_grad_other, 1)
    down_grad, down_all = chain(dot_tn(slot_grad, hidden).astype(jnp.bfloat16), down_all)
    down_back = send_grad(down_grad)
    pre_grad, slot_back_stay, slot_back_away = expert_backward(
        side, slot_grad_half, slot_grad_other, slope, gelu, down_all, gate_up_all
    )
    hidden_late, slot_back_away = chain(hidden, slot_back_away)
    slot_back_other = swap(slot_back_away)
    expert_out_part = dot_nt(hidden_late, down_all)
    expert_out_away, slot_back_other = chain(
        other_part(expert_out_part, 1).astype(jnp.bfloat16), slot_back_other
    )
    slot_back_half = (
        slot_back_stay + slot_back_other.astype(jnp.float32)
    ).astype(jnp.bfloat16)
    expert_out_half = (
        own_part(expert_out_part, 1) + swap(expert_out_away).astype(jnp.float32)
    ).astype(jnp.bfloat16)
    slot_back_half, down_back = chain(slot_back_half, down_back)
    last, slot_back = chain(
        jnp.concatenate(
            [
                dot_tn(ordered(expert_half, expert_other, 1), pre_grad)
                .astype(jnp.bfloat16)
                .reshape(dp_count, shard_rows, 2 * hidden_cols),
                pack(expert_out_half),
            ],
            axis=2,
        ),
        route(slot_back_half),
    )
    arrived_back = exchange(last)

    back_cols = dot_tn(pick, slot_back)
    norm_two_grad = ordered(
        own_part(back_cols, 0), swap(other_part(back_cols, 0).astype(jnp.bfloat16)).astype(jnp.float32), 1
    )
    mid_unit = mid * mid_scale
    mid_inner = norm_two_grad * gain_two
    mid_grad = own_valid * cotangent.astype(jnp.float32) + mid_scale * (
        mid_inner - mid_unit * jnp.mean(mid_inner * mid_unit, axis=-1, keepdims=True)
    )
    gain_two_grad = jnp.sum(norm_two_grad * mid_unit, axis=0)
    branch_grad = (own_valid * mid_grad).astype(jnp.bfloat16)
    branch_grad_all = ordered(branch_grad, swap(branch_grad), 0)

    attended_grad = dot_nn(branch_grad_all, out_all).astype(jnp.bfloat16)
    joined_grad, bias_sums = attend_backward(
        length_row, joined, attended_grad, totals, bias_rows
    )
    bias_grad = jnp.dot(
        bias_sums.reshape(head_count, 2 * seq), hot.T, precision=HIGHEST
    )
    norm_one_part = dot_nt(joined_grad, projection)
    layer_part = jnp.concatenate(
        [
            dot_tn(norm_one_all, joined_grad).astype(jnp.bfloat16),
            dot_tn(branch_grad_all, attended).astype(jnp.bfloat16),
        ],
        axis=1,
    )
    gain_one_grad = jnp.sum(norm_one_part * (inputs_all * scale_all), axis=0)
    norm_one_grad = own_part(norm_one_part, 0) + swap(
        other_part(norm_one_part, 0).astype(jnp.bfloat16)
    ).astype(jnp.float32)
    scale = lax.rsqrt(jnp.mean(inputs * inputs, axis=-1, keepdims=True) + EPSILON)
    unit = inputs * scale
    inner = norm_one_grad * gain_one
    input_grad = mid_grad + scale * (
        inner - unit * jnp.mean(inner * unit, axis=-1, keepdims=True)
    )
    gain_part = jnp.concatenate([gain_one_grad, gain_two_grad]).reshape(-1, LANES)
    small = jnp.concatenate(
        [gain_part + swap(gain_part), bias_grad.reshape(-1, LANES)], axis=0
    )

    row_size = layer_part.shape[1]
    small = jnp.pad(small.reshape(-1), (0, -small.size % row_size)).reshape(-1, row_size)
    small_rows = small.shape[0]

    def with_small(block):
        high = lax.reduce_precision(small, 8, 7)
        rows = jnp.concatenate([high, small - high], axis=0).astype(jnp.bfloat16)
        rows = jnp.pad(rows, ((0, -rows.shape[0] % 8), (0, 0)))
        return jnp.concatenate([block, rows], axis=0)

    def small_of(block, first):
        rows = block[first : first + 2 * small_rows].astype(jnp.float32)
        return rows[:small_rows] + rows[small_rows:]

    if dp_count == 16:
        blocks = layer_part.reshape(dp_count, shard_rows, row_size)
        for step in (1, 2):
            pieces = blocks.reshape(-1, 2, shard_rows, row_size)
            bit = (dp_index // step) % 2
            away = lax.dynamic_index_in_dim(pieces, 1 - bit, 1, keepdims=False)
            stay = lax.dynamic_index_in_dim(pieces, bit, 1, keepdims=False)
            if step == 1:
                came = partner(away, step)
                small = small + partner(small, step)
            else:
                down_out = regroup(down_back)
                ready = with_small(away.reshape(-1, row_size))
                came = partner(chain(ready, (down_out, input_grad))[0], step)
                small = small + small_of(came, away.shape[0] * shard_rows)
                came = came[: away.shape[0] * shard_rows].reshape(away.shape)
            blocks = (stay.astype(jnp.float32) + came.astype(jnp.float32)).astype(jnp.bfloat16)
        outer = dp_index // 4
        high = lax.reduce_precision(small, 8, 7)
        beside = jnp.concatenate([high, small - high], axis=0).astype(jnp.bfloat16)
        beside = beside.reshape(-1, LANES)
        beside = jnp.pad(beside, ((0, shard_rows - beside.shape[0]), (0, 0)))
        leaving = [
            jnp.concatenate(
                [lax.dynamic_index_in_dim(blocks, outer ^ k, 0, keepdims=False), beside], axis=1
            )
            for k in range(1, 4)
        ]
        small = small.reshape(-1, LANES)
        stay = lax.dynamic_index_in_dim(blocks, outer, 0, keepdims=False)
        arrived_back = chain(arrived_back, leaving)[0]
        came = [partner(piece, 4 * k) for k, piece in zip(range(1, 4), leaving, strict=True)]
    else:
        step = 1
        while step < dp_count:
            small = small + partner(small, step)
            step *= 2
    returned = unpack(arrived_back[:, :, 2 * hidden_cols :])
    mix_cols = dot_tn(pick_gate, returned)
    mix_away = other_part(mix_cols, 0).astype(jnp.bfloat16)
    mix_other = swap(mix_away)
    arrived_back = chain(arrived_back, mix_away)[0]
    gate_grad = regroup(arrived_back[:, :, :hidden_cols])
    up_grad = regroup(arrived_back[:, :, hidden_cols : 2 * hidden_cols])
    mix_own = ordered(own_part(mix_cols, 0), mix_other.astype(jnp.float32), 1)
    mixed = (mid + own_valid * mix_own).astype(jnp.bfloat16)
    if dp_count == 16:
        came = chain(came, (gate_grad, up_grad, mixed))[0]
        qkv_grad, out_grad, gains_grad, bias_out = finish(
            dp_index[None], stay, came, small, head_cols, bias_grad.shape
        )
    else:
        layer_grad = lax.psum_scatter(
            layer_part, "dp", scatter_dimension=0, tiled=True
        ).astype(jnp.float32)
        qkv_grad = (
            layer_grad[:, : 3 * head_cols]
            .reshape(shard_rows, pairs, 3, LANES)
            .transpose(2, 0, 1, 3)
            .reshape(3, shard_rows, head_cols)
        )
        out_grad = layer_grad[:, 3 * head_cols :]
        gain_sums = small[:1].reshape(2, width)
        gains_grad = lax.dynamic_slice_in_dim(gain_sums, dp_index * shard_rows, shard_rows, 1)
        bias_out = small[1, : head_count * bucket_count].reshape(head_count, bucket_count)
    return (
        mixed,
        input_grad,
        qkv_grad,
        out_grad,
        gains_grad,
        bias_out,
        gate_grad,
        up_grad,
        down_out if dp_count == 16 else regroup(down_back),
    )


def solution(mesh):
    rows = P(("dp", "tensor"), None)
    shard = P("dp", "tensor")
    stacked = P(None, "dp", "tensor")
    return jax.shard_map(
        on_device,
        mesh=mesh,
        in_specs=(
            rows,
            rows,
            P(),
            P(),
            P("dp", None),
            P("dp", None),
            stacked,
            shard,
            P(None, "dp"),
            P("tensor", None),
            stacked,
            stacked,
            stacked,
        ),
        out_specs=(
            rows,
            rows,
            stacked,
            shard,
            P(None, "dp"),
            P("tensor", None),
            stacked,
            stacked,
            stacked,
        ),
        check_vma=False,
    )
```
